32 devices in a mesh: horiz: 8 (over y, x, core), vert: 4 (over z).
Axes of the slice: x: 2, y: 2, z: 4, core: 2. Of those that a mesh axis runs over, the one named last changes fastest.
Arguments:
- velocity: float32 [3, 32, 256, 512], P(None, 'horiz', None, 'vert'), may hold values from -6 to 6
- dust: float32 [32, 256, 128], P('horiz', 'vert'), may hold values from 0.1 to 2
- eligible: int32 [32, 2], P('horiz'), may hold values 0 or 1
- terrain: int32 [32, 256], P('horiz', 'vert'), may hold values from 0 to 3
Outputs:
- velocity_next: float32 [3, 32, 256, 512], P(None, 'horiz', None, 'vert')
- dust_next: float32 [32, 256, 128], P('horiz', 'vert')
The draws below stay inside these ranges and needn't reach their ends.
All inputs are finite; a program needn't handle non-finite values. No bound on the sum of `eligible` on one device may be relied on, other than what follows from the above.
Results may differ from the reference program's by a relative error of at most 0.0015.
Values may be sent and summed in bfloat16 or wider, within the bound.
No kernel may reach another device: no remote copies, remote signals or barrier semaphores. Data moves between devices by JAX's collectives and lax.ppermute only.
A program may use at most 64 MiB of HBM per device.

```python
import math
import jax
import jax.numpy as jnp
from jax import lax

NY = 256
DSTEPS = 2
TOPS = 4
NX = 32
NZ = 512
NZD = 128


def plant(result, rng, smallest, top_value):
    dims = result.shape
    spot = [jax.random.randint(jax.random.fold_in(rng, axis), (), 0, dims[axis]) for axis in range(len(dims))]
    result = result.at[tuple(spot)].set(smallest)
    longest = dims.index(max(dims))
    spot[longest] = (spot[longest] + 1) % dims[longest]
    return result.at[tuple(spot)].set(top_value)


def steps_of(own_key, extent, pieces, low, top_value):
    def one(position, parts):
        steps = jax.random.uniform(jax.random.fold_in(jax.random.fold_in(own_key, 6), position), (parts,), jnp.float32, low / len(pieces), top_value / len(pieces))
        return jnp.repeat(jnp.exp(steps), extent[position] // parts).reshape((-1,) + (1,) * (len(extent) - position - 1))

    level = one(*pieces[0])
    for cut in pieces[1:]:
        level = level * one(*cut)
    return level


def bell_draw(key, dims, width, limit, cuts=(), kind=jnp.bfloat16):
    factor_of = steps_of(key, dims, cuts, -0.22, 0.18) if cuts else 1.0
    array = jax.random.normal(key, dims, jnp.float32) * width * factor_of
    return jnp.minimum(jnp.maximum(array, -limit), limit).astype(kind)


def setup_inputs(seed: int = 0) -> dict:
    keys = jax.random.split(jax.random.key(seed), 5)
    return {
        "velocity": bell_draw(keys[0], (3, NX, NY, NZ), 1.0, 6.0, ((1, 8), (3, 4)), jnp.float32),
        "dust": jnp.clip(jnp.exp(math.log(2.0) - 2.9957323 * jax.random.uniform(keys[1], (NX, NY, NZD), jnp.float32) ** steps_of(keys[1], (NX, NY, NZD), ((0, 8), (1, 4)), -0.2, 0.2)), 0.1, 2.0),
        "eligible": plant((jax.random.randint(keys[2], (NX, NY // 128), 0, 2) < 1).astype(jnp.int32), jax.random.fold_in(keys[2], 1), 0, 1),
        "terrain": plant(jax.random.randint(keys[3], (NX, NY), 0, TOPS), jax.random.fold_in(keys[3], 1), 0, TOPS - 1).astype(jnp.int32),
    }


def lap_zero(field):
    padded = jnp.pad(field, 1)
    near = padded[2:, 1:-1, 1:-1] + padded[:-2, 1:-1, 1:-1]
    near = near + padded[1:-1, 2:, 1:-1] + padded[1:-1, :-2, 1:-1]
    near = near + padded[1:-1, 1:-1, 2:] + padded[1:-1, 1:-1, :-2]
    return near - 6.0 * field

def reference(velocity, dust, eligible, terrain):
    velocity_next = lax.map(lambda comp: comp + 0.12 * lap_zero(comp), velocity)
    ground = velocity_next[:, :, :, :NZD].astype(jnp.bfloat16).astype(jnp.float32)
    gu, gv, gw = (ground[0], ground[1], ground[2] - 0.5)
    flags = jnp.repeat(eligible, 128, axis=1)
    layer = lax.broadcasted_iota(jnp.int32, dust.shape, 2)
    surface = layer == terrain[:, :, None]
    speed = jnp.sqrt(gu * gu + gv * gv)
    lift = jnp.where(surface & (flags[:, :, None] == 1), 0.5 * jnp.maximum(speed - 1.0, 0.0), 0.0)
    solid = layer < terrain[:, :, None]
    conc = dust
    for step in range(DSTEPS):
        padded = jnp.pad(conc, 1)
        tend = -(jnp.maximum(gu, 0.0) * (conc - padded[:-2, 1:-1, 1:-1]) + jnp.minimum(gu, 0.0) * (padded[2:, 1:-1, 1:-1] - conc))
        tend = tend - (jnp.maximum(gv, 0.0) * (conc - padded[1:-1, :-2, 1:-1]) + jnp.minimum(gv, 0.0) * (padded[1:-1, 2:, 1:-1] - conc))
        tend = tend - (jnp.maximum(gw, 0.0) * (conc - padded[1:-1, 1:-1, :-2]) + jnp.minimum(gw, 0.0) * (padded[1:-1, 1:-1, 2:] - conc))
        tend = tend + 0.1 * lap_zero(conc)
        conc = jnp.where(solid, 0.0, conc + 0.15 * tend + lift)
    return (velocity_next, conc)
```

```python
import functools

import jax
import jax.numpy as jnp
from jax import lax
from jax.experimental import pallas as pl
from jax.experimental.pallas import tpu as pltpu
from jax.sharding import PartitionSpec as P

DSTEPS = 2
LANES = 128
EDGE = 8
BF = jnp.bfloat16
F32 = jnp.float32

VMEM = pl.BlockSpec(memory_space=pltpu.VMEM)


def call(kernel, out_shape, name, scratch=(), cost=1 << 20, **kwargs):
    return pl.pallas_call(
        kernel,
        out_shape=out_shape,
        scratch_shapes=list(scratch),
        compiler_params=pltpu.CompilerParams(vmem_limit_bytes=40 << 20),
        cost_estimate=pl.CostEstimate(flops=cost, bytes_accessed=cost, transcendentals=0),
        name=name,
        **kwargs,
    )


def shaped(*dims, dtype=BF):
    return jax.ShapeDtypeStruct(dims, dtype)


def iota(shape, dim):
    return lax.broadcasted_iota(jnp.int32, shape, dim)


def pick(shape, pairs):
    row, col = iota(shape, 0), iota(shape, 1)
    hit = functools.reduce(jnp.logical_or, [(row == r) & (col == c) for r, c in pairs])
    return jnp.where(hit, 1.0, 0.0).astype(BF)


def pack_strips(v_ref, *outs):
    ncomp, nx, ny, _ = v_ref.shape
    strips, up_ref, down_ref = (outs[:-2], outs[-2], outs[-1])
    size = ny // len(strips)
    for t, out in enumerate(strips):
        low, high = (max(t * size - EDGE, 0), min((t + 1) * size + EDGE, ny))
        start = low - (t * size - EDGE)
        for comp in range(ncomp):
            for x in range(nx):
                rows = v_ref[comp, x, low:high, :]
                parts = [rows]
                if start:
                    parts = [jnp.zeros((start, LANES), F32)] + parts
                if start + high - low < size + 2 * EDGE:
                    parts = parts + [jnp.zeros((size + 2 * EDGE - start - high + low, LANES), F32)]
                rows = jnp.concatenate(parts, 0) if len(parts) > 1 else rows
                out[comp * nx + x] = rows.astype(BF)
    up_ref[...] = v_ref[:, nx - 1].astype(BF)
    down_ref[...] = v_ref[:, 0].astype(BF)


def pack_faces(size, v_ref, dust_ref, terrain_ref, zm_ref, zp_ref, lay_ref, low, high):
    ncomp, nx, ny, nz = v_ref.shape
    ends = pick((16, nz), [(0, 0), (1, nz - 1)])
    low[...] = jnp.zeros_like(low)
    high[...] = jnp.zeros_like(high)
    for j in range(ncomp * nx):
        for half in range(ny // LANES):
            block = v_ref[j // nx, j % nx, half * LANES : (half + 1) * LANES, :].astype(BF)
            both = lax.dot_general(ends, block, (((1,), (1,)), ((), ())), preferred_element_type=F32)
            low[j : j + 1, half * LANES : (half + 1) * LANES] = both[0:1]
            high[j : j + 1, half * LANES : (half + 1) * LANES] = both[1:2]
    terrain = terrain_ref[...].astype(F32)
    terrain = jnp.concatenate([terrain, jnp.zeros((nx, LANES - size), F32)], 1)
    terrain = jnp.concatenate([terrain, jnp.zeros((16 - nx, LANES), F32)], 0)
    lane = iota((16, LANES), 1)
    whole = low[...]
    for t in range(lay_ref.shape[0]):
        shift = (EDGE - t * size) % ny
        moved = pltpu.roll(whole, shift, 1) if shift else whole
        row = lane + (t * size - EDGE)
        lay_ref[t] = jnp.where((row >= 0) & (row < ny), moved[:, :LANES], 0.0).astype(BF)
    nb = ny // LANES
    for half in range(nb):
        zm_ref[half * 16 : half * 16 + 16] = low[:, half * LANES : (half + 1) * LANES].astype(BF)
        zp_ref[half * 16 : half * 16 + 16] = high[:, half * LANES : (half + 1) * LANES].astype(BF)
    at = nb * 16
    zm_ref[at : at + nx * EDGE] = dust_ref[:, :EDGE].reshape(nx * EDGE, LANES).astype(BF)
    zp_ref[at : at + nx * EDGE] = dust_ref[:, size - EDGE :].reshape(nx * EDGE, LANES).astype(BF)
    at = at + nx * EDGE
    zm_ref[at : at + 16] = terrain.astype(BF)
    zp_ref[at : at + 16] = terrain.astype(BF)
    zm_ref[at + 16 : at + 32] = lay_ref[0]


def advance(v_ref, below_ref, above_ref, rm_ref, rp_ref, out_ref):
    _, nx, ny, nz = v_ref.shape
    comp = pl.program_id(0)
    row, lane = iota((LANES, nz), 0), iota((LANES, nz), 1)
    brow, blane = iota((LANES, nz), 0), iota((LANES, nz), 1)
    nb = ny // LANES
    for half in range(nb):
        a = half * LANES
        faces = jnp.concatenate(
            [
                rm_ref[half * 16 : half * 16 + 16].astype(F32),
                rp_ref[half * 16 : half * 16 + 16].astype(F32),
                jnp.zeros((LANES - 32, LANES), F32),
            ],
            0,
        )
        turned = faces.T.astype(BF)
        for x in range(nx):
            j = comp * nx + x
            place = ((brow == j) & (blane == nz - 1)) | ((brow == 16 + j) & (blane == 0))
            place = jnp.where(place, 1.0, 0.0).astype(BF)
            side = lax.dot_general(turned, place, (((1,), (0,)), ((), ())), preferred_element_type=F32)
            f = v_ref[0, x, a : a + LANES, :]
            near = side + jnp.where(lane == 0, 0.0, pltpu.roll(f, 1, 1))
            near = near + jnp.where(lane == nz - 1, 0.0, pltpu.roll(f, nz - 1, 1))
            prev = v_ref[0, x, a - 1 : a, :] if a else jnp.zeros((1, nz), F32)
            post = v_ref[0, x, a + LANES : a + LANES + 1, :] if a + LANES < ny else jnp.zeros((1, nz), F32)
            near = near + jnp.where(row == 0, prev, pltpu.roll(f, 1, 0))
            near = near + jnp.where(row == LANES - 1, post, pltpu.roll(f, LANES - 1, 0))
            near = near + (v_ref[0, x - 1, a : a + LANES, :] if x else below_ref[0, a : a + LANES, :].astype(F32))
            near = near + (
                v_ref[0, x + 1, a : a + LANES, :] if x < nx - 1 else above_ref[0, a : a + LANES, :].astype(F32)
            )
            out_ref[0, x, a : a + LANES, :] = f + 0.12 * (near - 6.0 * f)


def prepare(nstrips, *refs):
    strips = refs[:nstrips]
    lays = refs[nstrips : 2 * nstrips - 1]
    dust_ref, terrain_ref, eligible_ref, rm_ref, rp_ref = refs[2 * nstrips - 1 : 2 * nstrips + 4]
    wind_ref, conc_ref, cols_ref, up_ref, down_ref, edge_ref, raw = refs[2 * nstrips + 4 :]
    nx, size, nz = dust_ref.shape
    ncomp = strips[0].shape[0] // nx
    rows = size + 2 * EDGE
    place = lax.axis_index("vert")
    for t in range(nstrips):
        @pl.when(place == t)
        def _(t=t):
            raw[...] = strips[t][...]

    face = (rm_ref.shape[0] - 32 - nx * EDGE)
    zero = jnp.zeros((16, LANES), F32)
    layer = jnp.where(place == 0, rm_ref[face + nx * EDGE + 16 : face + nx * EDGE + 32].astype(F32), zero)
    layer = layer + jnp.where(place == 1, lays[0][1].astype(F32), zero)
    for got in lays[1:]:
        layer = layer + got[...].astype(F32)
    layer = jnp.concatenate([layer, jnp.zeros((LANES - 16, LANES), F32)], 0)
    turned = layer.T.astype(BF)[:rows]
    brow, blane = iota((LANES, nz), 0), iota((LANES, nz), 1)
    beside = jnp.where((brow == blane + 1) | (brow == blane - 1), 1.0, 0.0).astype(BF)
    for comp in range(ncomp):
        f = [raw[comp * nx + x].astype(F32) for x in range(nx)]
        for x in range(nx):
            j = comp * nx + x
            near = jnp.dot(raw[j], beside, preferred_element_type=F32)
            top = jnp.where((brow == j) & (blane == nz - 1), 1.0, 0.0).astype(BF)
            near = near + jnp.dot(turned, top, preferred_element_type=F32)
            near = near + pltpu.roll(f[x], 1, 0) + pltpu.roll(f[x], rows - 1, 0)
            if x:
                near = near + f[x - 1]
            if x < nx - 1:
                near = near + f[x + 1]
            wind = 0.28 * f[x] + 0.12 * near
            wind_ref[j] = wind
            if x == 0:
                down_ref[comp * rows : (comp + 1) * rows] = raw[j]
                down_ref[(ncomp + comp) * rows : (ncomp + comp + 1) * rows] = wind.astype(BF)
                edge_ref[comp] = raw[j]
            if x == nx - 1:
                up_ref[comp * rows : (comp + 1) * rows] = raw[j]
                up_ref[(ncomp + comp) * rows : (ncomp + comp + 1) * rows] = wind.astype(BF)
                edge_ref[ncomp + comp] = raw[j]
    for x in range(nx):
        before = rp_ref[face + x * EDGE : face + (x + 1) * EDGE].astype(F32)
        after = rm_ref[face + x * EDGE : face + (x + 1) * EDGE].astype(F32)
        conc_ref[x] = jnp.concatenate([before, dust_ref[x], after], 0)
    at = 2 * ncomp * rows
    up_ref[at : at + rows] = conc_ref[nx - 1].astype(BF)
    up_ref[at + rows : at + 2 * rows] = conc_ref[nx - 2].astype(BF)
    down_ref[at : at + rows] = conc_ref[0].astype(BF)
    down_ref[at + rows : at + 2 * rows] = conc_ref[1].astype(BF)
    at = at + 2 * rows
    lane = iota((nx, LANES), 1)
    own = terrain_ref[...].astype(F32)
    own = jnp.concatenate([own, jnp.zeros((nx, LANES - size), F32)], 1)
    here = face + nx * EDGE
    before = pltpu.roll(rp_ref[here : here + 16].astype(F32), (EDGE - size) % LANES, 1)[:nx]
    after = pltpu.roll(rm_ref[here : here + 16].astype(F32), (EDGE + size) % LANES, 1)[:nx]
    ground = jnp.where(lane < EDGE, before, jnp.where(lane < EDGE + size, pltpu.roll(own, EDGE, 1), after))
    y = lane + (place * size - EDGE)
    flags = jnp.zeros((nx, LANES), jnp.int32)
    blocks = eligible_ref.shape[1]
    for b in range(blocks):
        inside = (y >= b * 128) & (y < (b + 1) * 128)
        flags = jnp.where(inside, jnp.broadcast_to(eligible_ref[:, b : b + 1], (nx, LANES)), flags)
    lifted = jnp.where(flags == 1, ground, -1.0)
    cols_ref[...] = jnp.zeros_like(cols_ref)
    cols_ref[:nx] = ground
    cols_ref[EDGE : EDGE + nx] = lifted
    fill = jnp.zeros((14, LANES), F32)
    up_ref[at : at + 16] = jnp.concatenate([ground[nx - 1 :], lifted[nx - 1 :], fill], 0).astype(BF)
    down_ref[at : at + 16] = jnp.concatenate([ground[:1], lifted[:1], fill], 0).astype(BF)


def transport(ny, nhoriz, wind_ref, edge_ref, conc_ref, cols_ref, below_ref, above_ref, out_ref):
    nx, size, nz = out_ref.shape
    ncomp = edge_ref.shape[0] // 2
    rows = size + 2 * EDGE
    column, place = (lax.axis_index("horiz"), lax.axis_index("vert"))
    at = 2 * ncomp * rows
    here = at + 2 * rows

    def part(ref, i):
        return ref[i * rows : (i + 1) * rows].astype(F32)

    conc = [part(below_ref, 2 * ncomp + 1), part(below_ref, 2 * ncomp)]
    conc += [conc_ref[x] for x in range(nx)]
    conc += [part(above_ref, 2 * ncomp), part(above_ref, 2 * ncomp + 1)]
    table = jnp.concatenate(
        [
            below_ref[here : here + 16].astype(F32),
            cols_ref[...],
            above_ref[here : here + 16].astype(F32),
            jnp.zeros((LANES - 48, LANES), F32),
        ],
        0,
    ).T[:rows]
    ground = [0] + [16 + x for x in range(nx)] + [32]
    lifted = [1] + [16 + EDGE + x for x in range(nx)] + [33]
    layer = iota((rows, nz), 1).astype(F32)
    y = iota((rows, nz), 0) + (place * size - EDGE)
    inside = (y >= 0) & (y < ny)
    first, last = layer == 0.0, layer == nz - 1.0
    zero = jnp.zeros((rows, nz), F32)
    state = [None] * (nx + 2)
    for p in range(nx + 2):
        comps = []
        for comp in range(ncomp):
            if p == 0:
                w = part(below_ref, ncomp + comp) + 0.12 * edge_ref[comp].astype(F32)
            elif p == nx + 1:
                w = part(above_ref, ncomp + comp) + 0.12 * edge_ref[ncomp + comp].astype(F32)
            else:
                w = wind_ref[comp * nx + p - 1]
                if p == 1:
                    w = w + 0.12 * part(below_ref, comp)
                if p == nx:
                    w = w + 0.12 * part(above_ref, comp)
            comps.append(w)
        gu, gv, gw = comps
        speed = jnp.sqrt(gu * gu + gv * gv)
        rise = jnp.broadcast_to(table[:, lifted[p] : lifted[p] + 1], (rows, nz))
        base = jnp.broadcast_to(table[:, ground[p] : ground[p] + 1], (rows, nz))
        lift = jnp.where(layer == rise, 0.5 * jnp.maximum(speed - 1.0, 0.0), 0.0)
        keep = (layer >= base) & inside
        if p == 0:
            keep = keep & (column > 0)
        if p == nx + 1:
            keep = keep & (column < nhoriz - 1)
        coef = [
            (0.15 * (0.1 - jnp.minimum(a, 0.0)), 0.15 * (0.1 + jnp.maximum(a, 0.0)))
            for a in (gu, gv, gw - 0.5)
        ]
        state[p] = (coef, lift, keep)

    def step(p, c, below, above):
        coef, lift, keep = state[p]
        total = c + lift
        pairs = (
            (above, below),
            (pltpu.roll(c, rows - 1, 0), pltpu.roll(c, 1, 0)),
            (
                jnp.where(last, zero, pltpu.roll(c, nz - 1, 1)),
                jnp.where(first, zero, pltpu.roll(c, 1, 1)),
            ),
        )
        for (ahead, behind), (post, prev) in zip(coef, pairs):
            total = total + ahead * (post - c) - behind * (c - prev)
        return jnp.where(keep, total, 0.0)

    once = [step(p, conc[p + 1], conc[p], conc[p + 2]) for p in range(nx + 2)]
    for x in range(nx):
        twice = step(x + 1, once[x + 1], once[x], once[x + 2])
        out_ref[x] = twice[EDGE : EDGE + size]


def local(velocity, dust, eligible, terrain):
    ncomp, nx, ny, nz = velocity.shape
    size = dust.shape[1]
    nh, nv = (lax.axis_size("horiz"), lax.axis_size("vert"))
    rows = size + 2 * EDGE
    up = [(i, i + 1) for i in range(nh - 1)]
    down = [(j, i) for i, j in up]
    rise = [(i, i + 1) for i in range(nv - 1)]
    fall = [(j, i) for i, j in rise]
    nplane = ncomp * nx

    packed = call(
        pack_strips,
        [shaped(nplane, rows, LANES)] * nv + [shaped(ncomp, ny, nz)] * 2,
        "pack_strips",
    )(velocity)
    strips = list(packed[:nv])
    got = [strips[0]] + [lax.ppermute(strips[t], "vert", [(0, t)]) for t in range(1, nv)]
    below = lax.ppermute(packed[nv], "horiz", up)
    above = lax.ppermute(packed[nv + 1], "horiz", down)

    face = ny // LANES * 16
    zm, zp, lay = call(
        functools.partial(pack_faces, size),
        [shaped(face + nx * EDGE + 32, LANES), shaped(face + nx * EDGE + 16, LANES), shaped(nv, 16, LANES)],
        "pack_faces",
        [pltpu.VMEM((16, ny), F32)] * 2,
    )(velocity, dust, terrain)
    rm = lax.ppermute(zm, "vert", fall)
    rp = lax.ppermute(zp, "vert", rise)
    lays = [lay] + [lax.ppermute(lay[t], "vert", [(1, t)]) for t in range(2, nv)]

    whole = pl.BlockSpec(memory_space=pltpu.VMEM)
    velocity_next = call(
        advance,
        jax.ShapeDtypeStruct(velocity.shape, F32),
        "advance",
        grid=(ncomp,),
        in_specs=[
            pl.BlockSpec((1, nx, ny, nz), lambda i: (i, 0, 0, 0)),
            pl.BlockSpec((1, ny, nz), lambda i: (i, 0, 0)),
            pl.BlockSpec((1, ny, nz), lambda i: (i, 0, 0)),
            whole,
            whole,
        ],
        out_specs=pl.BlockSpec((1, nx, ny, nz), lambda i: (i, 0, 0, 0)),
    )(velocity, below, above, rm, rp)

    wire = (2 * ncomp + 2) * rows + 16
    wind, conc, cols, mu, md, edge = call(
        functools.partial(prepare, nv),
        [
            shaped(nplane, rows, LANES, dtype=F32),
            shaped(nx, rows, LANES, dtype=F32),
            shaped(16, LANES, dtype=F32),
            shaped(wire, LANES),
            shaped(wire, LANES),
            shaped(2 * ncomp, rows, LANES),
        ],
        "prepare",
        [pltpu.VMEM((nplane, rows, LANES), BF)],
    )(*got, *lays, dust, terrain, eligible, rm, rp)
    mu = lax.ppermute(mu, "horiz", up)
    md = lax.ppermute(md, "horiz", down)
    dust_next = call(
        functools.partial(transport, ny, nh),
        jax.ShapeDtypeStruct(dust.shape, F32),
        "transport",
    )(wind, edge, conc, cols, mu, md)
    return (velocity_next, dust_next)


def solution(mesh):
    placed = (
        P(None, "horiz", None, "vert"),
        P("horiz", "vert", None),
        P("horiz", None),
        P("horiz", "vert"),
    )
    return jax.shard_map(
        local,
        mesh=mesh,
        in_specs=placed,
        out_specs=(P(None, "horiz", None, "vert"), P("horiz", "vert", None)),
        check_vma=False,
    )
```

```python
import functools

import jax
import jax.numpy as jnp
from jax import lax
from jax.experimental import pallas as pl
from jax.experimental.pallas import tpu as pltpu
from jax.sharding import PartitionSpec as P

DSTEPS = 2
LANES = 128
EDGE = 8
BF = jnp.bfloat16
F32 = jnp.float32

VMEM = pl.BlockSpec(memory_space=pltpu.VMEM)


def call(kernel, out_shape, name, scratch=(), cost=1 << 20, **kwargs):
    return pl.pallas_call(
        kernel,
        out_shape=out_shape,
        scratch_shapes=list(scratch),
        compiler_params=pltpu.CompilerParams(vmem_limit_bytes=40 << 20),
        cost_estimate=pl.CostEstimate(flops=cost, bytes_accessed=cost, transcendentals=0),
        name=name,
        **kwargs,
    )


def shaped(*dims, dtype=BF):
    return jax.ShapeDtypeStruct(dims, dtype)


def iota(shape, dim):
    return lax.broadcasted_iota(jnp.int32, shape, dim)


def pick(shape, pairs):
    row, col = iota(shape, 0), iota(shape, 1)
    hit = functools.reduce(jnp.logical_or, [(row == r) & (col == c) for r, c in pairs])
    return jnp.where(hit, 1.0, 0.0).astype(BF)


def pack_strips(size, v_ref, *refs):
    outs, (buf, side, sems) = (refs[:-3], refs[-3:])
    ncomp, nx, ny, nz = v_ref.shape

    @pl.when(lax.axis_index("vert") == 0)
    def _():
        copies = [pltpu.make_async_copy(v_ref.at[c], buf.at[c], sems.at[c]) for c in range(ncomp)]
        for copy in copies:
            copy.start()
        side[...] = jnp.zeros_like(side)
        for comp in range(ncomp):
            copies[comp].wait()
            for t, out in enumerate(outs):
                for x in range(nx):
                    j = comp * nx + x
                    out[j * size : (j + 1) * size] = buf[comp, x, t * size : (t + 1) * size, :].astype(BF)
                    for i, y in enumerate(halo_rows(t * size, size)):
                        if 0 <= y < ny:
                            side[t, i * 16 + j : i * 16 + j + 1] = buf[comp, x, y : y + 1, :]
        for t, out in enumerate(outs):
            out[ncomp * nx * size :] = side[t].astype(BF)


def halo_rows(start, size):
    return (start - 2, start - 1, start + size, start + size + 1)


def pack_sides(v_ref, rm_ref, far_ref, near_ref):
    del rm_ref
    nx = v_ref.shape[1]
    odd = lax.rem(lax.axis_index("horiz"), 2) == 1

    @pl.when(odd)
    def _():
        near_ref[...] = v_ref[:, 0].astype(BF)
        far_ref[...] = v_ref[:, nx - 1].astype(BF)

    @pl.when(jnp.logical_not(odd))
    def _():
        near_ref[...] = v_ref[:, nx - 1].astype(BF)
        far_ref[...] = v_ref[:, 0].astype(BF)


def pack_ends(size, v_ref, dust_ref, terrain_ref, strip_ref, zm_ref, zp_ref, lay_ref, low, high):
    del strip_ref
    ncomp, nx, ny, nz = v_ref.shape
    ends = pick((16, nz), [(0, 0), (1, nz - 1)])
    low[...] = jnp.zeros_like(low)
    high[...] = jnp.zeros_like(high)
    nb = ny // LANES
    for j in range(ncomp * nx):
        for half in range(nb):
            block = v_ref[j // nx, j % nx, half * LANES : (half + 1) * LANES, :].astype(BF)
            both = lax.dot_general(ends, block, (((1,), (1,)), ((), ())), preferred_element_type=F32)
            low[j : j + 1, half * LANES : (half + 1) * LANES] = both[0:1]
            high[j : j + 1, half * LANES : (half + 1) * LANES] = both[1:2]
    terrain = terrain_ref[...].astype(F32)
    terrain = jnp.concatenate([terrain, jnp.zeros((nx, LANES - size), F32)], 1)
    terrain = jnp.concatenate([terrain, jnp.zeros((16 - nx, LANES), F32)], 0)
    lane = iota((16, LANES), 1)
    whole = low[...]
    for t in range(lay_ref.shape[0]):
        shift = (EDGE - t * size) % ny
        moved = pltpu.roll(whole, shift, 1) if shift else whole
        row = lane + (t * size - EDGE)
        lay_ref[t] = jnp.where((row >= 0) & (row < ny), moved[:, :LANES], 0.0).astype(BF)
    for half in range(nb):
        zm_ref[half * 16 : half * 16 + 16] = low[:, half * LANES : (half + 1) * LANES].astype(BF)
        zp_ref[half * 16 : half * 16 + 16] = high[:, half * LANES : (half + 1) * LANES].astype(BF)
    at = nb * 16
    zm_ref[at : at + nx * EDGE] = dust_ref[:, :EDGE].reshape(nx * EDGE, LANES).astype(BF)
    zp_ref[at : at + nx * EDGE] = dust_ref[:, size - EDGE :].reshape(nx * EDGE, LANES).astype(BF)
    at = at + nx * EDGE
    zm_ref[at : at + 16] = terrain.astype(BF)
    zp_ref[at : at + 16] = terrain.astype(BF)
    zm_ref[at + 16 : at + 32] = lay_ref[0]
    zp_ref[at + 16 : at + 32] = lay_ref[min(2, lay_ref.shape[0] - 1)]


def advance(v_ref, far_ref, near_ref, rm_ref, rp_ref, out_ref, buf, sems):
    ncomp, nx, ny, nz = v_ref.shape
    odd = lax.rem(lax.axis_index("horiz"), 2) == 1
    row, lane = iota((LANES, nz), 0), iota((LANES, nz), 1)
    nb = ny // LANES
    turned = []
    for half in range(nb):
        faces = jnp.concatenate(
            [
                rm_ref[half * 16 : half * 16 + 16].astype(F32),
                rp_ref[half * 16 : half * 16 + 16].astype(F32),
                jnp.zeros((LANES - 32, LANES), F32),
            ],
            0,
        )
        turned.append(faces.T.astype(BF))
    copies = []
    for comp in range(ncomp):
        for half in range(nb):
            a = half * LANES
            span = slice(a, a + LANES)
            near, far = (near_ref[comp, span, :].astype(F32), far_ref[comp, span, :].astype(F32))
            below = jnp.where(odd, near, far)
            above = jnp.where(odd, far, near)
            for x in range(nx):
                j = comp * nx + x
                place = ((row == j) & (lane == nz - 1)) | ((row == 16 + j) & (lane == 0))
                place = jnp.where(place, 1.0, 0.0).astype(BF)
                sums = lax.dot_general(turned[half], place, (((1,), (0,)), ((), ())), preferred_element_type=F32)
                f = v_ref[comp, x, span, :]
                sums = sums + jnp.where(lane == 0, 0.0, pltpu.roll(f, 1, 1))
                sums = sums + jnp.where(lane == nz - 1, 0.0, pltpu.roll(f, nz - 1, 1))
                prev = v_ref[comp, x, a - 1 : a, :] if a else jnp.zeros((1, nz), F32)
                post = v_ref[comp, x, a + LANES : a + LANES + 1, :] if half < nb - 1 else jnp.zeros((1, nz), F32)
                sums = sums + jnp.where(row == 0, prev, pltpu.roll(f, 1, 0))
                sums = sums + jnp.where(row == LANES - 1, post, pltpu.roll(f, LANES - 1, 0))
                sums = sums + (v_ref[comp, x - 1, span, :] if x else below)
                sums = sums + (v_ref[comp, x + 1, span, :] if x < nx - 1 else above)
                buf[comp, x, span, :] = f + 0.12 * (sums - 6.0 * f)
        copies.append(pltpu.make_async_copy(buf.at[comp], out_ref.at[comp], sems.at[comp]))
        copies[-1].start()
    for copy in copies:
        copy.wait()


def prepare(nstrips, *refs):
    strips = refs[:nstrips]
    nlay = max(nstrips - 2, 1)
    lays = refs[nstrips : nstrips + nlay]
    dust_ref, terrain_ref, eligible_ref, rm_ref, rp_ref = refs[nstrips + nlay : nstrips + nlay + 5]
    wind_ref, conc_ref, cols_ref, far_ref, near_ref, edge_ref, frame = refs[nstrips + nlay + 5 :]
    nx, size, nz = dust_ref.shape
    nplane = frame.shape[0]
    ncomp = nplane // nx
    rows = size + 2 * EDGE
    place = lax.axis_index("vert")
    odd = lax.rem(lax.axis_index("horiz"), 2) == 1
    frame[:, :EDGE] = jnp.zeros((nplane, EDGE, nz), F32)
    frame[:, EDGE + size :] = jnp.zeros((nplane, EDGE, nz), F32)
    for t in range(nstrips):
        @pl.when(place == t)
        def _(t=t):
            beside = strips[t][nplane * size :].astype(F32)
            for j in range(nplane):
                frame[j, EDGE : EDGE + size] = strips[t][j * size : (j + 1) * size].astype(F32)
                for i, y in enumerate(halo_rows(EDGE, size)):
                    frame[j, y : y + 1] = beside[i * 16 + j : i * 16 + j + 1]

    face = rm_ref.shape[0] - 32 - nx * EDGE
    last = face + nx * EDGE + 16
    zero = jnp.zeros((16, LANES), F32)
    layer = jnp.where(place == 0, rm_ref[last : last + 16].astype(F32), zero)
    layer = layer + jnp.where(place == 1, lays[0][min(1, nstrips - 1)].astype(F32), zero)
    layer = layer + jnp.where(place == 2, rp_ref[last : last + 16].astype(F32), zero)
    for got in lays[1:]:
        layer = layer + got[...].astype(F32)
    layer = jnp.concatenate([layer, jnp.zeros((LANES - 16, LANES), F32)], 0)
    turned = layer.T.astype(BF)[:rows]
    brow, blane = iota((LANES, nz), 0), iota((LANES, nz), 1)
    beside = jnp.where((brow == blane + 1) | (brow == blane - 1), 1.0, 0.0).astype(BF)
    edges = {}
    for comp in range(ncomp):
        f = [frame[comp * nx + x] for x in range(nx)]
        for x in range(nx):
            j = comp * nx + x
            raw = f[x].astype(BF)
            near = jnp.dot(raw, beside, preferred_element_type=F32)
            top = jnp.where((brow == j) & (blane == nz - 1), 1.0, 0.0).astype(BF)
            near = near + jnp.dot(turned, top, preferred_element_type=F32)
            near = near + pltpu.roll(f[x], 1, 0) + pltpu.roll(f[x], rows - 1, 0)
            if x:
                near = near + f[x - 1]
            if x < nx - 1:
                near = near + f[x + 1]
            wind = 0.28 * f[x] + 0.12 * near
            wind_ref[j] = wind
            if x == 0:
                edge_ref[comp] = raw
            if x == nx - 1:
                edge_ref[ncomp + comp] = raw
    for x in range(nx):
        before = rp_ref[face + x * EDGE : face + (x + 1) * EDGE].astype(F32)
        after = rm_ref[face + x * EDGE : face + (x + 1) * EDGE].astype(F32)
        conc_ref[x] = jnp.concatenate([before, dust_ref[x], after], 0)
    lane = iota((nx, LANES), 1)
    own = terrain_ref[...].astype(F32)
    own = jnp.concatenate([own, jnp.zeros((nx, LANES - size), F32)], 1)
    here = face + nx * EDGE
    before = pltpu.roll(rp_ref[here : here + 16].astype(F32), (EDGE - size) % LANES, 1)[:nx]
    after = pltpu.roll(rm_ref[here : here + 16].astype(F32), (EDGE + size) % LANES, 1)[:nx]
    ground = jnp.where(lane < EDGE, before, jnp.where(lane < EDGE + size, pltpu.roll(own, EDGE, 1), after))
    y = lane + (place * size - EDGE)
    flags = jnp.zeros((nx, LANES), jnp.int32)
    for b in range(eligible_ref.shape[1]):
        inside = (y >= b * 128) & (y < (b + 1) * 128)
        flags = jnp.where(inside, jnp.broadcast_to(eligible_ref[:, b : b + 1], (nx, LANES)), flags)
    lifted = jnp.where(flags == 1, ground, -1.0)
    cols_ref[...] = jnp.zeros_like(cols_ref)
    cols_ref[:nx] = ground
    cols_ref[EDGE : EDGE + nx] = lifted
    fill = jnp.zeros((14, LANES), F32)

    def send(ref, x, inner):
        for comp in range(ncomp):
            ref[comp * rows : (comp + 1) * rows] = edge_ref[(ncomp if x else 0) + comp]
            ref[(ncomp + comp) * rows : (ncomp + comp + 1) * rows] = wind_ref[comp * nx + x].astype(BF)
        at = 2 * ncomp * rows
        ref[at : at + rows] = conc_ref[x].astype(BF)
        ref[at + rows : at + 2 * rows] = conc_ref[inner].astype(BF)
        at = at + 2 * rows
        ref[at : at + 16] = jnp.concatenate([ground[x : x + 1], lifted[x : x + 1], fill], 0).astype(BF)

    @pl.when(odd)
    def _():
        send(near_ref, 0, 1)
        send(far_ref, nx - 1, nx - 2)

    @pl.when(jnp.logical_not(odd))
    def _():
        send(near_ref, nx - 1, nx - 2)
        send(far_ref, 0, 1)


def transport(ny, nhoriz, wind_ref, edge_ref, conc_ref, cols_ref, far_ref, near_ref, out_ref):
    nx, size, nz = out_ref.shape
    ncomp = edge_ref.shape[0] // 2
    rows = size + 2 * EDGE
    column, place = (lax.axis_index("horiz"), lax.axis_index("vert"))
    odd = lax.rem(column, 2) == 1
    here = 2 * (ncomp + 1) * rows

    def below(start, n):
        return jnp.where(odd, near_ref[start : start + n].astype(F32), far_ref[start : start + n].astype(F32))

    def above(start, n):
        return jnp.where(odd, far_ref[start : start + n].astype(F32), near_ref[start : start + n].astype(F32))

    def part(side, i):
        return side(i * rows, rows)

    conc = [part(below, 2 * ncomp + 1), part(below, 2 * ncomp)]
    conc += [conc_ref[x] for x in range(nx)]
    conc += [part(above, 2 * ncomp), part(above, 2 * ncomp + 1)]
    table = jnp.concatenate(
        [below(here, 16), cols_ref[...], above(here, 16), jnp.zeros((LANES - 48, LANES), F32)], 0
    ).T[:rows]
    ground = [0] + [16 + x for x in range(nx)] + [32]
    lifted = [1] + [16 + EDGE + x for x in range(nx)] + [33]
    layer = iota((rows, nz), 1).astype(F32)
    y = iota((rows, nz), 0) + (place * size - EDGE)
    inside = (y >= 0) & (y < ny)
    first, last = layer == 0.0, layer == nz - 1.0
    zero = jnp.zeros((rows, nz), F32)
    state = [None] * (nx + 2)
    for p in range(nx + 2):
        comps = []
        for comp in range(ncomp):
            if p == 0:
                w = part(below, ncomp + comp) + 0.12 * edge_ref[comp].astype(F32)
            elif p == nx + 1:
                w = part(above, ncomp + comp) + 0.12 * edge_ref[ncomp + comp].astype(F32)
            else:
                w = wind_ref[comp * nx + p - 1]
                if p == 1:
                    w = w + 0.12 * part(below, comp)
                if p == nx:
                    w = w + 0.12 * part(above, comp)
            comps.append(w)
        gu, gv, gw = comps
        speed = jnp.sqrt(gu * gu + gv * gv)
        rise = jnp.broadcast_to(table[:, lifted[p] : lifted[p] + 1], (rows, nz))
        base = jnp.broadcast_to(table[:, ground[p] : ground[p] + 1], (rows, nz))
        lift = jnp.where(layer == rise, 0.5 * jnp.maximum(speed - 1.0, 0.0), 0.0)
        keep = (layer >= base) & inside
        if p == 0:
            keep = keep & (column > 0)
        if p == nx + 1:
            keep = keep & (column < nhoriz - 1)
        coef = [
            (0.15 * (0.1 - jnp.minimum(a, 0.0)), 0.15 * (0.1 + jnp.maximum(a, 0.0)))
            for a in (gu, gv, gw - 0.5)
        ]
        state[p] = (coef, lift, keep)

    def step(p, c, behind, ahead):
        coef, lift, keep = state[p]
        total = c + lift
        pairs = (
            (ahead, behind),
            (pltpu.roll(c, rows - 1, 0), pltpu.roll(c, 1, 0)),
            (
                jnp.where(last, zero, pltpu.roll(c, nz - 1, 1)),
                jnp.where(first, zero, pltpu.roll(c, 1, 1)),
            ),
        )
        for (forward, back), (post, prev) in zip(coef, pairs):
            total = total + forward * (post - c) - back * (c - prev)
        return jnp.where(keep, total, 0.0)

    once = [step(p, conc[p + 1], conc[p], conc[p + 2]) for p in range(nx + 2)]
    for x in range(nx):
        twice = step(x + 1, once[x + 1], once[x], once[x + 2])
        out_ref[x] = twice[EDGE : EDGE + size]


def local(velocity, dust, eligible, terrain):
    ncomp, nx, ny, nz = velocity.shape
    size = dust.shape[1]
    nh, nv = (lax.axis_size("horiz"), lax.axis_size("vert"))
    rows = size + 2 * EDGE
    rise = [(i, i + 1) for i in range(nv - 1)]
    fall = [(j, i) for i, j in rise]
    near_pairs = [p for i in range(0, nh - 1, 2) for p in ((i, i + 1), (i + 1, i))]
    far_pairs = [p for i in range(1, nh - 1, 2) for p in ((i, i + 1), (i + 1, i))]
    nplane = ncomp * nx
    anywhere = pl.BlockSpec(memory_space=pl.ANY)

    strips = call(
        functools.partial(pack_strips, size),
        [shaped(nplane * size + 64, LANES)] * nv,
        "pack_strips",
        [
            pltpu.VMEM((ncomp, nx, ny, nz), F32),
            pltpu.VMEM((nv, 64, LANES), F32),
            pltpu.SemaphoreType.DMA((ncomp,)),
        ],
        in_specs=[anywhere],
        out_specs=[VMEM] * nv,
    )(pltpu.with_memory_space_constraint(velocity, pltpu.HBM))
    got = [strips[0]] + [lax.ppermute(strips[t], "vert", [(0, t)]) for t in range(1, nv)]

    face = ny // LANES * 16
    zm, zp, lay = call(
        functools.partial(pack_ends, size),
        [shaped(face + nx * EDGE + 32, LANES)] * 2 + [shaped(nv, 16, LANES)],
        "pack_ends",
        [pltpu.VMEM((16, ny), F32)] * 2,
        in_specs=[VMEM] * 3 + [anywhere],
    )(velocity, dust, terrain, strips[-1])
    rm = lax.ppermute(zm, "vert", fall)
    rp = lax.ppermute(zp, "vert", rise)
    lays = [lay] + [lax.ppermute(lay[t], "vert", [(1, t)]) for t in range(3, nv)]

    far, near = call(pack_sides, [shaped(ncomp, ny, nz)] * 2, "pack_sides", in_specs=[VMEM, anywhere])(
        velocity, rm
    )
    far = lax.ppermute(far, "horiz", far_pairs)
    near = lax.ppermute(near, "horiz", near_pairs)

    velocity_next = call(
        advance,
        jax.ShapeDtypeStruct(velocity.shape, F32),
        "advance",
        [pltpu.VMEM((ncomp, nx, ny, nz), F32), pltpu.SemaphoreType.DMA((ncomp,))],
        in_specs=[VMEM] * 5,
        out_specs=anywhere,
    )(velocity, far, near, rm, rp)

    wire = (2 * ncomp + 2) * rows + 16
    wind, conc, cols, mf, mn, edge = call(
        functools.partial(prepare, nv),
        [
            shaped(nplane, rows, LANES, dtype=F32),
            shaped(nx, rows, LANES, dtype=F32),
            shaped(16, LANES, dtype=F32),
            shaped(wire, LANES),
            shaped(wire, LANES),
            shaped(2 * ncomp, rows, LANES),
        ],
        "prepare",
        [pltpu.VMEM((nplane, rows, LANES), F32)],
    )(*got, *lays, dust, terrain, eligible, rm, rp)
    mf = lax.ppermute(mf, "horiz", far_pairs)
    mn = lax.ppermute(mn, "horiz", near_pairs)
    dust_next = call(
        functools.partial(transport, ny, nh),
        jax.ShapeDtypeStruct(dust.shape, F32),
        "transport",
    )(wind, edge, conc, cols, mf, mn)
    return (velocity_next, dust_next)


def solution(mesh):
    placed = (
        P(None, "horiz", None, "vert"),
        P("horiz", "vert", None),
        P("horiz", None),
        P("horiz", "vert"),
    )
    return jax.shard_map(
        local,
        mesh=mesh,
        in_specs=placed,
        out_specs=(P(None, "horiz", None, "vert"), P("horiz", "vert", None)),
        check_vma=False,
    )
```

```python
import functools

import jax
import jax.numpy as jnp
from jax import lax
from jax.experimental import pallas as pl
from jax.experimental.pallas import tpu as pltpu
from jax.sharding import PartitionSpec as P

DSTEPS = 2
LANES = 128
EDGE = 8
BF = jnp.bfloat16
F32 = jnp.float32

VMEM = pl.BlockSpec(memory_space=pltpu.VMEM)


def call(kernel, out_shape, name, scratch=(), cost=1 << 20, **kwargs):
    return pl.pallas_call(
        kernel,
        out_shape=out_shape,
        scratch_shapes=list(scratch),
        compiler_params=pltpu.CompilerParams(vmem_limit_bytes=40 << 20),
        cost_estimate=pl.CostEstimate(flops=cost, bytes_accessed=cost, transcendentals=0),
        name=name,
        **kwargs,
    )


def shaped(*dims, dtype=BF):
    return jax.ShapeDtypeStruct(dims, dtype)


def iota(shape, dim):
    return lax.broadcasted_iota(jnp.int32, shape, dim)


def pick(shape, pairs):
    row, col = iota(shape, 0), iota(shape, 1)
    hit = functools.reduce(jnp.logical_or, [(row == r) & (col == c) for r, c in pairs])
    return jnp.where(hit, 1.0, 0.0).astype(BF)


def pack_low(size, v_ref, *refs):
    outs, (buf, side, sems) = (refs[:-3], refs[-3:])
    ncomp, nx, ny, nz = v_ref.shape

    @pl.when(lax.axis_index("vert") == 0)
    def _():
        copies = [pltpu.make_async_copy(v_ref.at[c], buf.at[c], sems.at[c]) for c in range(ncomp)]
        for copy in copies:
            copy.start()
        side[...] = jnp.zeros_like(side)
        for comp in range(ncomp):
            copies[comp].wait()
            for t, out in enumerate(outs):
                for x in range(nx):
                    j = comp * nx + x
                    out[j * size : (j + 1) * size] = buf[comp, x, t * size : (t + 1) * size, :].astype(BF)
                    for i, y in enumerate(halo_rows(t * size, size)):
                        if 0 <= y < ny:
                            side[t, i * 16 + j : i * 16 + j + 1] = buf[comp, x, y : y + 1, :]
        for t, out in enumerate(outs):
            out[ncomp * nx * size :] = side[t].astype(BF)


def gate(*refs):
    del refs


def turn_faces(v_ref, comp, ends, outs):
    _, nx, ny, _ = v_ref.shape
    for x in range(nx):
        j = comp * nx + x
        for half in range(ny // LANES):
            span = slice(half * LANES, (half + 1) * LANES)
            block = v_ref[comp, x, span, :].astype(BF)
            rows = lax.dot_general(ends, block, (((1,), (1,)), ((), ())), preferred_element_type=F32)
            for i, out in enumerate(outs):
                out[j : j + 1, span] = rows[i : i + 1]


def halo_rows(start, size):
    return (start - 2, start - 1, start + size, start + size + 1)


def pack_sides(v_ref, after_ref, far_ref, near_ref):
    del after_ref
    nx = v_ref.shape[1]
    odd = lax.rem(lax.axis_index("horiz"), 2) == 1

    @pl.when(odd)
    def _():
        near_ref[...] = v_ref[:, 0].astype(BF)
        far_ref[...] = v_ref[:, nx - 1].astype(BF)

    @pl.when(jnp.logical_not(odd))
    def _():
        near_ref[...] = v_ref[:, nx - 1].astype(BF)
        far_ref[...] = v_ref[:, 0].astype(BF)


def pack_ends(size, nstrips, v_ref, dust_ref, terrain_ref, after_ref, first_ref, second_ref, mine_ref, *refs):
    del after_ref
    lays, (low, high, dusts, land, sems) = (refs[:-5], refs[-5:])
    ncomp, nx, ny, nz = v_ref.shape
    odd = lax.rem(lax.axis_index("vert"), 2) == 1
    copies = [
        pltpu.make_async_copy(dust_ref.at[:, :EDGE], dusts.at[0], sems.at[0]),
        pltpu.make_async_copy(dust_ref.at[:, size - EDGE :], dusts.at[1], sems.at[1]),
        pltpu.make_async_copy(terrain_ref, land, sems.at[2]),
    ]
    for copy in copies:
        copy.start()
    low[...] = jnp.zeros_like(low)
    high[...] = jnp.zeros_like(high)
    ends = pick((16, nz), [(0, 0), (1, nz - 1)])
    for comp in range(ncomp):
        turn_faces(v_ref, comp, ends, [low, high])
    lane = iota((16, LANES), 1)
    whole = low[...]
    for t in range(nstrips):
        shift = (EDGE - t * size) % ny
        moved = pltpu.roll(whole, shift, 1) if shift else whole
        row = lane + (t * size - EDGE)
        part = jnp.where((row >= 0) & (row < ny), moved[:, :LANES], 0.0).astype(BF)
        if t < 3:
            mine_ref[t] = part
        else:
            lays[t - 3][...] = part
    for copy in copies:
        copy.wait()
    terrain = land[...].astype(F32)
    terrain = jnp.concatenate([terrain, jnp.zeros((nx, LANES - size), F32)], 1)
    terrain = jnp.concatenate([terrain, jnp.zeros((16 - nx, LANES), F32)], 0)

    def send(ref, face, which, layer):
        for half in range(ny // LANES):
            ref[half * 16 : half * 16 + 16] = face[:, half * LANES : (half + 1) * LANES].astype(BF)
        at = ny // LANES * 16
        ref[at : at + nx * EDGE] = dusts[which].reshape(nx * EDGE, LANES).astype(BF)
        at = at + nx * EDGE
        ref[at : at + 16] = terrain.astype(BF)
        ref[at + 16 : at + 32] = mine_ref[layer]

    @pl.when(odd)
    def _():
        send(first_ref, low, 0, 0)
        send(second_ref, high, 1, 2)

    @pl.when(jnp.logical_not(odd))
    def _():
        send(first_ref, high, 1, 2)
        send(second_ref, low, 0, 0)


def sorted_ends(first_ref, second_ref, start, n):
    odd = lax.rem(lax.axis_index("vert"), 2) == 1
    first, second = (first_ref[start : start + n].astype(F32), second_ref[start : start + n].astype(F32))
    return (jnp.where(odd, second, first), jnp.where(odd, first, second))


def advance(v_ref, far_ref, near_ref, first_ref, second_ref, out_ref, buf, sems):
    ncomp, nx, ny, nz = v_ref.shape
    odd = lax.rem(lax.axis_index("horiz"), 2) == 1
    row, lane = iota((LANES, nz), 0), iota((LANES, nz), 1)
    nb = ny // LANES
    turned = []
    for half in range(nb):
        over, under = sorted_ends(first_ref, second_ref, half * 16, 16)
        faces = jnp.concatenate([over, under, jnp.zeros((LANES - 32, LANES), F32)], 0)
        turned.append(faces.T.astype(BF))
    copies = []
    for comp in range(ncomp):
        for half in range(nb):
            a = half * LANES
            span = slice(a, a + LANES)
            near, far = (near_ref[comp, span, :].astype(F32), far_ref[comp, span, :].astype(F32))
            below = jnp.where(odd, near, far)
            above = jnp.where(odd, far, near)
            for x in range(nx):
                j = comp * nx + x
                place = ((row == j) & (lane == nz - 1)) | ((row == 16 + j) & (lane == 0))
                place = jnp.where(place, 1.0, 0.0).astype(BF)
                sums = lax.dot_general(turned[half], place, (((1,), (0,)), ((), ())), preferred_element_type=F32)
                f = v_ref[comp, x, span, :]
                sums = sums + jnp.where(lane == 0, 0.0, pltpu.roll(f, 1, 1))
                sums = sums + jnp.where(lane == nz - 1, 0.0, pltpu.roll(f, nz - 1, 1))
                prev = v_ref[comp, x, a - 1 : a, :] if a else jnp.zeros((1, nz), F32)
                post = v_ref[comp, x, a + LANES : a + LANES + 1, :] if half < nb - 1 else jnp.zeros((1, nz), F32)
                sums = sums + jnp.where(row == 0, prev, pltpu.roll(f, 1, 0))
                sums = sums + jnp.where(row == LANES - 1, post, pltpu.roll(f, LANES - 1, 0))
                sums = sums + (v_ref[comp, x - 1, span, :] if x else below)
                sums = sums + (v_ref[comp, x + 1, span, :] if x < nx - 1 else above)
                buf[comp, x, span, :] = f + 0.12 * (sums - 6.0 * f)
        copies.append(pltpu.make_async_copy(buf.at[comp], out_ref.at[comp], sems.at[comp]))
        copies[-1].start()
    for copy in copies:
        copy.wait()


def prepare(nstrips, *refs):
    strips = refs[:nstrips]
    nlay = 1 + max(nstrips - 3, 0)
    lays = refs[nstrips : nstrips + nlay]
    dust_ref, terrain_ref, eligible_ref, first_ref, second_ref = refs[nstrips + nlay : nstrips + nlay + 5]
    wind_ref, conc_ref, cols_ref, far_ref, near_ref, edge_ref, frame = refs[nstrips + nlay + 5 :]
    nx, size, nz = dust_ref.shape
    nplane = frame.shape[0]
    ncomp = nplane // nx
    rows = size + 2 * EDGE
    place = lax.axis_index("vert")
    odd = lax.rem(lax.axis_index("horiz"), 2) == 1
    frame[:, :EDGE] = jnp.zeros((nplane, EDGE, nz), F32)
    frame[:, EDGE + size :] = jnp.zeros((nplane, EDGE, nz), F32)
    for t in range(nstrips):
        @pl.when(place == t)
        def _(t=t):
            beside = strips[t][nplane * size :].astype(F32)
            for j in range(nplane):
                frame[j, EDGE : EDGE + size] = strips[t][j * size : (j + 1) * size].astype(F32)
                for i, y in enumerate(halo_rows(EDGE, size)):
                    frame[j, y : y + 1] = beside[i * 16 + j : i * 16 + j + 1]

    face = first_ref.shape[0] - 32 - nx * EDGE
    over, under = sorted_ends(first_ref, second_ref, face, nx * EDGE + 32)
    zero = jnp.zeros((16, LANES), F32)
    layer = jnp.where(place == 0, over[nx * EDGE + 16 :], zero)
    layer = layer + jnp.where(place == 1, lays[0][min(1, nstrips - 1)].astype(F32), zero)
    layer = layer + jnp.where(place == 2, under[nx * EDGE + 16 :], zero)
    for got in lays[1:]:
        layer = layer + got[...].astype(F32)
    layer = jnp.concatenate([layer, jnp.zeros((LANES - 16, LANES), F32)], 0)
    turned = layer.T.astype(BF)[:rows]
    brow, blane = iota((LANES, nz), 0), iota((LANES, nz), 1)
    beside = jnp.where((brow == blane + 1) | (brow == blane - 1), 1.0, 0.0).astype(BF)
    edges = {}
    for comp in range(ncomp):
        f = [frame[comp * nx + x] for x in range(nx)]
        for x in range(nx):
            j = comp * nx + x
            raw = f[x].astype(BF)
            near = jnp.dot(raw, beside, preferred_element_type=F32)
            top = jnp.where((brow == j) & (blane == nz - 1), 1.0, 0.0).astype(BF)
            near = near + jnp.dot(turned, top, preferred_element_type=F32)
            near = near + pltpu.roll(f[x], 1, 0) + pltpu.roll(f[x], rows - 1, 0)
            if x:
                near = near + f[x - 1]
            if x < nx - 1:
                near = near + f[x + 1]
            wind = 0.28 * f[x] + 0.12 * near
            wind_ref[j] = wind
            if x == 0:
                edge_ref[comp] = raw
            if x == nx - 1:
                edge_ref[ncomp + comp] = raw
    for x in range(nx):
        before, after = (under[x * EDGE : (x + 1) * EDGE], over[x * EDGE : (x + 1) * EDGE])
        conc_ref[x] = jnp.concatenate([before, dust_ref[x], after], 0)
    lane = iota((nx, LANES), 1)
    own = terrain_ref[...].astype(F32)
    own = jnp.concatenate([own, jnp.zeros((nx, LANES - size), F32)], 1)
    land = slice(nx * EDGE, nx * EDGE + 16)
    before = pltpu.roll(under[land], (EDGE - size) % LANES, 1)[:nx]
    after = pltpu.roll(over[land], (EDGE + size) % LANES, 1)[:nx]
    ground = jnp.where(lane < EDGE, before, jnp.where(lane < EDGE + size, pltpu.roll(own, EDGE, 1), after))
    y = lane + (place * size - EDGE)
    flags = jnp.zeros((nx, LANES), jnp.int32)
    for b in range(eligible_ref.shape[1]):
        inside = (y >= b * 128) & (y < (b + 1) * 128)
        flags = jnp.where(inside, jnp.broadcast_to(eligible_ref[:, b : b + 1], (nx, LANES)), flags)
    lifted = jnp.where(flags == 1, ground, -1.0)
    cols_ref[...] = jnp.zeros_like(cols_ref)
    cols_ref[:nx] = ground
    cols_ref[EDGE : EDGE + nx] = lifted
    fill = jnp.zeros((16 - 2 * ncomp - 4, LANES), F32)
    strip, first, last = (slice(EDGE, EDGE + size), slice(EDGE - 1, EDGE), slice(EDGE + size, EDGE + size + 1))

    def send(ref, x, inner):
        for comp in range(ncomp):
            j = comp * nx + x
            ref[comp * size : (comp + 1) * size] = frame[j, strip].astype(BF)
            ref[(ncomp + comp) * size : (ncomp + comp + 1) * size] = wind_ref[j, strip].astype(BF)
        at = 2 * ncomp * size
        ref[at : at + size] = conc_ref[x, strip].astype(BF)
        ref[at + size : at + 2 * size] = conc_ref[inner, strip].astype(BF)
        at = at + 2 * size
        rows = [frame[comp * nx + x, first] for comp in range(ncomp)] + [conc_ref[x, first]]
        rows += [frame[comp * nx + x, last] for comp in range(ncomp)] + [conc_ref[x, last]]
        ref[at : at + 16] = jnp.concatenate(rows + [ground[x : x + 1], lifted[x : x + 1], fill], 0).astype(BF)

    @pl.when(odd)
    def _():
        send(near_ref, 0, 1)
        send(far_ref, nx - 1, nx - 2)

    @pl.when(jnp.logical_not(odd))
    def _():
        send(near_ref, nx - 1, nx - 2)
        send(far_ref, 0, 1)


def transport(ny, nhoriz, wind_ref, edge_ref, conc_ref, cols_ref, far_ref, near_ref, out_ref):
    nx, size, nz = out_ref.shape
    ncomp = edge_ref.shape[0] // 2
    rows = size + 2 * EDGE
    column, place = (lax.axis_index("horiz"), lax.axis_index("vert"))
    odd = lax.rem(column, 2) == 1
    here = 2 * (ncomp + 1) * size
    low = iota((EDGE, nz), 0)

    def below(start, n):
        return jnp.where(odd, near_ref[start : start + n].astype(F32), far_ref[start : start + n].astype(F32))

    def above(start, n):
        return jnp.where(odd, far_ref[start : start + n].astype(F32), near_ref[start : start + n].astype(F32))

    def part(side, i, halo=None):
        head, tail = (jnp.zeros((EDGE, nz), F32),) * 2
        if halo is not None:
            rest = ends[side]
            head = jnp.where(low == EDGE - 1, rest[halo : halo + 1], head)
            tail = jnp.where(low == 0, rest[ncomp + 1 + halo : ncomp + 2 + halo], tail)
        return jnp.concatenate([head, side(i * size, size), tail], 0)

    ends = {below: below(here, 16), above: above(here, 16)}
    conc = [part(below, 2 * ncomp + 1), part(below, 2 * ncomp, ncomp)]
    conc += [conc_ref[x] for x in range(nx)]
    conc += [part(above, 2 * ncomp, ncomp), part(above, 2 * ncomp + 1)]
    table = jnp.concatenate([ends[below], cols_ref[...], ends[above], jnp.zeros((LANES - 48, LANES), F32)], 0).T[:rows]
    mark = 2 * (ncomp + 1)
    ground = [mark] + [16 + x for x in range(nx)] + [32 + mark]
    lifted = [mark + 1] + [16 + EDGE + x for x in range(nx)] + [33 + mark]
    layer = iota((rows, nz), 1).astype(F32)
    y = iota((rows, nz), 0) + (place * size - EDGE)
    inside = (y >= 0) & (y < ny)
    first, last = layer == 0.0, layer == nz - 1.0
    zero = jnp.zeros((rows, nz), F32)
    state = [None] * (nx + 2)
    for p in range(nx + 2):
        comps = []
        for comp in range(ncomp):
            if p == 0:
                w = part(below, ncomp + comp) + 0.12 * edge_ref[comp].astype(F32)
            elif p == nx + 1:
                w = part(above, ncomp + comp) + 0.12 * edge_ref[ncomp + comp].astype(F32)
            else:
                w = wind_ref[comp * nx + p - 1]
                if p == 1:
                    w = w + 0.12 * part(below, comp, comp)
                if p == nx:
                    w = w + 0.12 * part(above, comp, comp)
            comps.append(w)
        gu, gv, gw = comps
        speed = jnp.sqrt(gu * gu + gv * gv)
        rise = jnp.broadcast_to(table[:, lifted[p] : lifted[p] + 1], (rows, nz))
        base = jnp.broadcast_to(table[:, ground[p] : ground[p] + 1], (rows, nz))
        lift = jnp.where(layer == rise, 0.5 * jnp.maximum(speed - 1.0, 0.0), 0.0)
        keep = (layer >= base) & inside
        if p == 0:
            keep = keep & (column > 0)
        if p == nx + 1:
            keep = keep & (column < nhoriz - 1)
        coef = [
            (0.15 * (0.1 - jnp.minimum(a, 0.0)), 0.15 * (0.1 + jnp.maximum(a, 0.0)))
            for a in (gu, gv, gw - 0.5)
        ]
        state[p] = (coef, lift, keep)

    def step(p, c, behind, ahead):
        coef, lift, keep = state[p]
        total = c + lift
        pairs = (
            (ahead, behind),
            (pltpu.roll(c, rows - 1, 0), pltpu.roll(c, 1, 0)),
            (
                jnp.where(last, zero, pltpu.roll(c, nz - 1, 1)),
                jnp.where(first, zero, pltpu.roll(c, 1, 1)),
            ),
        )
        for (forward, back), (post, prev) in zip(coef, pairs):
            total = total + forward * (post - c) - back * (c - prev)
        return jnp.where(keep, total, 0.0)

    once = [step(p, conc[p + 1], conc[p], conc[p + 2]) for p in range(nx + 2)]
    for x in range(nx):
        twice = step(x + 1, once[x + 1], once[x], once[x + 2])
        out_ref[x] = twice[EDGE : EDGE + size]


def pairs(size, start):
    return [p for i in range(start, size - 1, 2) for p in ((i, i + 1), (i + 1, i))]


def local(velocity, dust, eligible, terrain):
    ncomp, nx, ny, nz = velocity.shape
    size = dust.shape[1]
    nh, nv = (lax.axis_size("horiz"), lax.axis_size("vert"))
    rows = size + 2 * EDGE
    near_pairs, far_pairs = (pairs(nh, 0), pairs(nh, 1))
    nplane = ncomp * nx
    anywhere = pl.BlockSpec(memory_space=pl.ANY)

    strips = call(
        functools.partial(pack_low, size),
        [shaped(nplane * size + 64, LANES)] * nv,
        "pack_low",
        [
            pltpu.VMEM((ncomp, nx, ny, nz), F32),
            pltpu.VMEM((nv, 64, LANES), F32),
            pltpu.SemaphoreType.DMA((ncomp,)),
        ],
        in_specs=[anywhere],
        out_specs=[VMEM] * nv,
    )(pltpu.with_memory_space_constraint(velocity, pltpu.HBM))
    ends = ny // LANES * 16 + nx * EDGE + 32
    first, second, mine, *lays = call(
        functools.partial(pack_ends, size, nv),
        [shaped(ends, LANES)] * 2 + [shaped(3, 16, LANES)] + [shaped(16, LANES)] * (nv - 3),
        "pack_ends",
        [pltpu.VMEM((16, ny), F32)] * 2
        + [pltpu.VMEM((2, nx, EDGE, nz), F32), pltpu.VMEM((nx, size), jnp.int32), pltpu.SemaphoreType.DMA((3,))],
        in_specs=[VMEM, anywhere, anywhere, anywhere],
    )(
        velocity,
        pltpu.with_memory_space_constraint(dust, pltpu.HBM),
        pltpu.with_memory_space_constraint(terrain, pltpu.HBM),
        strips[-1],
    )
    first = lax.ppermute(first, "vert", pairs(nv, 0))
    second = lax.ppermute(second, "vert", pairs(nv, 1))
    lays = [mine] + [lax.ppermute(lay, "vert", [(1, t + 3)]) for t, lay in enumerate(lays)]

    sent = call(
        gate,
        [jax.ShapeDtypeStruct(rows.shape, rows.dtype) for rows in strips[1:]],
        "gate",
        in_specs=[anywhere] * nv,
        out_specs=[anywhere] * (nv - 1),
        input_output_aliases={t: t for t in range(nv - 1)},
    )(*strips[1:], first)
    got = [lax.ppermute(sent[t - 1], "vert", [(0, t)]) for t in range(nv - 1, 0, -1)]
    got = [strips[0]] + got[::-1]

    far, near = call(
        pack_sides, [shaped(ncomp, ny, nz)] * 2, "pack_sides", cost=1 << 26, in_specs=[VMEM, anywhere]
    )(velocity, sent[-1])
    far = lax.ppermute(far, "horiz", far_pairs)
    near = lax.ppermute(near, "horiz", near_pairs)

    velocity_next = call(
        advance,
        jax.ShapeDtypeStruct(velocity.shape, F32),
        "advance",
        [pltpu.VMEM((ncomp, nx, ny, nz), F32), pltpu.SemaphoreType.DMA((ncomp,))],
        in_specs=[VMEM] * 5,
        out_specs=anywhere,
    )(velocity, far, near, first, second)

    wire = (2 * ncomp + 2) * size + 16
    wind, conc, cols, mf, mn, edge = call(
        functools.partial(prepare, nv),
        [
            shaped(nplane, rows, LANES, dtype=F32),
            shaped(nx, rows, LANES, dtype=F32),
            shaped(16, LANES, dtype=F32),
            shaped(wire, LANES),
            shaped(wire, LANES),
            shaped(2 * ncomp, rows, LANES),
        ],
        "prepare",
        [pltpu.VMEM((nplane, rows, LANES), F32)],
    )(*got, *lays, dust, terrain, eligible, first, second)
    mf = lax.ppermute(mf, "horiz", far_pairs)
    mn = lax.ppermute(mn, "horiz", near_pairs)
    dust_next = call(
        functools.partial(transport, ny, nh),
        jax.ShapeDtypeStruct(dust.shape, F32),
        "transport",
    )(wind, edge, conc, cols, mf, mn)
    return (velocity_next, dust_next)


def solution(mesh):
    placed = (
        P(None, "horiz", None, "vert"),
        P("horiz", "vert", None),
        P("horiz", None),
        P("horiz", "vert"),
    )
    return jax.shard_map(
        local,
        mesh=mesh,
        in_specs=placed,
        out_specs=(P(None, "horiz", None, "vert"), P("horiz", "vert", None)),
        check_vma=False,
    )
```

```python
import functools

import jax
import jax.numpy as jnp
from jax import lax
from jax.experimental import pallas as pl
from jax.experimental.pallas import tpu as pltpu
from jax.sharding import PartitionSpec as P

DSTEPS = 2
LANES = 128
EDGE = 8
BF = jnp.bfloat16
F32 = jnp.float32

VMEM = pl.BlockSpec(memory_space=pltpu.VMEM)


def call(kernel, out_shape, name, scratch=(), cost=1 << 20, **kwargs):
    return pl.pallas_call(
        kernel,
        out_shape=out_shape,
        scratch_shapes=list(scratch),
        compiler_params=pltpu.CompilerParams(vmem_limit_bytes=40 << 20),
        cost_estimate=pl.CostEstimate(flops=cost, bytes_accessed=cost, transcendentals=0),
        name=name,
        **kwargs,
    )


def shaped(*dims, dtype=BF):
    return jax.ShapeDtypeStruct(dims, dtype)


def iota(shape, dim):
    return lax.broadcasted_iota(jnp.int32, shape, dim)


def pick(shape, pairs):
    row, col = iota(shape, 0), iota(shape, 1)
    hit = functools.reduce(jnp.logical_or, [(row == r) & (col == c) for r, c in pairs])
    return jnp.where(hit, 1.0, 0.0).astype(BF)


def turn_faces(v_ref, comp, ends, outs):
    _, nx, ny, _ = v_ref.shape
    for x in range(nx):
        j = comp * nx + x
        for half in range(ny // LANES):
            span = slice(half * LANES, (half + 1) * LANES)
            block = v_ref[comp, x, span, :].astype(BF)
            rows = lax.dot_general(ends, block, (((1,), (1,)), ((), ())), preferred_element_type=F32)
            for i, out in enumerate(outs):
                out[j : j + 1, span] = rows[i : i + 1]


def halo_rows(start, size):
    return (start - 2, start - 1, start + size, start + size + 1)


def pack_sides(v_ref, after_ref, far_ref, near_ref):
    del after_ref
    nx = v_ref.shape[1]
    odd = lax.rem(lax.axis_index("horiz"), 2) == 1

    @pl.when(odd)
    def _():
        near_ref[...] = v_ref[:, 0].astype(BF)
        far_ref[...] = v_ref[:, nx - 1].astype(BF)

    @pl.when(jnp.logical_not(odd))
    def _():
        near_ref[...] = v_ref[:, nx - 1].astype(BF)
        far_ref[...] = v_ref[:, 0].astype(BF)


def start_all(copies):
    for copy in copies:
        copy.start()
    return copies


def wait_all(copies):
    for copy in copies:
        copy.wait()


def write_ends(ref, at, face, dust, land, layer):
    nx, size = land.shape
    ny = face.shape[1]
    terrain = jnp.concatenate([land.astype(F32), jnp.zeros((nx, LANES - size), F32)], 1)
    terrain = jnp.concatenate([terrain, jnp.zeros((16 - nx, LANES), F32)], 0)
    for half in range(ny // LANES):
        ref[at + half * 16 : at + half * 16 + 16] = face[:, half * LANES : (half + 1) * LANES].astype(BF)
    at = at + ny // LANES * 16
    ref[at : at + nx * EDGE] = dust.reshape(nx * EDGE, LANES).astype(BF)
    at = at + nx * EDGE
    ref[at : at + 16] = terrain.astype(BF)
    ref[at + 16 : at + 32] = layer


def pack_low(size, v_ref, dust_ref, terrain_ref, *refs):
    outs, (buf, high, side, dusts, land, sems) = (refs[:-6], refs[-6:])
    ncomp, nx, ny, nz = v_ref.shape
    nplane = ncomp * nx

    @pl.when(lax.axis_index("vert") == 0)
    def _():
        planes = start_all(
            [pltpu.make_async_copy(v_ref.at[j // nx, j % nx], buf.at[j // nx, j % nx], sems.at[j]) for j in range(nplane)]
        )
        small = start_all(
            [
                pltpu.make_async_copy(dust_ref.at[:, size - EDGE :], dusts, sems.at[nplane]),
                pltpu.make_async_copy(terrain_ref, land, sems.at[nplane + 1]),
            ]
        )
        side[...] = jnp.zeros_like(side)
        high[...] = jnp.zeros_like(high)
        end = pick((16, nz), [(0, nz - 1)])
        for comp in range(ncomp):
            wait_all(planes[comp * nx : (comp + 1) * nx])
            turn_faces(buf, comp, end, [high])
            for x in range(nx):
                j = comp * nx + x
                for t, out in enumerate(outs):
                    out[j * size : (j + 1) * size] = buf[comp, x, t * size : (t + 1) * size, :].astype(BF)
                    for i, y in enumerate(halo_rows(t * size, size)):
                        if 0 <= y < ny:
                            side[t, i * 16 + j : i * 16 + j + 1] = buf[comp, x, y : y + 1, :]
        for t, out in enumerate(outs):
            out[nplane * size : nplane * size + 64] = side[t].astype(BF)
        wait_all(small)
        write_ends(outs[1], nplane * size + 64, high, dusts[...], land[...], jnp.zeros((16, LANES), BF))


def pack_ends(size, nstrips, v_ref, dust_ref, terrain_ref, after_ref, first_ref, second_ref, mine_ref, *refs):
    del after_ref
    lays, (low, high, dusts, land, sems) = (refs[:-5], refs[-5:])
    ncomp, nx, ny, nz = v_ref.shape
    odd = lax.rem(lax.axis_index("vert"), 2) == 1
    small = start_all(
        [
            pltpu.make_async_copy(dust_ref.at[:, :EDGE], dusts.at[0], sems.at[0]),
            pltpu.make_async_copy(dust_ref.at[:, size - EDGE :], dusts.at[1], sems.at[1]),
            pltpu.make_async_copy(terrain_ref, land, sems.at[2]),
        ]
    )
    low[...] = jnp.zeros_like(low)
    high[...] = jnp.zeros_like(high)
    ends = pick((16, nz), [(0, 0), (1, nz - 1)])
    for comp in range(ncomp):
        turn_faces(v_ref, comp, ends, [low, high])
    lane = iota((16, LANES), 1)
    whole = low[...]
    for t in range(nstrips):
        shift = (EDGE - t * size) % ny
        moved = pltpu.roll(whole, shift, 1) if shift else whole
        row = lane + (t * size - EDGE)
        part = jnp.where((row >= 0) & (row < ny), moved[:, :LANES], 0.0).astype(BF)
        if t < 3:
            mine_ref[t] = part
        else:
            lays[t - 3][...] = part
    wait_all(small)

    @pl.when(odd)
    def _():
        write_ends(first_ref, 0, low, dusts[0], land[...], mine_ref[0])
        write_ends(second_ref, 0, high, dusts[1], land[...], mine_ref[2])

    @pl.when(jnp.logical_not(odd))
    def _():
        write_ends(first_ref, 0, high, dusts[1], land[...], mine_ref[2])
        write_ends(second_ref, 0, low, dusts[0], land[...], mine_ref[0])


def sorted_ends(first_ref, second_ref, strip_ref, start, n):
    place = lax.axis_index("vert")
    odd = lax.rem(place, 2) == 1
    base = strip_ref.shape[0] - first_ref.shape[0] + start
    first, second = (first_ref[start : start + n].astype(F32), second_ref[start : start + n].astype(F32))
    below = jnp.where(place == 1, strip_ref[base : base + n].astype(F32), jnp.where(odd, first, second))
    return (jnp.where(odd, second, first), below)


def advance(v_ref, far_ref, near_ref, first_ref, second_ref, strip_ref, out_ref, buf, sems):
    ncomp, nx, ny, nz = v_ref.shape
    odd = lax.rem(lax.axis_index("horiz"), 2) == 1
    row, lane = iota((LANES, nz), 0), iota((LANES, nz), 1)
    nb = ny // LANES
    turned = []
    for half in range(nb):
        over, under = sorted_ends(first_ref, second_ref, strip_ref, half * 16, 16)
        faces = jnp.concatenate([over, under, jnp.zeros((LANES - 32, LANES), F32)], 0)
        turned.append(faces.T.astype(BF))
    copies = []
    for comp in range(ncomp):
        for half in range(nb):
            a = half * LANES
            span = slice(a, a + LANES)
            near, far = (near_ref[comp, span, :].astype(F32), far_ref[comp, span, :].astype(F32))
            below = jnp.where(odd, near, far)
            above = jnp.where(odd, far, near)
            for x in range(nx):
                j = comp * nx + x
                place = ((row == j) & (lane == nz - 1)) | ((row == 16 + j) & (lane == 0))
                place = jnp.where(place, 1.0, 0.0).astype(BF)
                sums = lax.dot_general(turned[half], place, (((1,), (0,)), ((), ())), preferred_element_type=F32)
                f = v_ref[comp, x, span, :]
                sums = sums + jnp.where(lane == 0, 0.0, pltpu.roll(f, 1, 1))
                sums = sums + jnp.where(lane == nz - 1, 0.0, pltpu.roll(f, nz - 1, 1))
                prev = v_ref[comp, x, a - 1 : a, :] if a else jnp.zeros((1, nz), F32)
                post = v_ref[comp, x, a + LANES : a + LANES + 1, :] if half < nb - 1 else jnp.zeros((1, nz), F32)
                sums = sums + jnp.where(row == 0, prev, pltpu.roll(f, 1, 0))
                sums = sums + jnp.where(row == LANES - 1, post, pltpu.roll(f, LANES - 1, 0))
                sums = sums + (v_ref[comp, x - 1, span, :] if x else below)
                sums = sums + (v_ref[comp, x + 1, span, :] if x < nx - 1 else above)
                buf[comp, x, span, :] = f + 0.12 * (sums - 6.0 * f)
        copies.append(pltpu.make_async_copy(buf.at[comp], out_ref.at[comp], sems.at[comp]))
        copies[-1].start()
    for copy in copies:
        copy.wait()


def prepare(nstrips, *refs):
    strips = refs[:1] + refs[nstrips - 1 : 0 : -1]
    nlay = 1 + max(nstrips - 3, 0)
    lays = refs[nstrips : nstrips + nlay]
    dust_ref, terrain_ref, eligible_ref, first_ref, second_ref = refs[nstrips + nlay : nstrips + nlay + 5]
    wind_ref, conc_ref, cols_ref, far_ref, near_ref, edge_ref, frame = refs[nstrips + nlay + 5 :]
    nx, size, nz = dust_ref.shape
    nplane = frame.shape[0]
    ncomp = nplane // nx
    rows = size + 2 * EDGE
    place = lax.axis_index("vert")
    odd = lax.rem(lax.axis_index("horiz"), 2) == 1
    frame[:, :EDGE] = jnp.zeros((nplane, EDGE, nz), F32)
    frame[:, EDGE + size :] = jnp.zeros((nplane, EDGE, nz), F32)
    for t in range(nstrips):
        @pl.when(place == t)
        def _(t=t):
            beside = strips[t][nplane * size : nplane * size + 64].astype(F32)
            for j in range(nplane):
                frame[j, EDGE : EDGE + size] = strips[t][j * size : (j + 1) * size].astype(F32)
                for i, y in enumerate(halo_rows(EDGE, size)):
                    frame[j, y : y + 1] = beside[i * 16 + j : i * 16 + j + 1]

    face = first_ref.shape[0] - 32 - nx * EDGE
    over, under = sorted_ends(first_ref, second_ref, strips[1], face, nx * EDGE + 32)
    zero = jnp.zeros((16, LANES), F32)
    layer = jnp.where(place == 0, over[nx * EDGE + 16 :], zero)
    layer = layer + jnp.where(place == 1, lays[0][min(1, nstrips - 1)].astype(F32), zero)
    layer = layer + jnp.where(place == 2, under[nx * EDGE + 16 :], zero)
    for got in lays[1:]:
        layer = layer + got[...].astype(F32)
    layer = jnp.concatenate([layer, jnp.zeros((LANES - 16, LANES), F32)], 0)
    turned = layer.T.astype(BF)[:rows]
    brow, blane = iota((LANES, nz), 0), iota((LANES, nz), 1)
    beside = jnp.where((brow == blane + 1) | (brow == blane - 1), 1.0, 0.0).astype(BF)
    edges = {}
    for comp in range(ncomp):
        f = [frame[comp * nx + x] for x in range(nx)]
        for x in range(nx):
            j = comp * nx + x
            raw = f[x].astype(BF)
            near = jnp.dot(raw, beside, preferred_element_type=F32)
            top = jnp.where((brow == j) & (blane == nz - 1), 1.0, 0.0).astype(BF)
            near = near + jnp.dot(turned, top, preferred_element_type=F32)
            near = near + pltpu.roll(f[x], 1, 0) + pltpu.roll(f[x], rows - 1, 0)
            if x:
                near = near + f[x - 1]
            if x < nx - 1:
                near = near + f[x + 1]
            wind = 0.28 * f[x] + 0.12 * near
            wind_ref[j] = wind
            if x == 0:
                edge_ref[comp] = raw
            if x == nx - 1:
                edge_ref[ncomp + comp] = raw
    for x in range(nx):
        before, after = (under[x * EDGE : (x + 1) * EDGE], over[x * EDGE : (x + 1) * EDGE])
        conc_ref[x] = jnp.concatenate([before, dust_ref[x], after], 0)
    lane = iota((nx, LANES), 1)
    own = terrain_ref[...].astype(F32)
    own = jnp.concatenate([own, jnp.zeros((nx, LANES - size), F32)], 1)
    land = slice(nx * EDGE, nx * EDGE + 16)
    before = pltpu.roll(under[land], (EDGE - size) % LANES, 1)[:nx]
    after = pltpu.roll(over[land], (EDGE + size) % LANES, 1)[:nx]
    ground = jnp.where(lane < EDGE, before, jnp.where(lane < EDGE + size, pltpu.roll(own, EDGE, 1), after))
    y = lane + (place * size - EDGE)
    flags = jnp.zeros((nx, LANES), jnp.int32)
    for b in range(eligible_ref.shape[1]):
        inside = (y >= b * 128) & (y < (b + 1) * 128)
        flags = jnp.where(inside, jnp.broadcast_to(eligible_ref[:, b : b + 1], (nx, LANES)), flags)
    lifted = jnp.where(flags == 1, ground, -1.0)
    cols_ref[...] = jnp.zeros_like(cols_ref)
    cols_ref[:nx] = ground
    cols_ref[EDGE : EDGE + nx] = lifted
    fill = jnp.zeros((16 - 2 * ncomp - 4, LANES), F32)
    strip, first, last = (slice(EDGE, EDGE + size), slice(EDGE - 1, EDGE), slice(EDGE + size, EDGE + size + 1))

    def send(ref, x, inner):
        for comp in range(ncomp):
            j = comp * nx + x
            ref[comp * size : (comp + 1) * size] = frame[j, strip].astype(BF)
            ref[(ncomp + comp) * size : (ncomp + comp + 1) * size] = wind_ref[j, strip].astype(BF)
        at = 2 * ncomp * size
        ref[at : at + size] = conc_ref[x, strip].astype(BF)
        ref[at + size : at + 2 * size] = conc_ref[inner, strip].astype(BF)
        at = at + 2 * size
        rows = [frame[comp * nx + x, first] for comp in range(ncomp)] + [conc_ref[x, first]]
        rows += [frame[comp * nx + x, last] for comp in range(ncomp)] + [conc_ref[x, last]]
        ref[at : at + 16] = jnp.concatenate(rows + [ground[x : x + 1], lifted[x : x + 1], fill], 0).astype(BF)

    @pl.when(odd)
    def _():
        send(near_ref, 0, 1)
        send(far_ref, nx - 1, nx - 2)

    @pl.when(jnp.logical_not(odd))
    def _():
        send(near_ref, nx - 1, nx - 2)
        send(far_ref, 0, 1)


def transport(ny, nhoriz, wind_ref, edge_ref, conc_ref, cols_ref, far_ref, near_ref, out_ref):
    nx, size, nz = out_ref.shape
    ncomp = edge_ref.shape[0] // 2
    rows = size + 2 * EDGE
    column, place = (lax.axis_index("horiz"), lax.axis_index("vert"))
    odd = lax.rem(column, 2) == 1
    here = 2 * (ncomp + 1) * size
    low = iota((EDGE, nz), 0)

    def below(start, n):
        return jnp.where(odd, near_ref[start : start + n].astype(F32), far_ref[start : start + n].astype(F32))

    def above(start, n):
        return jnp.where(odd, far_ref[start : start + n].astype(F32), near_ref[start : start + n].astype(F32))

    def part(side, i, halo=None):
        head, tail = (jnp.zeros((EDGE, nz), F32),) * 2
        if halo is not None:
            rest = ends[side]
            head = jnp.where(low == EDGE - 1, rest[halo : halo + 1], head)
            tail = jnp.where(low == 0, rest[ncomp + 1 + halo : ncomp + 2 + halo], tail)
        return jnp.concatenate([head, side(i * size, size), tail], 0)

    ends = {below: below(here, 16), above: above(here, 16)}
    conc = [part(below, 2 * ncomp + 1), part(below, 2 * ncomp, ncomp)]
    conc += [conc_ref[x] for x in range(nx)]
    conc += [part(above, 2 * ncomp, ncomp), part(above, 2 * ncomp + 1)]
    table = jnp.concatenate([ends[below], cols_ref[...], ends[above], jnp.zeros((LANES - 48, LANES), F32)], 0).T[:rows]
    mark = 2 * (ncomp + 1)
    ground = [mark] + [16 + x for x in range(nx)] + [32 + mark]
    lifted = [mark + 1] + [16 + EDGE + x for x in range(nx)] + [33 + mark]
    layer = iota((rows, nz), 1).astype(F32)
    y = iota((rows, nz), 0) + (place * size - EDGE)
    inside = (y >= 0) & (y < ny)
    first, last = layer == 0.0, layer == nz - 1.0
    zero = jnp.zeros((rows, nz), F32)
    state = [None] * (nx + 2)
    for p in range(nx + 2):
        comps = []
        for comp in range(ncomp):
            if p == 0:
                w = part(below, ncomp + comp) + 0.12 * edge_ref[comp].astype(F32)
            elif p == nx + 1:
                w = part(above, ncomp + comp) + 0.12 * edge_ref[ncomp + comp].astype(F32)
            else:
                w = wind_ref[comp * nx + p - 1]
                if p == 1:
                    w = w + 0.12 * part(below, comp, comp)
                if p == nx:
                    w = w + 0.12 * part(above, comp, comp)
            comps.append(w)
        gu, gv, gw = comps
        speed = jnp.sqrt(gu * gu + gv * gv)
        rise = jnp.broadcast_to(table[:, lifted[p] : lifted[p] + 1], (rows, nz))
        base = jnp.broadcast_to(table[:, ground[p] : ground[p] + 1], (rows, nz))
        lift = jnp.where(layer == rise, 0.5 * jnp.maximum(speed - 1.0, 0.0), 0.0)
        keep = (layer >= base) & inside
        if p == 0:
            keep = keep & (column > 0)
        if p == nx + 1:
            keep = keep & (column < nhoriz - 1)
        coef = [
            (0.15 * (0.1 - jnp.minimum(a, 0.0)), 0.15 * (0.1 + jnp.maximum(a, 0.0)))
            for a in (gu, gv, gw - 0.5)
        ]
        state[p] = (coef, lift, keep)

    def step(p, c, behind, ahead):
        coef, lift, keep = state[p]
        total = c + lift
        pairs = (
            (ahead, behind),
            (pltpu.roll(c, rows - 1, 0), pltpu.roll(c, 1, 0)),
            (
                jnp.where(last, zero, pltpu.roll(c, nz - 1, 1)),
                jnp.where(first, zero, pltpu.roll(c, 1, 1)),
            ),
        )
        for (forward, back), (post, prev) in zip(coef, pairs):
            total = total + forward * (post - c) - back * (c - prev)
        return jnp.where(keep, total, 0.0)

    once = [step(p, conc[p + 1], conc[p], conc[p + 2]) for p in range(nx + 2)]
    for x in range(nx):
        twice = step(x + 1, once[x + 1], once[x], once[x + 2])
        out_ref[x] = twice[EDGE : EDGE + size]


def pairs(size, start):
    return [p for i in range(start, size - 1, 2) for p in ((i, i + 1), (i + 1, i))]


def local(velocity, dust, eligible, terrain):
    ncomp, nx, ny, nz = velocity.shape
    size = dust.shape[1]
    nh, nv = (lax.axis_size("horiz"), lax.axis_size("vert"))
    rows = size + 2 * EDGE
    near_pairs, far_pairs = (pairs(nh, 0), pairs(nh, 1))
    nplane = ncomp * nx
    anywhere = pl.BlockSpec(memory_space=pl.ANY)

    ends = ny // LANES * 16 + nx * EDGE + 32
    strip = nplane * size + 64
    held = [pltpu.with_memory_space_constraint(array, pltpu.HBM) for array in (velocity, dust, terrain)]
    strips = call(
        functools.partial(pack_low, size),
        [shaped(strip + (ends if t == 1 else 0), LANES) for t in range(nv)],
        "pack_low",
        [
            pltpu.VMEM((ncomp, nx, ny, nz), F32),
            pltpu.VMEM((16, ny), F32),
            pltpu.VMEM((nv, 64, LANES), F32),
            pltpu.VMEM((nx, EDGE, nz), F32),
            pltpu.VMEM((nx, size), jnp.int32),
            pltpu.SemaphoreType.DMA((nplane + 2,)),
        ],
        in_specs=[anywhere] * 3,
        out_specs=[VMEM] * nv,
    )(*held)
    got = [lax.ppermute(strips[t], "vert", [(0, t)]) for t in range(nv - 1, 0, -1)]
    got = [strips[0]] + got

    first, second, mine, *lays = call(
        functools.partial(pack_ends, size, nv),
        [shaped(ends, LANES)] * 2 + [shaped(3, 16, LANES)] + [shaped(16, LANES)] * (nv - 3),
        "pack_ends",
        [pltpu.VMEM((16, ny), F32)] * 2
        + [pltpu.VMEM((2, nx, EDGE, nz), F32), pltpu.VMEM((nx, size), jnp.int32), pltpu.SemaphoreType.DMA((3,))],
        in_specs=[VMEM] + [anywhere] * 3,
    )(velocity, *held[1:], strips[-1])
    first = lax.ppermute(first, "vert", pairs(nv, 0)[1:])
    second = lax.ppermute(second, "vert", pairs(nv, 1))
    lays = [mine] + [lax.ppermute(lay, "vert", [(1, t + 3)]) for t, lay in enumerate(lays)]

    far, near = call(
        pack_sides, [shaped(ncomp, ny, nz)] * 2, "pack_sides", cost=1 << 26, in_specs=[VMEM, anywhere]
    )(velocity, lays[-1])
    far = lax.ppermute(far, "horiz", far_pairs)
    near = lax.ppermute(near, "horiz", near_pairs)

    velocity_next = call(
        advance,
        jax.ShapeDtypeStruct(velocity.shape, F32),
        "advance",
        [pltpu.VMEM((ncomp, nx, ny, nz), F32), pltpu.SemaphoreType.DMA((ncomp,))],
        in_specs=[VMEM] * 6,
        out_specs=anywhere,
    )(velocity, far, near, first, second, got[-1])

    wire = (2 * ncomp + 2) * size + 16
    wind, conc, cols, mf, mn, edge = call(
        functools.partial(prepare, nv),
        [
            shaped(nplane, rows, LANES, dtype=F32),
            shaped(nx, rows, LANES, dtype=F32),
            shaped(16, LANES, dtype=F32),
            shaped(wire, LANES),
            shaped(wire, LANES),
            shaped(2 * ncomp, rows, LANES),
        ],
        "prepare",
        [pltpu.VMEM((nplane, rows, LANES), F32)],
    )(*got, *lays, dust, terrain, eligible, first, second)
    mf = lax.ppermute(mf, "horiz", far_pairs)
    mn = lax.ppermute(mn, "horiz", near_pairs)
    dust_next = call(
        functools.partial(transport, ny, nh),
        jax.ShapeDtypeStruct(dust.shape, F32),
        "transport",
    )(wind, edge, conc, cols, mf, mn)
    return (velocity_next, dust_next)


def solution(mesh):
    placed = (
        P(None, "horiz", None, "vert"),
        P("horiz", "vert", None),
        P("horiz", None),
        P("horiz", "vert"),
    )
    return jax.shard_map(
        local,
        mesh=mesh,
        in_specs=placed,
        out_specs=(P(None, "horiz", None, "vert"), P("horiz", "vert", None)),
        check_vma=False,
    )
```

```python
import functools

import jax
import jax.numpy as jnp
from jax import lax
from jax.experimental import pallas as pl
from jax.experimental.pallas import tpu as pltpu
from jax.sharding import PartitionSpec as P

DSTEPS = 2
LANES = 128
EDGE = 8
BF = jnp.bfloat16
F32 = jnp.float32

VMEM = pl.BlockSpec(memory_space=pltpu.VMEM)


def call(kernel, out_shape, name, scratch=(), cost=1 << 20, **kwargs):
    return pl.pallas_call(
        kernel,
        out_shape=out_shape,
        scratch_shapes=list(scratch),
        compiler_params=pltpu.CompilerParams(vmem_limit_bytes=40 << 20),
        cost_estimate=pl.CostEstimate(flops=cost, bytes_accessed=cost, transcendentals=0),
        name=name,
        **kwargs,
    )


def shaped(*dims, dtype=BF):
    return jax.ShapeDtypeStruct(dims, dtype)


def iota(shape, dim):
    return lax.broadcasted_iota(jnp.int32, shape, dim)


def pick(shape, pairs):
    row, col = iota(shape, 0), iota(shape, 1)
    hit = functools.reduce(jnp.logical_or, [(row == r) & (col == c) for r, c in pairs])
    return jnp.where(hit, 1.0, 0.0).astype(BF)


def turn_faces(v_ref, comp, ends, outs):
    _, nx, ny, _ = v_ref.shape
    for x in range(nx):
        j = comp * nx + x
        for half in range(ny // LANES):
            span = slice(half * LANES, (half + 1) * LANES)
            block = v_ref[comp, x, span, :].astype(BF)
            rows = lax.dot_general(ends, block, (((1,), (1,)), ((), ())), preferred_element_type=F32)
            for i, out in enumerate(outs):
                out[j : j + 1, span] = rows[i : i + 1]


def halo_rows(start, size):
    return (start - 2, start - 1, start + size, start + size + 1)


def columns(place, terrain_ref, eligible_ref):
    nx, size = terrain_ref.shape
    own = jnp.concatenate([terrain_ref[...].astype(F32), jnp.zeros((nx, LANES - size), F32)], 1)
    ground = pltpu.roll(own, EDGE, 1)
    return ground, lifted_layer(place, ground, eligible_ref, size)


def lifted_layer(place, ground, eligible_ref, size):
    y = iota(ground.shape, 1) + (place * size - EDGE)
    flags = jnp.zeros(ground.shape, jnp.int32)
    for b in range(eligible_ref.shape[1]):
        inside = (y >= b * 128) & (y < (b + 1) * 128)
        flags = jnp.where(inside, jnp.broadcast_to(eligible_ref[:, b : b + 1], ground.shape), flags)
    return jnp.where(flags == 1, ground, -1.0)


def pack_sides(v_ref, dust_ref, terrain_ref, eligible_ref, after_ref, far_ref, near_ref):
    del after_ref
    ncomp, nx, ny, _ = v_ref.shape
    size = dust_ref.shape[1]
    odd = lax.rem(lax.axis_index("horiz"), 2) == 1
    ground, lifted = columns(lax.axis_index("vert"), terrain_ref, eligible_ref)
    fill = jnp.zeros((14, LANES), F32)

    def send(ref, x, inner):
        for comp in range(ncomp):
            ref[comp * ny : (comp + 1) * ny] = v_ref[comp, x].astype(BF)
        at = ncomp * ny
        ref[at : at + size] = dust_ref[x].astype(BF)
        ref[at + size : at + 2 * size] = dust_ref[inner].astype(BF)
        at = at + 2 * size
        ref[at : at + 16] = jnp.concatenate([ground[x : x + 1], lifted[x : x + 1], fill], 0).astype(BF)

    send_both(odd, send, near_ref, far_ref, nx)


def send_both(odd, send, near_ref, far_ref, nx):
    @pl.when(odd)
    def _():
        send(near_ref, 0, 1)
        send(far_ref, nx - 1, nx - 2)

    @pl.when(jnp.logical_not(odd))
    def _():
        send(near_ref, nx - 1, nx - 2)
        send(far_ref, 0, 1)


def start_all(copies):
    for copy in copies:
        copy.start()
    return copies


def wait_all(copies):
    for copy in copies:
        copy.wait()


def write_ends(ref, at, face, dust, land, layer):
    nx, size = land.shape
    ny = face.shape[1]
    terrain = jnp.concatenate([land.astype(F32), jnp.zeros((nx, LANES - size), F32)], 1)
    terrain = jnp.concatenate([terrain, jnp.zeros((16 - nx, LANES), F32)], 0)
    for half in range(ny // LANES):
        ref[at + half * 16 : at + half * 16 + 16] = face[:, half * LANES : (half + 1) * LANES].astype(BF)
    at = at + ny // LANES * 16
    ref[at : at + nx * EDGE] = dust.reshape(nx * EDGE, LANES).astype(BF)
    at = at + nx * EDGE
    ref[at : at + 16] = terrain.astype(BF)
    ref[at + 16 : at + 32] = layer


def pack_low(size, v_ref, dust_ref, terrain_ref, *refs):
    outs, (buf, high, side, dusts, land, sems) = (refs[:-6], refs[-6:])
    ncomp, nx, ny, nz = v_ref.shape
    nplane = ncomp * nx

    @pl.when(lax.axis_index("vert") == 0)
    def _():
        planes = start_all(
            [pltpu.make_async_copy(v_ref.at[j // nx, j % nx], buf.at[j // nx, j % nx], sems.at[j]) for j in range(nplane)]
        )
        small = start_all(
            [
                pltpu.make_async_copy(dust_ref.at[:, size - EDGE :], dusts, sems.at[nplane]),
                pltpu.make_async_copy(terrain_ref, land, sems.at[nplane + 1]),
            ]
        )
        side[...] = jnp.zeros_like(side)
        high[...] = jnp.zeros_like(high)
        end = pick((16, nz), [(0, nz - 1)])
        for comp in range(ncomp):
            wait_all(planes[comp * nx : (comp + 1) * nx])
            turn_faces(buf, comp, end, [high])
            for x in range(nx):
                j = comp * nx + x
                for t, out in enumerate(outs):
                    out[j * size : (j + 1) * size] = buf[comp, x, t * size : (t + 1) * size, :].astype(BF)
                    for i, y in enumerate(halo_rows(t * size, size)):
                        if 0 <= y < ny:
                            side[t, i * nplane + j : i * nplane + j + 1] = buf[comp, x, y : y + 1, :]
        for t, out in enumerate(outs):
            out[nplane * size : nplane * (size + 4)] = side[t].astype(BF)
        wait_all(small)
        write_ends(outs[1], nplane * (size + 4), high, dusts[...], land[...], jnp.zeros((16, LANES), BF))


def pack_ends(size, nstrips, v_ref, dust_ref, terrain_ref, after_ref, first_ref, second_ref, mine_ref, *refs):
    del after_ref
    lays, (low, high, dusts, land, sems) = (refs[:-5], refs[-5:])
    ncomp, nx, ny, nz = v_ref.shape
    odd = lax.rem(lax.axis_index("vert"), 2) == 1
    small = start_all(
        [
            pltpu.make_async_copy(dust_ref.at[:, :EDGE], dusts.at[0], sems.at[0]),
            pltpu.make_async_copy(dust_ref.at[:, size - EDGE :], dusts.at[1], sems.at[1]),
            pltpu.make_async_copy(terrain_ref, land, sems.at[2]),
        ]
    )
    low[...] = jnp.zeros_like(low)
    high[...] = jnp.zeros_like(high)
    ends = pick((16, nz), [(0, 0), (1, nz - 1)])
    for comp in range(ncomp):
        turn_faces(v_ref, comp, ends, [low, high])
    lane = iota((16, LANES), 1)
    whole = low[...]
    for t in range(nstrips):
        shift = (EDGE - t * size) % ny
        moved = pltpu.roll(whole, shift, 1) if shift else whole
        row = lane + (t * size - EDGE)
        part = jnp.where((row >= 0) & (row < ny), moved[:, :LANES], 0.0).astype(BF)
        if t < 3:
            mine_ref[t] = part
        else:
            lays[t - 3][...] = part
    wait_all(small)

    @pl.when(odd)
    def _():
        write_ends(first_ref, 0, low, dusts[0], land[...], mine_ref[0])
        write_ends(second_ref, 0, high, dusts[1], land[...], mine_ref[2])

    @pl.when(jnp.logical_not(odd))
    def _():
        write_ends(first_ref, 0, high, dusts[1], land[...], mine_ref[2])
        write_ends(second_ref, 0, low, dusts[0], land[...], mine_ref[0])


def sorted_ends(first_ref, second_ref, strip_ref, start, n):
    place = lax.axis_index("vert")
    odd = lax.rem(place, 2) == 1
    base = strip_ref.shape[0] - first_ref.shape[0] + start
    first, second = (first_ref[start : start + n].astype(F32), second_ref[start : start + n].astype(F32))
    below = jnp.where(place == 1, strip_ref[base : base + n].astype(F32), jnp.where(odd, first, second))
    return (jnp.where(odd, second, first), below)


def advance(v_ref, far_ref, near_ref, first_ref, second_ref, strip_ref, out_ref, buf, sems):
    ncomp, nx, ny, nz = v_ref.shape
    odd = lax.rem(lax.axis_index("horiz"), 2) == 1
    row, lane = iota((LANES, nz), 0), iota((LANES, nz), 1)
    nb = ny // LANES
    turned = []
    for half in range(nb):
        over, under = sorted_ends(first_ref, second_ref, strip_ref, half * 16, 16)
        faces = jnp.concatenate([over, under, jnp.zeros((LANES - 32, LANES), F32)], 0)
        turned.append(faces.T.astype(BF))
    copies = []
    for comp in range(ncomp):
        for half in range(nb):
            a = half * LANES
            span = slice(a, a + LANES)
            rows = slice(comp * ny + a, comp * ny + a + LANES)
            near, far = (near_ref[rows].astype(F32), far_ref[rows].astype(F32))
            below = jnp.where(odd, near, far)
            above = jnp.where(odd, far, near)
            for x in range(nx):
                j = comp * nx + x
                place = ((row == j) & (lane == nz - 1)) | ((row == 16 + j) & (lane == 0))
                place = jnp.where(place, 1.0, 0.0).astype(BF)
                sums = lax.dot_general(turned[half], place, (((1,), (0,)), ((), ())), preferred_element_type=F32)
                f = v_ref[comp, x, span, :]
                sums = sums + jnp.where(lane == 0, 0.0, pltpu.roll(f, 1, 1))
                sums = sums + jnp.where(lane == nz - 1, 0.0, pltpu.roll(f, nz - 1, 1))
                prev = v_ref[comp, x, a - 1 : a, :] if a else jnp.zeros((1, nz), F32)
                post = v_ref[comp, x, a + LANES : a + LANES + 1, :] if half < nb - 1 else jnp.zeros((1, nz), F32)
                sums = sums + jnp.where(row == 0, prev, pltpu.roll(f, 1, 0))
                sums = sums + jnp.where(row == LANES - 1, post, pltpu.roll(f, LANES - 1, 0))
                sums = sums + (v_ref[comp, x - 1, span, :] if x else below)
                sums = sums + (v_ref[comp, x + 1, span, :] if x < nx - 1 else above)
                buf[comp, x, span, :] = f + 0.12 * (sums - 6.0 * f)
        copies.append(pltpu.make_async_copy(buf.at[comp], out_ref.at[comp], sems.at[comp]))
        copies[-1].start()
    for copy in copies:
        copy.wait()


def prepare(nstrips, *refs):
    strips = refs[:nstrips]
    nlay = 1 + max(nstrips - 3, 0)
    lays = refs[nstrips : nstrips + nlay]
    dust_ref, terrain_ref, eligible_ref, first_ref, second_ref = refs[nstrips + nlay : nstrips + nlay + 5]
    wind_ref, conc_ref, cols_ref, far_ref, near_ref, edge_ref, frame = refs[nstrips + nlay + 5 :]
    nx, size, nz = dust_ref.shape
    nplane = frame.shape[0]
    ncomp = nplane // nx
    rows = size + 2 * EDGE
    place = lax.axis_index("vert")
    odd = lax.rem(lax.axis_index("horiz"), 2) == 1
    frame[:, :EDGE] = jnp.zeros((nplane, EDGE, nz), F32)
    frame[:, EDGE + size :] = jnp.zeros((nplane, EDGE, nz), F32)
    for t in range(nstrips):
        @pl.when(place == t)
        def _(t=t):
            beside = strips[t][nplane * size : nplane * (size + 4)].astype(F32)
            for j in range(nplane):
                frame[j, EDGE : EDGE + size] = strips[t][j * size : (j + 1) * size].astype(F32)
                for i, y in enumerate(halo_rows(EDGE, size)):
                    frame[j, y : y + 1] = beside[i * nplane + j : i * nplane + j + 1]

    face = first_ref.shape[0] - 32 - nx * EDGE
    over, under = sorted_ends(first_ref, second_ref, strips[1], face, nx * EDGE + 32)
    zero = jnp.zeros((16, LANES), F32)
    layer = jnp.where(place == 0, over[nx * EDGE + 16 :], zero)
    layer = layer + jnp.where(place == 1, lays[0][min(1, nstrips - 1)].astype(F32), zero)
    layer = layer + jnp.where(place == 2, under[nx * EDGE + 16 :], zero)
    for got in lays[1:]:
        layer = layer + got[...].astype(F32)
    layer = jnp.concatenate([layer, jnp.zeros((LANES - 16, LANES), F32)], 0)
    turned = layer.T.astype(BF)[:rows]
    brow, blane = iota((LANES, nz), 0), iota((LANES, nz), 1)
    beside = jnp.where((brow == blane + 1) | (brow == blane - 1), 1.0, 0.0).astype(BF)
    edges = {}
    for comp in range(ncomp):
        f = [frame[comp * nx + x] for x in range(nx)]
        for x in range(nx):
            j = comp * nx + x
            raw = f[x].astype(BF)
            near = jnp.dot(raw, beside, preferred_element_type=F32)
            top = jnp.where((brow == j) & (blane == nz - 1), 1.0, 0.0).astype(BF)
            near = near + jnp.dot(turned, top, preferred_element_type=F32)
            near = near + pltpu.roll(f[x], 1, 0) + pltpu.roll(f[x], rows - 1, 0)
            if x:
                near = near + f[x - 1]
            if x < nx - 1:
                near = near + f[x + 1]
            wind = 0.28 * f[x] + 0.12 * near
            wind_ref[j] = wind
            if x == 0:
                edge_ref[comp] = raw
            if x == nx - 1:
                edge_ref[ncomp + comp] = raw
    for x in range(nx):
        before, after = (under[x * EDGE : (x + 1) * EDGE], over[x * EDGE : (x + 1) * EDGE])
        conc_ref[x] = jnp.concatenate([before, dust_ref[x], after], 0)
    lane = iota((nx, LANES), 1)
    own = terrain_ref[...].astype(F32)
    own = jnp.concatenate([own, jnp.zeros((nx, LANES - size), F32)], 1)
    land = slice(nx * EDGE, nx * EDGE + 16)
    before = pltpu.roll(under[land], (EDGE - size) % LANES, 1)[:nx]
    after = pltpu.roll(over[land], (EDGE + size) % LANES, 1)[:nx]
    ground = jnp.where(lane < EDGE, before, jnp.where(lane < EDGE + size, pltpu.roll(own, EDGE, 1), after))
    lifted = lifted_layer(place, ground, eligible_ref, size)
    cols_ref[...] = jnp.zeros_like(cols_ref)
    cols_ref[:nx] = ground
    cols_ref[EDGE : EDGE + nx] = lifted
    fill = jnp.zeros((16 - 2 * ncomp - 2, LANES), F32)
    strip, first, last = (slice(EDGE, EDGE + size), slice(EDGE - 1, EDGE), slice(EDGE + size, EDGE + size + 1))

    def send(ref, x, inner):
        del inner
        for comp in range(ncomp):
            j = comp * nx + x
            ref[comp * size : (comp + 1) * size] = frame[j, strip].astype(BF)
            ref[(ncomp + comp) * size : (ncomp + comp + 1) * size] = wind_ref[j, strip].astype(BF)
        at = 2 * ncomp * size
        rows = [frame[comp * nx + x, first] for comp in range(ncomp)] + [conc_ref[x, first]]
        rows += [frame[comp * nx + x, last] for comp in range(ncomp)] + [conc_ref[x, last]]
        ref[at : at + 16] = jnp.concatenate(rows + [fill], 0).astype(BF)

    send_both(odd, send, near_ref, far_ref, nx)


def transport(ny, nhoriz, wind_ref, edge_ref, conc_ref, cols_ref, face_far, face_near, far_ref, near_ref, out_ref):
    nx, size, nz = out_ref.shape
    ncomp = edge_ref.shape[0] // 2
    rows = size + 2 * EDGE
    column, place = (lax.axis_index("horiz"), lax.axis_index("vert"))
    odd = lax.rem(column, 2) == 1
    low = iota((EDGE, nz), 0)

    def either(one, other, start, n):
        return jnp.where(odd, one[start : start + n].astype(F32), other[start : start + n].astype(F32))

    def framed(rows, ends=None, halo=0):
        head, tail = (jnp.zeros((EDGE, nz), F32),) * 2
        if ends is not None:
            head = jnp.where(low == EDGE - 1, ends[halo : halo + 1], head)
            tail = jnp.where(low == 0, ends[ncomp + 1 + halo : ncomp + 2 + halo], tail)
        return jnp.concatenate([head, rows, tail], 0)

    pairs_of = {"below": (near_ref, far_ref, face_near, face_far), "above": (far_ref, near_ref, face_far, face_near)}
    ends, dusts, marks = ({}, {}, {})
    for side, (one, other, face_one, face_other) in pairs_of.items():
        ends[side] = either(one, other, 2 * ncomp * size, 16)
        at = ncomp * ny
        dusts[side] = (
            framed(either(face_one, face_other, at, size), ends[side], ncomp),
            framed(either(face_one, face_other, at + size, size)),
        )
        marks[side] = either(face_one, face_other, at + 2 * size, 16)

    def part(side, i, halo=None):
        rows = either(*pairs_of[side][:2], i * size, size)
        return framed(rows) if halo is None else framed(rows, ends[side], halo)

    below, above = ("below", "above")
    conc = [dusts[below][1], dusts[below][0]]
    conc += [conc_ref[x] for x in range(nx)]
    conc += [dusts[above][0], dusts[above][1]]
    table = jnp.concatenate([marks[below], cols_ref[...], marks[above], jnp.zeros((LANES - 48, LANES), F32)], 0).T[:rows]
    mark = 0
    ground = [mark] + [16 + x for x in range(nx)] + [32 + mark]
    lifted = [mark + 1] + [16 + EDGE + x for x in range(nx)] + [33 + mark]
    layer = iota((rows, nz), 1).astype(F32)
    y = iota((rows, nz), 0) + (place * size - EDGE)
    inside = (y >= 0) & (y < ny)
    first, last = layer == 0.0, layer == nz - 1.0
    zero = jnp.zeros((rows, nz), F32)
    state = [None] * (nx + 2)
    for p in range(nx + 2):
        comps = []
        for comp in range(ncomp):
            if p == 0:
                w = part(below, ncomp + comp) + 0.12 * edge_ref[comp].astype(F32)
            elif p == nx + 1:
                w = part(above, ncomp + comp) + 0.12 * edge_ref[ncomp + comp].astype(F32)
            else:
                w = wind_ref[comp * nx + p - 1]
                if p == 1:
                    w = w + 0.12 * part(below, comp, comp)
                if p == nx:
                    w = w + 0.12 * part(above, comp, comp)
            comps.append(w)
        gu, gv, gw = comps
        speed = jnp.sqrt(gu * gu + gv * gv)
        rise = jnp.broadcast_to(table[:, lifted[p] : lifted[p] + 1], (rows, nz))
        base = jnp.broadcast_to(table[:, ground[p] : ground[p] + 1], (rows, nz))
        lift = jnp.where(layer == rise, 0.5 * jnp.maximum(speed - 1.0, 0.0), 0.0)
        keep = (layer >= base) & inside
        if p == 0:
            keep = keep & (column > 0)
        if p == nx + 1:
            keep = keep & (column < nhoriz - 1)
        coef = [
            (0.15 * (0.1 - jnp.minimum(a, 0.0)), 0.15 * (0.1 + jnp.maximum(a, 0.0)))
            for a in (gu, gv, gw - 0.5)
        ]
        state[p] = (coef, lift, keep)

    def step(p, c, behind, ahead):
        coef, lift, keep = state[p]
        total = c + lift
        pairs = (
            (ahead, behind),
            (pltpu.roll(c, rows - 1, 0), pltpu.roll(c, 1, 0)),
            (
                jnp.where(last, zero, pltpu.roll(c, nz - 1, 1)),
                jnp.where(first, zero, pltpu.roll(c, 1, 1)),
            ),
        )
        for (forward, back), (post, prev) in zip(coef, pairs):
            total = total + forward * (post - c) - back * (c - prev)
        return jnp.where(keep, total, 0.0)

    once = [step(p, conc[p + 1], conc[p], conc[p + 2]) for p in range(nx + 2)]
    for x in range(nx):
        twice = step(x + 1, once[x + 1], once[x], once[x + 2])
        out_ref[x] = twice[EDGE : EDGE + size]


def pairs(size, start):
    return [p for i in range(start, size - 1, 2) for p in ((i, i + 1), (i + 1, i))]


def local(velocity, dust, eligible, terrain):
    ncomp, nx, ny, nz = velocity.shape
    size = dust.shape[1]
    nh, nv = (lax.axis_size("horiz"), lax.axis_size("vert"))
    rows = size + 2 * EDGE
    near_pairs, far_pairs = (pairs(nh, 0), pairs(nh, 1))
    nplane = ncomp * nx
    anywhere = pl.BlockSpec(memory_space=pl.ANY)

    ends = ny // LANES * 16 + nx * EDGE + 32
    strip = nplane * (size + 4)
    held = [pltpu.with_memory_space_constraint(array, pltpu.HBM) for array in (velocity, dust, terrain)]
    strips = call(
        functools.partial(pack_low, size),
        [shaped(strip + {1: ends, 2: 16}.get(t, 0), LANES) for t in range(nv)],
        "pack_low",
        [
            pltpu.VMEM((ncomp, nx, ny, nz), F32),
            pltpu.VMEM((16, ny), F32),
            pltpu.VMEM((nv, 4 * nplane, LANES), F32),
            pltpu.VMEM((nx, EDGE, nz), F32),
            pltpu.VMEM((nx, size), jnp.int32),
            pltpu.SemaphoreType.DMA((nplane + 2,)),
        ],
        in_specs=[anywhere] * 3,
        out_specs=[VMEM] * nv,
    )(*held)
    got = [strips[0]] + [lax.ppermute(strips[t], "vert", [(0, t)]) for t in range(1, nv)]

    first, second, mine, *lays = call(
        functools.partial(pack_ends, size, nv),
        [shaped(ends, LANES)] * 2 + [shaped(3, 16, LANES)] + [shaped(16, LANES)] * (nv - 3),
        "pack_ends",
        [pltpu.VMEM((16, ny), F32)] * 2
        + [pltpu.VMEM((2, nx, EDGE, nz), F32), pltpu.VMEM((nx, size), jnp.int32), pltpu.SemaphoreType.DMA((3,))],
        in_specs=[VMEM] + [anywhere] * 3,
    )(velocity, *held[1:], strips[-1])
    first = lax.ppermute(first, "vert", pairs(nv, 0)[1:])
    second = lax.ppermute(second, "vert", pairs(nv, 1))
    lays = [mine] + [lax.ppermute(lay, "vert", [(1, t + 3)]) for t, lay in enumerate(lays)]

    far, near = call(
        pack_sides, [shaped(ncomp * ny + 2 * size + 16, LANES)] * 2, "pack_sides", in_specs=[VMEM] * 4 + [anywhere]
    )(velocity, dust, terrain, eligible, lays[-1])
    far = lax.ppermute(far, "horiz", far_pairs)
    near = lax.ppermute(near, "horiz", near_pairs)

    velocity_next = call(
        advance,
        jax.ShapeDtypeStruct(velocity.shape, F32),
        "advance",
        [pltpu.VMEM((ncomp, nx, ny, nz), F32), pltpu.SemaphoreType.DMA((ncomp,))],
        in_specs=[VMEM] * 6,
        out_specs=anywhere,
    )(velocity, far, near, first, second, got[1])

    wire = 2 * ncomp * size + 16
    wind, conc, cols, mf, mn, edge = call(
        functools.partial(prepare, nv),
        [
            shaped(nplane, rows, LANES, dtype=F32),
            shaped(nx, rows, LANES, dtype=F32),
            shaped(16, LANES, dtype=F32),
            shaped(wire, LANES),
            shaped(wire, LANES),
            shaped(2 * ncomp, rows, LANES),
        ],
        "prepare",
        [pltpu.VMEM((nplane, rows, LANES), F32)],
    )(*got, *lays, dust, terrain, eligible, first, second)
    mf = lax.ppermute(mf, "horiz", far_pairs)
    mn = lax.ppermute(mn, "horiz", near_pairs)
    dust_next = call(
        functools.partial(transport, ny, nh),
        jax.ShapeDtypeStruct(dust.shape, F32),
        "transport",
    )(wind, edge, conc, cols, far, near, mf, mn)
    return (velocity_next, dust_next)


def solution(mesh):
    placed = (
        P(None, "horiz", None, "vert"),
        P("horiz", "vert", None),
        P("horiz", None),
        P("horiz", "vert"),
    )
    return jax.shard_map(
        local,
        mesh=mesh,
        in_specs=placed,
        out_specs=(P(None, "horiz", None, "vert"), P("horiz", "vert", None)),
        check_vma=False,
    )
```

```python
import functools

import jax
import jax.numpy as jnp
from jax import lax
from jax.experimental import pallas as pl
from jax.experimental.pallas import tpu as pltpu
from jax.sharding import PartitionSpec as P

DSTEPS = 2
LANES = 128
EDGE = 8
BF = jnp.bfloat16
F32 = jnp.float32

VMEM = pl.BlockSpec(memory_space=pltpu.VMEM)


def call(kernel, out_shape, name, scratch=(), cost=1 << 20, **kwargs):
    return pl.pallas_call(
        kernel,
        out_shape=out_shape,
        scratch_shapes=list(scratch),
        compiler_params=pltpu.CompilerParams(vmem_limit_bytes=40 << 20),
        cost_estimate=pl.CostEstimate(flops=cost, bytes_accessed=cost, transcendentals=0),
        name=name,
        **kwargs,
    )


def shaped(*dims, dtype=BF):
    return jax.ShapeDtypeStruct(dims, dtype)


def iota(shape, dim):
    return lax.broadcasted_iota(jnp.int32, shape, dim)


def pick(shape, pairs):
    row, col = iota(shape, 0), iota(shape, 1)
    hit = functools.reduce(jnp.logical_or, [(row == r) & (col == c) for r, c in pairs])
    return jnp.where(hit, 1.0, 0.0).astype(BF)


def turn_faces(v_ref, comp, ends, outs):
    _, nx, ny, _ = v_ref.shape
    for x in range(nx):
        j = comp * nx + x
        for half in range(ny // LANES):
            span = slice(half * LANES, (half + 1) * LANES)
            block = v_ref[comp, x, span, :].astype(BF)
            rows = lax.dot_general(ends, block, (((1,), (1,)), ((), ())), preferred_element_type=F32)
            for i, out in enumerate(outs):
                out[j : j + 1, span] = rows[i : i + 1]


def beside_rows(nplane, t, nstrips):
    return -(-2 * nplane // 16) * 16 if t == nstrips - 1 else 4 * nplane


def halo_rows(start, size):
    return (start - 2, start - 1, start + size, start + size + 1)


def columns(place, terrain_ref, eligible_ref):
    nx, size = terrain_ref.shape
    own = jnp.concatenate([terrain_ref[...].astype(F32), jnp.zeros((nx, LANES - size), F32)], 1)
    ground = pltpu.roll(own, EDGE, 1)
    return ground, lifted_layer(place, ground, eligible_ref, size)


def lifted_layer(place, ground, eligible_ref, size):
    y = iota(ground.shape, 1) + (place * size - EDGE)
    flags = jnp.zeros(ground.shape, jnp.int32)
    for b in range(eligible_ref.shape[1]):
        inside = (y >= b * 128) & (y < (b + 1) * 128)
        flags = jnp.where(inside, jnp.broadcast_to(eligible_ref[:, b : b + 1], ground.shape), flags)
    return jnp.where(flags == 1, ground, -1.0)


def pack_sides(v_ref, dust_ref, terrain_ref, eligible_ref, after_ref, far_ref, near_ref):
    del after_ref
    ncomp, nx, ny, _ = v_ref.shape
    size = dust_ref.shape[1]
    odd = lax.rem(lax.axis_index("horiz"), 2) == 1
    ground, lifted = columns(lax.axis_index("vert"), terrain_ref, eligible_ref)
    fill = jnp.zeros((14, LANES), F32)

    def send(ref, x, inner):
        for comp in range(ncomp):
            ref[comp * ny : (comp + 1) * ny] = v_ref[comp, x].astype(BF)
        at = ncomp * ny
        ref[at : at + size] = dust_ref[x].astype(BF)
        ref[at + size : at + 2 * size] = dust_ref[inner].astype(BF)
        at = at + 2 * size
        ref[at : at + 16] = jnp.concatenate([ground[x : x + 1], lifted[x : x + 1], fill], 0).astype(BF)

    send_both(odd, send, near_ref, far_ref, nx)


def send_both(odd, send, near_ref, far_ref, nx):
    @pl.when(odd)
    def _():
        send(near_ref, 0, 1)
        send(far_ref, nx - 1, nx - 2)

    @pl.when(jnp.logical_not(odd))
    def _():
        send(near_ref, nx - 1, nx - 2)
        send(far_ref, 0, 1)


def start_all(copies):
    for copy in copies:
        copy.start()
    return copies


def wait_all(copies):
    for copy in copies:
        copy.wait()


def write_ends(ref, at, face, dust, land, layer=None):
    nx, size = land.shape
    terrain = jnp.concatenate([land.astype(F32), jnp.zeros((nx, LANES - size), F32)], 1)
    fill = jnp.zeros((16 - 3 * nx, LANES), F32)
    for half in range(face.shape[1] // LANES):
        ref[at : at + 16] = face[:, half * LANES : (half + 1) * LANES].astype(BF)
        at = at + 16
    ref[at : at + 16] = jnp.concatenate([dust[x] for x in range(nx)] + [terrain, fill], 0).astype(BF)
    if layer is not None:
        ref[at + 16 : at + 32] = layer


def pack_low(size, v_ref, dust_ref, terrain_ref, *refs):
    outs, (buf, high, side, dusts, land, sems) = (refs[:-6], refs[-6:])
    ncomp, nx, ny, nz = v_ref.shape
    nplane = ncomp * nx

    @pl.when(lax.axis_index("vert") == 0)
    def _():
        planes = start_all(
            [pltpu.make_async_copy(v_ref.at[j // nx, j % nx], buf.at[j // nx, j % nx], sems.at[j]) for j in range(nplane)]
        )
        small = start_all(
            [
                pltpu.make_async_copy(dust_ref.at[:, size - EDGE :], dusts, sems.at[nplane]),
                pltpu.make_async_copy(terrain_ref, land, sems.at[nplane + 1]),
            ]
        )
        side[...] = jnp.zeros_like(side)
        high[...] = jnp.zeros_like(high)
        end = pick((16, nz), [(0, nz - 1)])
        for comp in range(ncomp):
            wait_all(planes[comp * nx : (comp + 1) * nx])
            turn_faces(buf, comp, end, [high])
            for x in range(nx):
                j = comp * nx + x
                for t, out in enumerate(outs):
                    out[j * size : (j + 1) * size] = buf[comp, x, t * size : (t + 1) * size, :].astype(BF)
                    for i, y in enumerate(halo_rows(t * size, size)):
                        if 0 <= y < ny:
                            side[t, i * nplane + j : i * nplane + j + 1] = buf[comp, x, y : y + 1, :]
        for t, out in enumerate(outs):
            count = beside_rows(nplane, t, len(outs))
            out[nplane * size : nplane * size + count] = side[t, :count].astype(BF)
        wait_all(small)
        write_ends(outs[1], nplane * (size + 4), high, dusts[:, EDGE - 2 :], land[...])


def pack_ends(size, nstrips, v_ref, dust_ref, terrain_ref, after_ref, first_ref, second_ref, mine_ref, *refs):
    del after_ref
    lays, (low, high, dusts, land, sems) = (refs[:-5], refs[-5:])
    ncomp, nx, ny, nz = v_ref.shape
    odd = lax.rem(lax.axis_index("vert"), 2) == 1
    small = start_all(
        [
            pltpu.make_async_copy(dust_ref.at[:, :EDGE], dusts.at[0], sems.at[0]),
            pltpu.make_async_copy(dust_ref.at[:, size - EDGE :], dusts.at[1], sems.at[1]),
            pltpu.make_async_copy(terrain_ref, land, sems.at[2]),
        ]
    )
    low[...] = jnp.zeros_like(low)
    high[...] = jnp.zeros_like(high)
    ends = pick((16, nz), [(0, 0), (1, nz - 1)])
    for comp in range(ncomp):
        turn_faces(v_ref, comp, ends, [low, high])
    lane = iota((16, LANES), 1)
    whole = low[...]
    for t in range(nstrips):
        shift = (EDGE - t * size) % ny
        moved = pltpu.roll(whole, shift, 1) if shift else whole
        row = lane + (t * size - EDGE)
        part = jnp.where((row >= 0) & (row < ny), moved[:, :LANES], 0.0).astype(BF)
        if t < 3:
            mine_ref[t] = part
        elif t == 3:
            second_ref[second_ref.shape[0] - 16 :] = part
        else:
            lays[t - 4][...] = part
    wait_all(small)

    @pl.when(odd)
    def _():
        write_ends(first_ref, 0, low, dusts[0, :, :2], land[...], mine_ref[0])
        write_ends(second_ref, 0, high, dusts[1, :, EDGE - 2 :], land[...], mine_ref[2])

    @pl.when(jnp.logical_not(odd))
    def _():
        write_ends(first_ref, 0, high, dusts[1, :, EDGE - 2 :], land[...], mine_ref[2])
        write_ends(second_ref, 0, low, dusts[0, :, :2], land[...], mine_ref[0])


def relay(base_ref, second_ref, first_ref):
    first_ref[...] = base_ref[...]

    @pl.when(lax.axis_index("vert") == 2)
    def _():
        first_ref[first_ref.shape[0] - 16 :] = second_ref[second_ref.shape[0] - 16 :]


def sorted_ends(first_ref, second_ref, strip_ref, start, n):
    place = lax.axis_index("vert")
    odd = lax.rem(place, 2) == 1
    base = strip_ref.shape[0] - first_ref.shape[0] + 16 + start
    first, second = (first_ref[start : start + n].astype(F32), second_ref[start : start + n].astype(F32))
    below = jnp.where(place == 1, strip_ref[base : base + n].astype(F32), jnp.where(odd, first, second))
    return (jnp.where(odd, second, first), below)


def advance(v_ref, far_ref, near_ref, first_ref, second_ref, strip_ref, out_ref, buf, sems):
    ncomp, nx, ny, nz = v_ref.shape
    odd = lax.rem(lax.axis_index("horiz"), 2) == 1
    row, lane = iota((LANES, nz), 0), iota((LANES, nz), 1)
    nb = ny // LANES
    turned = []
    for half in range(nb):
        over, under = sorted_ends(first_ref, second_ref, strip_ref, half * 16, 16)
        faces = jnp.concatenate([over, under, jnp.zeros((LANES - 32, LANES), F32)], 0)
        turned.append(faces.T.astype(BF))
    copies = []
    for comp in range(ncomp):
        for half in range(nb):
            a = half * LANES
            span = slice(a, a + LANES)
            rows = slice(comp * ny + a, comp * ny + a + LANES)
            near, far = (near_ref[rows].astype(F32), far_ref[rows].astype(F32))
            below = jnp.where(odd, near, far)
            above = jnp.where(odd, far, near)
            for x in range(nx):
                j = comp * nx + x
                place = ((row == j) & (lane == nz - 1)) | ((row == 16 + j) & (lane == 0))
                place = jnp.where(place, 1.0, 0.0).astype(BF)
                sums = lax.dot_general(turned[half], place, (((1,), (0,)), ((), ())), preferred_element_type=F32)
                f = v_ref[comp, x, span, :]
                sums = sums + jnp.where(lane == 0, 0.0, pltpu.roll(f, 1, 1))
                sums = sums + jnp.where(lane == nz - 1, 0.0, pltpu.roll(f, nz - 1, 1))
                prev = v_ref[comp, x, a - 1 : a, :] if a else jnp.zeros((1, nz), F32)
                post = v_ref[comp, x, a + LANES : a + LANES + 1, :] if half < nb - 1 else jnp.zeros((1, nz), F32)
                sums = sums + jnp.where(row == 0, prev, pltpu.roll(f, 1, 0))
                sums = sums + jnp.where(row == LANES - 1, post, pltpu.roll(f, LANES - 1, 0))
                sums = sums + (v_ref[comp, x - 1, span, :] if x else below)
                sums = sums + (v_ref[comp, x + 1, span, :] if x < nx - 1 else above)
                buf[comp, x, span, :] = f + 0.12 * (sums - 6.0 * f)
        copies.append(pltpu.make_async_copy(buf.at[comp], out_ref.at[comp], sems.at[comp]))
        copies[-1].start()
    for copy in copies:
        copy.wait()


def prepare(nstrips, *refs):
    strips = refs[:nstrips]
    nlay = 1 + max(nstrips - 4, 0)
    lays = refs[nstrips : nstrips + nlay]
    dust_ref, terrain_ref, eligible_ref, first_ref, second_ref = refs[nstrips + nlay : nstrips + nlay + 5]
    wind_ref, conc_ref, cols_ref, far_ref, near_ref, edge_ref, frame = refs[nstrips + nlay + 5 :]
    nx, size, nz = dust_ref.shape
    nplane = frame.shape[0]
    ncomp = nplane // nx
    rows = size + 2 * EDGE
    place = lax.axis_index("vert")
    odd = lax.rem(lax.axis_index("horiz"), 2) == 1
    frame[:, :EDGE] = jnp.zeros((nplane, EDGE, nz), F32)
    frame[:, EDGE + size :] = jnp.zeros((nplane, EDGE, nz), F32)
    for t in range(nstrips):
        @pl.when(place == t)
        def _(t=t):
            count = beside_rows(nplane, t, nstrips)
            beside = strips[t][nplane * size : nplane * size + count].astype(F32)
            for j in range(nplane):
                frame[j, EDGE : EDGE + size] = strips[t][j * size : (j + 1) * size].astype(F32)
                for i, y in enumerate(halo_rows(EDGE, size)[: count // nplane]):
                    frame[j, y : y + 1] = beside[i * nplane + j : i * nplane + j + 1]

    face = first_ref.shape[0] - 32
    over, under = sorted_ends(first_ref, second_ref, strips[1], face, 16)
    zero = jnp.zeros((16, LANES), F32)
    layer = jnp.where(place == 0, first_ref[face + 16 : face + 32].astype(F32), zero)
    layer = layer + jnp.where(place == 1, lays[0][min(1, nstrips - 1)].astype(F32), zero)
    layer = layer + jnp.where(place == 2, second_ref[face + 16 : face + 32].astype(F32), zero)
    layer = layer + jnp.where(place == 3, first_ref[face + 16 : face + 32].astype(F32), zero)
    for got in lays[1:]:
        layer = layer + got[...].astype(F32)
    layer = jnp.concatenate([layer, jnp.zeros((LANES - 16, LANES), F32)], 0)
    turned = layer.T.astype(BF)[:rows]
    brow, blane = iota((LANES, nz), 0), iota((LANES, nz), 1)
    beside = jnp.where((brow == blane + 1) | (brow == blane - 1), 1.0, 0.0).astype(BF)
    edges = {}
    for comp in range(ncomp):
        f = [frame[comp * nx + x] for x in range(nx)]
        for x in range(nx):
            j = comp * nx + x
            raw = f[x].astype(BF)
            near = jnp.dot(raw, beside, preferred_element_type=F32)
            top = jnp.where((brow == j) & (blane == nz - 1), 1.0, 0.0).astype(BF)
            near = near + jnp.dot(turned, top, preferred_element_type=F32)
            near = near + pltpu.roll(f[x], 1, 0) + pltpu.roll(f[x], rows - 1, 0)
            if x:
                near = near + f[x - 1]
            if x < nx - 1:
                near = near + f[x + 1]
            wind = 0.28 * f[x] + 0.12 * near
            wind_ref[j] = wind
            if x == 0:
                edge_ref[comp] = raw
            if x == nx - 1:
                edge_ref[ncomp + comp] = raw
    row = iota((EDGE, nz), 0)
    for x in range(nx):
        one, two = (slice(2 * x, 2 * x + 1), slice(2 * x + 1, 2 * x + 2))
        before = jnp.where(row == EDGE - 2, under[one], jnp.where(row == EDGE - 1, under[two], 0.0))
        after = jnp.where(row == 0, over[one], jnp.where(row == 1, over[two], 0.0))
        conc_ref[x] = jnp.concatenate([before, dust_ref[x], after], 0)
    lane = iota((nx, LANES), 1)
    own = terrain_ref[...].astype(F32)
    own = jnp.concatenate([own, jnp.zeros((nx, LANES - size), F32)], 1)
    land = slice(2 * nx, 3 * nx)
    before = pltpu.roll(under, (EDGE - size) % LANES, 1)[land]
    after = pltpu.roll(over, (EDGE + size) % LANES, 1)[land]
    ground = jnp.where(lane < EDGE, before, jnp.where(lane < EDGE + size, pltpu.roll(own, EDGE, 1), after))
    lifted = lifted_layer(place, ground, eligible_ref, size)
    cols_ref[...] = jnp.zeros_like(cols_ref)
    cols_ref[:nx] = ground
    cols_ref[EDGE : EDGE + nx] = lifted
    fill = jnp.zeros((16 - 2 * ncomp - 2, LANES), F32)
    strip, first, last = (slice(EDGE, EDGE + size), slice(EDGE - 1, EDGE), slice(EDGE + size, EDGE + size + 1))

    def send(ref, x, inner):
        del inner
        for comp in range(ncomp):
            j = comp * nx + x
            ref[comp * size : (comp + 1) * size] = frame[j, strip].astype(BF)
            ref[(ncomp + comp) * size : (ncomp + comp + 1) * size] = wind_ref[j, strip].astype(BF)
        at = 2 * ncomp * size
        rows = [frame[comp * nx + x, first] for comp in range(ncomp)] + [conc_ref[x, first]]
        rows += [frame[comp * nx + x, last] for comp in range(ncomp)] + [conc_ref[x, last]]
        ref[at : at + 16] = jnp.concatenate(rows + [fill], 0).astype(BF)

    send_both(odd, send, near_ref, far_ref, nx)


def transport(ny, nhoriz, wind_ref, edge_ref, conc_ref, cols_ref, face_far, face_near, far_ref, near_ref, out_ref):
    nx, size, nz = out_ref.shape
    ncomp = edge_ref.shape[0] // 2
    rows = size + 2 * EDGE
    column, place = (lax.axis_index("horiz"), lax.axis_index("vert"))
    odd = lax.rem(column, 2) == 1
    low = iota((EDGE, nz), 0)

    def either(one, other, start, n):
        return jnp.where(odd, one[start : start + n].astype(F32), other[start : start + n].astype(F32))

    def framed(rows, ends=None, halo=0):
        head, tail = (jnp.zeros((EDGE, nz), F32),) * 2
        if ends is not None:
            head = jnp.where(low == EDGE - 1, ends[halo : halo + 1], head)
            tail = jnp.where(low == 0, ends[ncomp + 1 + halo : ncomp + 2 + halo], tail)
        return jnp.concatenate([head, rows, tail], 0)

    pairs_of = {"below": (near_ref, far_ref, face_near, face_far), "above": (far_ref, near_ref, face_far, face_near)}
    ends, dusts, marks = ({}, {}, {})
    for side, (one, other, face_one, face_other) in pairs_of.items():
        ends[side] = either(one, other, 2 * ncomp * size, 16)
        at = ncomp * ny
        dusts[side] = (
            framed(either(face_one, face_other, at, size), ends[side], ncomp),
            framed(either(face_one, face_other, at + size, size)),
        )
        marks[side] = either(face_one, face_other, at + 2 * size, 16)

    def part(side, i, halo=None):
        rows = either(*pairs_of[side][:2], i * size, size)
        return framed(rows) if halo is None else framed(rows, ends[side], halo)

    below, above = ("below", "above")
    conc = [dusts[below][1], dusts[below][0]]
    conc += [conc_ref[x] for x in range(nx)]
    conc += [dusts[above][0], dusts[above][1]]
    table = jnp.concatenate([marks[below], cols_ref[...], marks[above], jnp.zeros((LANES - 48, LANES), F32)], 0).T[:rows]
    mark = 0
    ground = [mark] + [16 + x for x in range(nx)] + [32 + mark]
    lifted = [mark + 1] + [16 + EDGE + x for x in range(nx)] + [33 + mark]
    layer = iota((rows, nz), 1).astype(F32)
    y = iota((rows, nz), 0) + (place * size - EDGE)
    inside = (y >= 0) & (y < ny)
    first, last = layer == 0.0, layer == nz - 1.0
    zero = jnp.zeros((rows, nz), F32)
    state = [None] * (nx + 2)
    for p in range(nx + 2):
        comps = []
        for comp in range(ncomp):
            if p == 0:
                w = part(below, ncomp + comp) + 0.12 * edge_ref[comp].astype(F32)
            elif p == nx + 1:
                w = part(above, ncomp + comp) + 0.12 * edge_ref[ncomp + comp].astype(F32)
            else:
                w = wind_ref[comp * nx + p - 1]
                if p == 1:
                    w = w + 0.12 * part(below, comp, comp)
                if p == nx:
                    w = w + 0.12 * part(above, comp, comp)
            comps.append(w)
        gu, gv, gw = comps
        speed = jnp.sqrt(gu * gu + gv * gv)
        rise = jnp.broadcast_to(table[:, lifted[p] : lifted[p] + 1], (rows, nz))
        base = jnp.broadcast_to(table[:, ground[p] : ground[p] + 1], (rows, nz))
        lift = jnp.where(layer == rise, 0.5 * jnp.maximum(speed - 1.0, 0.0), 0.0)
        keep = (layer >= base) & inside
        if p == 0:
            keep = keep & (column > 0)
        if p == nx + 1:
            keep = keep & (column < nhoriz - 1)
        coef = [
            (0.15 * (0.1 - jnp.minimum(a, 0.0)), 0.15 * (0.1 + jnp.maximum(a, 0.0)))
            for a in (gu, gv, gw - 0.5)
        ]
        state[p] = (coef, lift, keep)

    def step(p, c, behind, ahead):
        coef, lift, keep = state[p]
        total = c + lift
        pairs = (
            (ahead, behind),
            (pltpu.roll(c, rows - 1, 0), pltpu.roll(c, 1, 0)),
            (
                jnp.where(last, zero, pltpu.roll(c, nz - 1, 1)),
                jnp.where(first, zero, pltpu.roll(c, 1, 1)),
            ),
        )
        for (forward, back), (post, prev) in zip(coef, pairs):
            total = total + forward * (post - c) - back * (c - prev)
        return jnp.where(keep, total, 0.0)

    once = [step(p, conc[p + 1], conc[p], conc[p + 2]) for p in range(nx + 2)]
    for x in range(nx):
        twice = step(x + 1, once[x + 1], once[x], once[x + 2])
        out_ref[x] = twice[EDGE : EDGE + size]


def pairs(size, start):
    return [p for i in range(start, size - 1, 2) for p in ((i, i + 1), (i + 1, i))]


def local(velocity, dust, eligible, terrain):
    ncomp, nx, ny, nz = velocity.shape
    size = dust.shape[1]
    nh, nv = (lax.axis_size("horiz"), lax.axis_size("vert"))
    rows = size + 2 * EDGE
    near_pairs, far_pairs = (pairs(nh, 0), pairs(nh, 1))
    nplane = ncomp * nx
    anywhere = pl.BlockSpec(memory_space=pl.ANY)

    ends = ny // LANES * 16 + 32
    held = [pltpu.with_memory_space_constraint(array, pltpu.HBM) for array in (velocity, dust, terrain)]
    strips = call(
        functools.partial(pack_low, size),
        [shaped(nplane * size + beside_rows(nplane, t, nv) + (ends - 16 if t == 1 else 0), LANES) for t in range(nv)],
        "pack_low",
        [
            pltpu.VMEM((ncomp, nx, ny, nz), F32),
            pltpu.VMEM((16, ny), F32),
            pltpu.VMEM((nv, 4 * nplane, LANES), F32),
            pltpu.VMEM((nx, EDGE, nz), F32),
            pltpu.VMEM((nx, size), jnp.int32),
            pltpu.SemaphoreType.DMA((nplane + 2,)),
        ],
        in_specs=[anywhere] * 3,
        out_specs=[VMEM] * nv,
    )(*held)
    got = [strips[0]] + [lax.ppermute(strips[t], "vert", [(0, t)]) for t in range(1, nv)]

    first, second, mine, *lays = call(
        functools.partial(pack_ends, size, nv),
        [shaped(ends, LANES), shaped(ends + 16, LANES), shaped(3, 16, LANES)] + [shaped(16, LANES)] * (nv - 4),
        "pack_ends",
        [pltpu.VMEM((16, ny), F32)] * 2
        + [pltpu.VMEM((2, nx, EDGE, nz), F32), pltpu.VMEM((nx, size), jnp.int32), pltpu.SemaphoreType.DMA((3,))],
        in_specs=[VMEM] + [anywhere] * 3,
    )(velocity, *held[1:], strips[-1])
    second = lax.ppermute(second, "vert", pairs(nv, 1))
    first = call(relay, shaped(ends, LANES), "relay")(first, second)
    first = lax.ppermute(first, "vert", pairs(nv, 0)[1:])
    lays = [mine] + [lax.ppermute(lay, "vert", [(1, t + 4)]) for t, lay in enumerate(lays)]

    far, near = call(
        pack_sides, [shaped(ncomp * ny + 2 * size + 16, LANES)] * 2, "pack_sides", in_specs=[VMEM] * 4 + [anywhere]
    )(velocity, dust, terrain, eligible, second)
    far = lax.ppermute(far, "horiz", far_pairs)
    near = lax.ppermute(near, "horiz", near_pairs)

    velocity_next = call(
        advance,
        jax.ShapeDtypeStruct(velocity.shape, F32),
        "advance",
        [pltpu.VMEM((ncomp, nx, ny, nz), F32), pltpu.SemaphoreType.DMA((ncomp,))],
        in_specs=[VMEM] * 6,
        out_specs=anywhere,
    )(velocity, far, near, first, second, got[1])

    wire = 2 * ncomp * size + 16
    wind, conc, cols, mf, mn, edge = call(
        functools.partial(prepare, nv),
        [
            shaped(nplane, rows, LANES, dtype=F32),
            shaped(nx, rows, LANES, dtype=F32),
            shaped(16, LANES, dtype=F32),
            shaped(wire, LANES),
            shaped(wire, LANES),
            shaped(2 * ncomp, rows, LANES),
        ],
        "prepare",
        [pltpu.VMEM((nplane, rows, LANES), F32)],
    )(*got, *lays, dust, terrain, eligible, first, second)
    mf = lax.ppermute(mf, "horiz", far_pairs)
    mn = lax.ppermute(mn, "horiz", near_pairs)
    dust_next = call(
        functools.partial(transport, ny, nh),
        jax.ShapeDtypeStruct(dust.shape, F32),
        "transport",
    )(wind, edge, conc, cols, far, near, mf, mn)
    return (velocity_next, dust_next)


def solution(mesh):
    placed = (
        P(None, "horiz", None, "vert"),
        P("horiz", "vert", None),
        P("horiz", None),
        P("horiz", "vert"),
    )
    return jax.shard_map(
        local,
        mesh=mesh,
        in_specs=placed,
        out_specs=(P(None, "horiz", None, "vert"), P("horiz", "vert", None)),
        check_vma=False,
    )
```

```python
import functools

import jax
import jax.numpy as jnp
from jax import lax
from jax.experimental import pallas as pl
from jax.experimental.pallas import tpu as pltpu
from jax.sharding import PartitionSpec as P

DSTEPS = 2
LANES = 128
EDGE = 8
BF = jnp.bfloat16
F32 = jnp.float32

VMEM = pl.BlockSpec(memory_space=pltpu.VMEM)


def call(kernel, out_shape, name, scratch=(), cost=1 << 20, **kwargs):
    return pl.pallas_call(
        kernel,
        out_shape=out_shape,
        scratch_shapes=list(scratch),
        compiler_params=pltpu.CompilerParams(vmem_limit_bytes=40 << 20),
        cost_estimate=pl.CostEstimate(flops=cost, bytes_accessed=cost, transcendentals=0),
        name=name,
        **kwargs,
    )


def shaped(*dims, dtype=BF):
    return jax.ShapeDtypeStruct(dims, dtype)


def iota(shape, dim):
    return lax.broadcasted_iota(jnp.int32, shape, dim)


def pick(shape, pairs):
    row, col = iota(shape, 0), iota(shape, 1)
    hit = functools.reduce(jnp.logical_or, [(row == r) & (col == c) for r, c in pairs])
    return jnp.where(hit, 1.0, 0.0).astype(BF)


def turn_faces(v_ref, comp, ends, outs):
    _, nx, ny, _ = v_ref.shape
    for x in range(nx):
        j = comp * nx + x
        for half in range(ny // LANES):
            span = slice(half * LANES, (half + 1) * LANES)
            block = v_ref[comp, x, span, :].astype(BF)
            rows = lax.dot_general(ends, block, (((1,), (1,)), ((), ())), preferred_element_type=F32)
            for i, out in enumerate(outs):
                out[j : j + 1, span] = rows[i : i + 1]


def beside_rows(nplane, t, nstrips):
    return -(-2 * nplane // 16) * 16 if t == nstrips - 1 else 4 * nplane


def halo_rows(start, size):
    return (start - 2, start - 1, start + size, start + size + 1)


def columns(place, terrain_ref, eligible_ref):
    nx, size = terrain_ref.shape
    own = jnp.concatenate([terrain_ref[...].astype(F32), jnp.zeros((nx, LANES - size), F32)], 1)
    ground = pltpu.roll(own, EDGE, 1)
    return ground, lifted_layer(place, ground, eligible_ref, size)


def lifted_layer(place, ground, eligible_ref, size):
    y = iota(ground.shape, 1) + (place * size - EDGE)
    flags = jnp.zeros(ground.shape, jnp.int32)
    for b in range(eligible_ref.shape[1]):
        inside = (y >= b * 128) & (y < (b + 1) * 128)
        flags = jnp.where(inside, jnp.broadcast_to(eligible_ref[:, b : b + 1], ground.shape), flags)
    return jnp.where(flags == 1, ground, -1.0)


def pack_sides(v_ref, dust_ref, terrain_ref, eligible_ref, after_ref, far_ref, near_ref):
    del after_ref
    ncomp, nx, ny, _ = v_ref.shape
    size = dust_ref.shape[1]
    odd = lax.rem(lax.axis_index("horiz"), 2) == 1
    ground, lifted = columns(lax.axis_index("vert"), terrain_ref, eligible_ref)
    fill = jnp.zeros((14, LANES), F32)

    def send(ref, x, inner):
        for comp in range(ncomp):
            ref[comp * ny : (comp + 1) * ny] = v_ref[comp, x].astype(BF)
        at = ncomp * ny
        ref[at : at + size] = dust_ref[x].astype(BF)
        ref[at + size : at + 2 * size] = dust_ref[inner].astype(BF)
        at = at + 2 * size
        ref[at : at + 16] = jnp.concatenate([ground[x : x + 1], lifted[x : x + 1], fill], 0).astype(BF)

    send_both(odd, send, near_ref, far_ref, nx)


def send_both(odd, send, near_ref, far_ref, nx):
    @pl.when(odd)
    def _():
        send(near_ref, 0, 1)
        send(far_ref, nx - 1, nx - 2)

    @pl.when(jnp.logical_not(odd))
    def _():
        send(near_ref, nx - 1, nx - 2)
        send(far_ref, 0, 1)


def start_all(copies):
    for copy in copies:
        copy.start()
    return copies


def wait_all(copies):
    for copy in copies:
        copy.wait()


def write_ends(ref, at, face, dust, land, layer=None):
    nx, size = land.shape
    terrain = jnp.concatenate([land.astype(F32), jnp.zeros((nx, LANES - size), F32)], 1)
    fill = jnp.zeros((16 - 3 * nx, LANES), F32)
    for half in range(face.shape[1] // LANES):
        ref[at : at + 16] = face[:, half * LANES : (half + 1) * LANES].astype(BF)
        at = at + 16
    ref[at : at + 16] = jnp.concatenate([dust[x] for x in range(nx)] + [terrain, fill], 0).astype(BF)
    if layer is not None:
        ref[at + 16 : at + 32] = layer


def pack_low(size, v_ref, dust_ref, terrain_ref, *refs):
    outs, (buf, high, side, dusts, land, sems) = (refs[:-6], refs[-6:])
    ncomp, nx, ny, nz = v_ref.shape
    nplane = ncomp * nx

    @pl.when(lax.axis_index("vert") == 0)
    def _():
        planes = start_all(
            [pltpu.make_async_copy(v_ref.at[j // nx, j % nx], buf.at[j // nx, j % nx], sems.at[j]) for j in range(nplane)]
        )
        small = start_all(
            [
                pltpu.make_async_copy(dust_ref.at[:, size - EDGE :], dusts, sems.at[nplane]),
                pltpu.make_async_copy(terrain_ref, land, sems.at[nplane + 1]),
            ]
        )
        side[...] = jnp.zeros_like(side)
        high[...] = jnp.zeros_like(high)
        end = pick((16, nz), [(0, nz - 1)])
        for comp in range(ncomp):
            wait_all(planes[comp * nx : (comp + 1) * nx])
            turn_faces(buf, comp, end, [high])
            for x in range(nx):
                j = comp * nx + x
                for t, out in enumerate(outs):
                    out[j * size : (j + 1) * size] = buf[comp, x, t * size : (t + 1) * size, :].astype(BF)
                    for i, y in enumerate(halo_rows(t * size, size)):
                        if 0 <= y < ny:
                            side[t, i * nplane + j : i * nplane + j + 1] = buf[comp, x, y : y + 1, :]
        for t, out in enumerate(outs):
            count = beside_rows(nplane, t, len(outs))
            out[nplane * size : nplane * size + count] = side[t, :count].astype(BF)
        wait_all(small)
        write_ends(outs[1], nplane * (size + 4), high, dusts[:, EDGE - 2 :], land[...])


def pack_ends(size, nstrips, v_ref, dust_ref, terrain_ref, after_ref, first_ref, second_ref, mine_ref, *refs):
    del after_ref
    lays, (low, high, dusts, land, sems) = (refs[:-5], refs[-5:])
    ncomp, nx, ny, nz = v_ref.shape
    odd = lax.rem(lax.axis_index("vert"), 2) == 1
    small = start_all(
        [
            pltpu.make_async_copy(dust_ref.at[:, :EDGE], dusts.at[0], sems.at[0]),
            pltpu.make_async_copy(dust_ref.at[:, size - EDGE :], dusts.at[1], sems.at[1]),
            pltpu.make_async_copy(terrain_ref, land, sems.at[2]),
        ]
    )
    low[...] = jnp.zeros_like(low)
    high[...] = jnp.zeros_like(high)
    ends = pick((16, nz), [(0, 0), (1, nz - 1)])
    for comp in range(ncomp):
        turn_faces(v_ref, comp, ends, [low, high])
    lane = iota((16, LANES), 1)
    whole = low[...]
    for t in range(nstrips):
        shift = (EDGE - t * size) % ny
        moved = pltpu.roll(whole, shift, 1) if shift else whole
        row = lane + (t * size - EDGE)
        part = jnp.where((row >= 0) & (row < ny), moved[:, :LANES], 0.0).astype(BF)
        if t < 3:
            mine_ref[t] = part
        elif t == 3:
            second_ref[second_ref.shape[0] - 16 :] = part
        else:
            lays[t - 4][...] = part
    wait_all(small)

    @pl.when(odd)
    def _():
        write_ends(first_ref, 0, low, dusts[0, :, :2], land[...], mine_ref[0])
        write_ends(second_ref, 0, high, dusts[1, :, EDGE - 2 :], land[...], mine_ref[2])

    @pl.when(jnp.logical_not(odd))
    def _():
        write_ends(first_ref, 0, high, dusts[1, :, EDGE - 2 :], land[...], mine_ref[2])
        write_ends(second_ref, 0, low, dusts[0, :, :2], land[...], mine_ref[0])


def relay(base_ref, second_ref, first_ref):
    first_ref[...] = base_ref[...]

    @pl.when(lax.axis_index("vert") == 2)
    def _():
        first_ref[first_ref.shape[0] - 16 :] = second_ref[second_ref.shape[0] - 16 :]


def sorted_ends(first_ref, second_ref, strip_ref, start, n):
    place = lax.axis_index("vert")
    odd = lax.rem(place, 2) == 1
    base = strip_ref.shape[0] - first_ref.shape[0] + 16 + start
    first, second = (first_ref[start : start + n].astype(F32), second_ref[start : start + n].astype(F32))
    below = jnp.where(place == 1, strip_ref[base : base + n].astype(F32), jnp.where(odd, first, second))
    return (jnp.where(odd, second, first), below)


def advance(v_ref, far_ref, near_ref, first_ref, second_ref, strip_ref, out_ref, buf, sems):
    ncomp, nx, ny, nz = v_ref.shape
    odd = lax.rem(lax.axis_index("horiz"), 2) == 1
    row, lane = iota((LANES, nz), 0), iota((LANES, nz), 1)
    nb = ny // LANES
    turned = []
    for half in range(nb):
        over, under = sorted_ends(first_ref, second_ref, strip_ref, half * 16, 16)
        faces = jnp.concatenate([over, under, jnp.zeros((LANES - 32, LANES), F32)], 0)
        turned.append(faces.T.astype(BF))
    copies = []
    for comp in range(ncomp):
        for half in range(nb):
            a = half * LANES
            span = slice(a, a + LANES)
            rows = slice(comp * ny + a, comp * ny + a + LANES)
            near, far = (near_ref[rows].astype(F32), far_ref[rows].astype(F32))
            below = jnp.where(odd, near, far)
            above = jnp.where(odd, far, near)
            for x in range(nx):
                j = comp * nx + x
                place = ((row == j) & (lane == nz - 1)) | ((row == 16 + j) & (lane == 0))
                place = jnp.where(place, 1.0, 0.0).astype(BF)
                sums = lax.dot_general(turned[half], place, (((1,), (0,)), ((), ())), preferred_element_type=F32)
                f = v_ref[comp, x, span, :]
                sums = sums + jnp.where(lane == 0, 0.0, pltpu.roll(f, 1, 1))
                sums = sums + jnp.where(lane == nz - 1, 0.0, pltpu.roll(f, nz - 1, 1))
                prev = v_ref[comp, x, a - 1 : a, :] if a else jnp.zeros((1, nz), F32)
                post = v_ref[comp, x, a + LANES : a + LANES + 1, :] if half < nb - 1 else jnp.zeros((1, nz), F32)
                sums = sums + jnp.where(row == 0, prev, pltpu.roll(f, 1, 0))
                sums = sums + jnp.where(row == LANES - 1, post, pltpu.roll(f, LANES - 1, 0))
                sums = sums + (v_ref[comp, x - 1, span, :] if x else below)
                sums = sums + (v_ref[comp, x + 1, span, :] if x < nx - 1 else above)
                buf[comp, x, span, :] = f + 0.12 * (sums - 6.0 * f)
        copies.append(pltpu.make_async_copy(buf.at[comp], out_ref.at[comp], sems.at[comp]))
        copies[-1].start()
    for copy in copies:
        copy.wait()


def strip_winds(frame, layer, nx, planes):
    nplane, rows, nz = frame.shape
    turned = jnp.concatenate([layer, jnp.zeros((LANES - 16, LANES), F32)], 0).T.astype(BF)[:rows]
    brow, blane = iota((LANES, nz), 0), iota((LANES, nz), 1)
    beside = jnp.where((brow == blane + 1) | (brow == blane - 1), 1.0, 0.0).astype(BF)
    winds = {}
    for comp in range(nplane // nx):
        for x in planes:
            j = comp * nx + x
            f = frame[j]
            near = jnp.dot(f.astype(BF), beside, preferred_element_type=F32)
            top = jnp.where((brow == j) & (blane == nz - 1), 1.0, 0.0).astype(BF)
            near = near + jnp.dot(turned, top, preferred_element_type=F32)
            near = near + pltpu.roll(f, 1, 0) + pltpu.roll(f, rows - 1, 0)
            if x:
                near = near + frame[j - 1]
            if x < nx - 1:
                near = near + frame[j + 1]
            winds[comp, x] = 0.28 * f + 0.12 * near
    return winds


def prepare(nstrips, *refs):
    strips = refs[:nstrips]
    nlay = 1 + max(nstrips - 4, 0)
    lays = refs[nstrips : nstrips + nlay]
    dust_ref, terrain_ref, eligible_ref, first_ref, second_ref = refs[nstrips + nlay : nstrips + nlay + 5]
    wind_ref, conc_ref, cols_ref, far_ref, near_ref, layer_ref, frame = refs[nstrips + nlay + 5 :]
    nx, size, nz = dust_ref.shape
    nplane = frame.shape[0]
    ncomp = nplane // nx
    rows = size + 2 * EDGE
    place = lax.axis_index("vert")
    odd = lax.rem(lax.axis_index("horiz"), 2) == 1
    frame[:, :EDGE] = jnp.zeros((nplane, EDGE, nz), F32)
    frame[:, EDGE + size :] = jnp.zeros((nplane, EDGE, nz), F32)
    for t in range(nstrips):
        @pl.when(place == t)
        def _(t=t):
            count = beside_rows(nplane, t, nstrips)
            beside = strips[t][nplane * size : nplane * size + count].astype(F32)
            for j in range(nplane):
                frame[j, EDGE : EDGE + size] = strips[t][j * size : (j + 1) * size].astype(F32)
                for i, y in enumerate(halo_rows(EDGE, size)[: count // nplane]):
                    frame[j, y : y + 1] = beside[i * nplane + j : i * nplane + j + 1]

    face = first_ref.shape[0] - 32
    over, under = sorted_ends(first_ref, second_ref, strips[1], face, 16)
    zero = jnp.zeros((16, LANES), F32)
    layer = jnp.where(place == 0, first_ref[face + 16 : face + 32].astype(F32), zero)
    layer = layer + jnp.where(place == 1, lays[0][min(1, nstrips - 1)].astype(F32), zero)
    layer = layer + jnp.where(place == 2, second_ref[face + 16 : face + 32].astype(F32), zero)
    layer = layer + jnp.where(place == 3, first_ref[face + 16 : face + 32].astype(F32), zero)
    for got in lays[1:]:
        layer = layer + got[...].astype(F32)
    layer_ref[...] = layer
    winds = strip_winds(frame, layer, nx, (0, nx - 1))
    for comp in range(ncomp):
        wind_ref[comp] = winds[comp, 0]
        wind_ref[ncomp + comp] = winds[comp, nx - 1]
    row = iota((EDGE, nz), 0)
    for x in range(nx):
        one, two = (slice(2 * x, 2 * x + 1), slice(2 * x + 1, 2 * x + 2))
        before = jnp.where(row == EDGE - 2, under[one], jnp.where(row == EDGE - 1, under[two], 0.0))
        after = jnp.where(row == 0, over[one], jnp.where(row == 1, over[two], 0.0))
        conc_ref[x] = jnp.concatenate([before, dust_ref[x], after], 0)
    lane = iota((nx, LANES), 1)
    own = terrain_ref[...].astype(F32)
    own = jnp.concatenate([own, jnp.zeros((nx, LANES - size), F32)], 1)
    land = slice(2 * nx, 3 * nx)
    before = pltpu.roll(under, (EDGE - size) % LANES, 1)[land]
    after = pltpu.roll(over, (EDGE + size) % LANES, 1)[land]
    ground = jnp.where(lane < EDGE, before, jnp.where(lane < EDGE + size, pltpu.roll(own, EDGE, 1), after))
    lifted = lifted_layer(place, ground, eligible_ref, size)
    cols_ref[...] = jnp.zeros_like(cols_ref)
    cols_ref[:nx] = ground
    cols_ref[EDGE : EDGE + nx] = lifted
    fill = jnp.zeros((16 - 2 * ncomp - 2, LANES), F32)
    strip, first, last = (slice(EDGE, EDGE + size), slice(EDGE - 1, EDGE), slice(EDGE + size, EDGE + size + 1))

    def send(ref, x, inner):
        del inner
        for comp in range(ncomp):
            j = comp * nx + x
            ref[comp * size : (comp + 1) * size] = frame[j, strip].astype(BF)
            ref[(ncomp + comp) * size : (ncomp + comp + 1) * size] = wind_ref[(ncomp if x else 0) + comp, strip].astype(BF)
        at = 2 * ncomp * size
        rows = [frame[comp * nx + x, first] for comp in range(ncomp)] + [conc_ref[x, first]]
        rows += [frame[comp * nx + x, last] for comp in range(ncomp)] + [conc_ref[x, last]]
        ref[at : at + 16] = jnp.concatenate(rows + [fill], 0).astype(BF)

    send_both(odd, send, near_ref, far_ref, nx)


def plane_state(comps, rise, base, inside):
    gu, gv, gw = comps
    shape = gu.shape
    layer = iota(shape, 1).astype(F32)
    speed = jnp.sqrt(gu * gu + gv * gv)
    lift = jnp.where(layer == jnp.broadcast_to(rise, shape), 0.5 * jnp.maximum(speed - 1.0, 0.0), 0.0)
    keep = (layer >= jnp.broadcast_to(base, shape)) & inside
    coef = [
        (0.15 * (0.1 - jnp.minimum(a, 0.0)), 0.15 * (0.1 + jnp.maximum(a, 0.0)))
        for a in (gu, gv, gw - 0.5)
    ]
    return coef, lift, keep


def step(state, c, behind, ahead, span=slice(None)):
    coef, lift, keep = state
    rows, nz = c.shape
    layer = iota(lift.shape, 1)
    here = c[span]
    total = here + lift
    pairs = (
        (ahead, behind),
        (pltpu.roll(c, rows - 1, 0)[span], pltpu.roll(c, 1, 0)[span]),
        (
            jnp.where(layer == nz - 1, 0.0, pltpu.roll(here, nz - 1, 1)),
            jnp.where(layer == 0, 0.0, pltpu.roll(here, 1, 1)),
        ),
    )
    for (forward, back), (post, prev) in zip(coef, pairs):
        total = total + forward * (post - here) - back * (here - prev)
    return jnp.where(keep, total, 0.0)


def rows_of(state, span):
    coef, lift, keep = state
    return [(forward[span], back[span]) for forward, back in coef], lift[span], keep[span]


def domain_rows(shape, ny, size):
    y = iota(shape, 0) + (lax.axis_index("vert") * size - EDGE)
    return (y >= 0) & (y < ny)


def interior(ny, size, frame, layer_ref, conc_ref, cols_ref, after_ref, coef_ref, lift_ref, keep_ref, once_ref):
    del after_ref
    nx, rows, nz = conc_ref.shape
    ncomp = frame.shape[0] // nx
    winds = strip_winds(frame, layer_ref[...], nx, range(1, nx - 1))
    table = jnp.concatenate([cols_ref[...], jnp.zeros((LANES - 16, LANES), F32)], 0).T[:rows]
    inside = domain_rows((rows, nz), ny, size)
    for x in range(1, nx - 1):
        comps = [winds[comp, x] for comp in range(ncomp)]
        state = plane_state(comps, table[:, EDGE + x : EDGE + x + 1], table[:, x : x + 1], inside)
        coef, lift, keep = state
        for i, pair in enumerate(coef):
            coef_ref[x - 1, 2 * i], coef_ref[x - 1, 2 * i + 1] = pair
        lift_ref[x - 1] = lift
        keep_ref[x - 1] = jnp.where(keep, 1.0, 0.0)
        once_ref[x - 1] = step(state, conc_ref[x], conc_ref[x - 1], conc_ref[x + 1])


def transport(ny, nhoriz, *refs):
    wind_ref, frame, conc_ref, cols_ref, face_far, face_near, far_ref, near_ref = refs[:8]
    coef_ref, lift_ref, keep_ref, once_ref, out_ref = refs[8:]
    nx, size, nz = out_ref.shape
    ncomp = frame.shape[0] // nx
    rows = size + 2 * EDGE
    column = lax.axis_index("horiz")
    odd = lax.rem(column, 2) == 1
    low = iota((EDGE, nz), 0)

    def either(one, other, start, n):
        return jnp.where(odd, one[start : start + n].astype(F32), other[start : start + n].astype(F32))

    def framed(rows, ends=None, halo=0):
        head, tail = (jnp.zeros((EDGE, nz), F32),) * 2
        if ends is not None:
            head = jnp.where(low == EDGE - 1, ends[halo : halo + 1], head)
            tail = jnp.where(low == 0, ends[ncomp + 1 + halo : ncomp + 2 + halo], tail)
        return jnp.concatenate([head, rows, tail], 0)

    pairs_of = {"below": (near_ref, far_ref, face_near, face_far), "above": (far_ref, near_ref, face_far, face_near)}
    ends, dusts, marks = ({}, {}, {})
    for side, (one, other, face_one, face_other) in pairs_of.items():
        ends[side] = either(one, other, 2 * ncomp * size, 16)
        at = ncomp * ny
        dusts[side] = (
            framed(either(face_one, face_other, at, size), ends[side], ncomp),
            either(face_one, face_other, at + size, size),
        )
        marks[side] = either(face_one, face_other, at + 2 * size, 16)

    def part(side, i, halo=None):
        rows = either(*pairs_of[side][:2], i * size, size)
        return rows if halo is None else framed(rows, ends[side], halo)

    below, above = ("below", "above")
    conc = [dusts[below][1], dusts[below][0]]
    conc += [conc_ref[x] for x in range(nx)]
    conc += [dusts[above][0], dusts[above][1]]
    table = jnp.concatenate([marks[below], cols_ref[...], marks[above], jnp.zeros((LANES - 48, LANES), F32)], 0).T[:rows]
    mark = 0
    ground = [mark] + [16 + x for x in range(nx)] + [32 + mark]
    lifted = [mark + 1] + [16 + EDGE + x for x in range(nx)] + [33 + mark]
    inside = domain_rows((rows, nz), ny, size)
    strip = slice(EDGE, EDGE + size)
    state = [None] * (nx + 2)
    for p in range(nx + 2):
        if 1 < p < nx:
            coef = [(coef_ref[p - 2, 2 * i], coef_ref[p - 2, 2 * i + 1]) for i in range(3)]
            state[p] = (coef, lift_ref[p - 2], keep_ref[p - 2] > 0.5)
            continue
        comps = []
        for comp in range(ncomp):
            if p == 0:
                w = part(below, ncomp + comp) + 0.12 * frame[comp * nx, strip]
            elif p == nx + 1:
                w = part(above, ncomp + comp) + 0.12 * frame[comp * nx + nx - 1, strip]
            elif p == 1:
                w = wind_ref[comp] + 0.12 * part(below, comp, comp)
            else:
                w = wind_ref[ncomp + comp] + 0.12 * part(above, comp, comp)
            comps.append(w)
        rise, base = (table[:, lifted[p] : lifted[p] + 1], table[:, ground[p] : ground[p] + 1])
        if p == 0:
            state[p] = plane_state(comps, rise[strip], base[strip], inside[strip] & (column > 0))
        elif p == nx + 1:
            state[p] = plane_state(comps, rise[strip], base[strip], inside[strip] & (column < nhoriz - 1))
        else:
            state[p] = plane_state(comps, rise, base, inside)

    once = []
    for p in range(nx + 2):
        c, behind, ahead = (conc[p + 1], conc[p], conc[p + 2])
        if 1 < p < nx:
            once.append(once_ref[p - 2])
        elif p in (0, nx + 1):
            behind = behind if p == 0 else behind[strip]
            ahead = ahead[strip] if p == 0 else ahead
            once.append(step(state[p], c, behind, ahead, strip))
        else:
            once.append(step(state[p], c, behind, ahead))
    for x in range(nx):
        behind = once[x] if x == 0 else once[x][strip]
        ahead = once[x + 2] if x == nx - 1 else once[x + 2][strip]
        out_ref[x] = step(rows_of(state[x + 1], strip), once[x + 1], behind, ahead, strip)


def pairs(size, start):
    return [p for i in range(start, size - 1, 2) for p in ((i, i + 1), (i + 1, i))]


def local(velocity, dust, eligible, terrain):
    ncomp, nx, ny, nz = velocity.shape
    size = dust.shape[1]
    nh, nv = (lax.axis_size("horiz"), lax.axis_size("vert"))
    rows = size + 2 * EDGE
    near_pairs, far_pairs = (pairs(nh, 0), pairs(nh, 1))
    nplane = ncomp * nx
    anywhere = pl.BlockSpec(memory_space=pl.ANY)

    ends = ny // LANES * 16 + 32
    held = [pltpu.with_memory_space_constraint(array, pltpu.HBM) for array in (velocity, dust, terrain)]
    strips = call(
        functools.partial(pack_low, size),
        [shaped(nplane * size + beside_rows(nplane, t, nv) + (ends - 16 if t == 1 else 0), LANES) for t in range(nv)],
        "pack_low",
        [
            pltpu.VMEM((ncomp, nx, ny, nz), F32),
            pltpu.VMEM((16, ny), F32),
            pltpu.VMEM((nv, 4 * nplane, LANES), F32),
            pltpu.VMEM((nx, EDGE, nz), F32),
            pltpu.VMEM((nx, size), jnp.int32),
            pltpu.SemaphoreType.DMA((nplane + 2,)),
        ],
        in_specs=[anywhere] * 3,
        out_specs=[VMEM] * nv,
    )(*held)
    got = [strips[0]] + [lax.ppermute(strips[t], "vert", [(0, t)]) for t in range(1, nv)]

    first, second, mine, *lays = call(
        functools.partial(pack_ends, size, nv),
        [shaped(ends, LANES), shaped(ends + 16, LANES), shaped(3, 16, LANES)] + [shaped(16, LANES)] * (nv - 4),
        "pack_ends",
        [pltpu.VMEM((16, ny), F32)] * 2
        + [pltpu.VMEM((2, nx, EDGE, nz), F32), pltpu.VMEM((nx, size), jnp.int32), pltpu.SemaphoreType.DMA((3,))],
        in_specs=[VMEM] + [anywhere] * 3,
    )(velocity, *held[1:], strips[-1])
    second = lax.ppermute(second, "vert", pairs(nv, 1))
    first = call(relay, shaped(ends, LANES), "relay")(first, second)
    first = lax.ppermute(first, "vert", pairs(nv, 0)[1:])
    lays = [mine] + [lax.ppermute(lay, "vert", [(1, t + 4)]) for t, lay in enumerate(lays)]

    far, near = call(
        pack_sides, [shaped(ncomp * ny + 2 * size + 16, LANES)] * 2, "pack_sides", in_specs=[VMEM] * 4 + [anywhere]
    )(velocity, dust, terrain, eligible, second)
    far = lax.ppermute(far, "horiz", far_pairs)
    near = lax.ppermute(near, "horiz", near_pairs)

    velocity_next = call(
        advance,
        jax.ShapeDtypeStruct(velocity.shape, F32),
        "advance",
        [pltpu.VMEM((ncomp, nx, ny, nz), F32), pltpu.SemaphoreType.DMA((ncomp,))],
        in_specs=[VMEM] * 6,
        out_specs=anywhere,
    )(velocity, far, near, first, second, got[1])

    wire = 2 * ncomp * size + 16
    wind, conc, cols, mf, mn, layer, frame = call(
        functools.partial(prepare, nv),
        [
            shaped(2 * ncomp, rows, LANES, dtype=F32),
            shaped(nx, rows, LANES, dtype=F32),
            shaped(16, LANES, dtype=F32),
            shaped(wire, LANES),
            shaped(wire, LANES),
            shaped(16, LANES, dtype=F32),
            shaped(nplane, rows, LANES, dtype=F32),
        ],
        "prepare",
    )(*got, *lays, dust, terrain, eligible, first, second)
    mf = lax.ppermute(mf, "horiz", far_pairs)
    mn = lax.ppermute(mn, "horiz", near_pairs)
    inner = [shaped(nx - 2, *dims, rows, LANES, dtype=F32) for dims in ((6,), (), (), ())]
    inner = call(
        functools.partial(interior, ny, size), inner, "interior", in_specs=[VMEM] * 4 + [anywhere]
    )(frame, layer, conc, cols, far)
    dust_next = call(
        functools.partial(transport, ny, nh),
        jax.ShapeDtypeStruct(dust.shape, F32),
        "transport",
    )(wind, frame, conc, cols, far, near, mf, mn, *inner)
    return (velocity_next, dust_next)


def solution(mesh):
    placed = (
        P(None, "horiz", None, "vert"),
        P("horiz", "vert", None),
        P("horiz", None),
        P("horiz", "vert"),
    )
    return jax.shard_map(
        local,
        mesh=mesh,
        in_specs=placed,
        out_specs=(P(None, "horiz", None, "vert"), P("horiz", "vert", None)),
        check_vma=False,
    )
```

```python
import functools

import jax
import jax.numpy as jnp
from jax import lax
from jax.experimental import pallas as pl
from jax.experimental.pallas import tpu as pltpu
from jax.sharding import PartitionSpec as P

DSTEPS = 2
LANES = 128
EDGE = 8
BF = jnp.bfloat16
F32 = jnp.float32

VMEM = pl.BlockSpec(memory_space=pltpu.VMEM)


def call(kernel, out_shape, name, scratch=(), cost=1 << 20, **kwargs):
    return pl.pallas_call(
        kernel,
        out_shape=out_shape,
        scratch_shapes=list(scratch),
        compiler_params=pltpu.CompilerParams(vmem_limit_bytes=40 << 20),
        cost_estimate=pl.CostEstimate(flops=cost, bytes_accessed=cost, transcendentals=0),
        name=name,
        **kwargs,
    )


def shaped(*dims, dtype=BF):
    return jax.ShapeDtypeStruct(dims, dtype)


def iota(shape, dim):
    return lax.broadcasted_iota(jnp.int32, shape, dim)


def pick(shape, pairs):
    row, col = iota(shape, 0), iota(shape, 1)
    hit = functools.reduce(jnp.logical_or, [(row == r) & (col == c) for r, c in pairs])
    return jnp.where(hit, 1.0, 0.0).astype(BF)


def turn_faces(v_ref, comp, ends, outs):
    _, nx, ny, _ = v_ref.shape
    for x in range(nx):
        j = comp * nx + x
        for half in range(ny // LANES):
            span = slice(half * LANES, (half + 1) * LANES)
            block = v_ref[comp, x, span, :].astype(BF)
            rows = lax.dot_general(ends, block, (((1,), (1,)), ((), ())), preferred_element_type=F32)
            for i, out in enumerate(outs):
                out[j : j + 1, span] = rows[i : i + 1]


def beside_rows(nplane, t, nstrips):
    return -(-2 * nplane // 16) * 16 if t == nstrips - 1 else 4 * nplane


def halo_rows(start, size):
    return (start - 2, start - 1, start + size, start + size + 1)


def columns(place, terrain_ref, eligible_ref):
    nx, size = terrain_ref.shape
    own = jnp.concatenate([terrain_ref[...].astype(F32), jnp.zeros((nx, LANES - size), F32)], 1)
    ground = pltpu.roll(own, EDGE, 1)
    return ground, lifted_layer(place, ground, eligible_ref, size)


def lifted_layer(place, ground, eligible_ref, size):
    y = iota(ground.shape, 1) + (place * size - EDGE)
    flags = jnp.zeros(ground.shape, jnp.int32)
    for b in range(eligible_ref.shape[1]):
        inside = (y >= b * 128) & (y < (b + 1) * 128)
        flags = jnp.where(inside, jnp.broadcast_to(eligible_ref[:, b : b + 1], ground.shape), flags)
    return jnp.where(flags == 1, ground, -1.0)


def pack_sides(v_ref, dust_ref, terrain_ref, eligible_ref, after_ref, far_ref, near_ref):
    del after_ref
    ncomp, nx, ny, _ = v_ref.shape
    size = dust_ref.shape[1]
    odd = lax.rem(lax.axis_index("horiz"), 2) == 1
    ground, lifted = columns(lax.axis_index("vert"), terrain_ref, eligible_ref)
    fill = jnp.zeros((14, LANES), F32)

    def send(ref, x, inner):
        for comp in range(ncomp):
            ref[comp * ny : (comp + 1) * ny] = v_ref[comp, x].astype(BF)
        at = ncomp * ny
        ref[at : at + size] = dust_ref[x].astype(BF)
        ref[at + size : at + 2 * size] = dust_ref[inner].astype(BF)
        at = at + 2 * size
        ref[at : at + 16] = jnp.concatenate([ground[x : x + 1], lifted[x : x + 1], fill], 0).astype(BF)

    send_both(odd, send, near_ref, far_ref, nx)


def send_both(odd, send, near_ref, far_ref, nx):
    @pl.when(odd)
    def _():
        send(near_ref, 0, 1)
        send(far_ref, nx - 1, nx - 2)

    @pl.when(jnp.logical_not(odd))
    def _():
        send(near_ref, nx - 1, nx - 2)
        send(far_ref, 0, 1)


def start_all(copies):
    for copy in copies:
        copy.start()
    return copies


def wait_all(copies):
    for copy in copies:
        copy.wait()


def write_ends(ref, at, face, dust, land, layer=None):
    nx, size = land.shape
    terrain = jnp.concatenate([land.astype(F32), jnp.zeros((nx, LANES - size), F32)], 1)
    fill = jnp.zeros((16 - 3 * nx, LANES), F32)
    for half in range(face.shape[1] // LANES):
        ref[at : at + 16] = face[:, half * LANES : (half + 1) * LANES].astype(BF)
        at = at + 16
    ref[at : at + 16] = jnp.concatenate([dust[x] for x in range(nx)] + [terrain, fill], 0).astype(BF)
    if layer is not None:
        ref[at + 16 : at + 32] = layer


def pack_low(size, v_ref, dust_ref, terrain_ref, *refs):
    outs, (buf, high, side, dusts, land, sems) = (refs[:-6], refs[-6:])
    ncomp, nx, ny, nz = v_ref.shape
    nplane = ncomp * nx

    @pl.when(lax.axis_index("vert") == 0)
    def _():
        planes = start_all(
            [pltpu.make_async_copy(v_ref.at[j // nx, j % nx], buf.at[j // nx, j % nx], sems.at[j]) for j in range(nplane)]
        )
        small = start_all(
            [
                pltpu.make_async_copy(dust_ref.at[:, size - EDGE :], dusts, sems.at[nplane]),
                pltpu.make_async_copy(terrain_ref, land, sems.at[nplane + 1]),
            ]
        )
        side[...] = jnp.zeros_like(side)
        high[...] = jnp.zeros_like(high)
        end = pick((16, nz), [(0, nz - 1)])
        for comp in range(ncomp):
            wait_all(planes[comp * nx : (comp + 1) * nx])
            turn_faces(buf, comp, end, [high])
            for x in range(nx):
                j = comp * nx + x
                for t, out in enumerate(outs):
                    out[j * size : (j + 1) * size] = buf[comp, x, t * size : (t + 1) * size, :].astype(BF)
                    for i, y in enumerate(halo_rows(t * size, size)):
                        if 0 <= y < ny:
                            side[t, i * nplane + j : i * nplane + j + 1] = buf[comp, x, y : y + 1, :]
        for t, out in enumerate(outs):
            count = beside_rows(nplane, t, len(outs))
            out[nplane * size : nplane * size + count] = side[t, :count].astype(BF)
        wait_all(small)
        write_ends(outs[1], nplane * (size + 4), high, dusts[:, EDGE - 2 :], land[...])


def pack_ends(size, nstrips, v_ref, dust_ref, terrain_ref, after_ref, first_ref, second_ref, mine_ref, *refs):
    del after_ref
    lays, (low, high, dusts, land, sems) = (refs[:-5], refs[-5:])
    ncomp, nx, ny, nz = v_ref.shape
    odd = lax.rem(lax.axis_index("vert"), 2) == 1
    small = start_all(
        [
            pltpu.make_async_copy(dust_ref.at[:, :EDGE], dusts.at[0], sems.at[0]),
            pltpu.make_async_copy(dust_ref.at[:, size - EDGE :], dusts.at[1], sems.at[1]),
            pltpu.make_async_copy(terrain_ref, land, sems.at[2]),
        ]
    )
    low[...] = jnp.zeros_like(low)
    high[...] = jnp.zeros_like(high)
    ends = pick((16, nz), [(0, 0), (1, nz - 1)])
    for comp in range(ncomp):
        turn_faces(v_ref, comp, ends, [low, high])
    lane = iota((16, LANES), 1)
    whole = low[...]
    for t in range(nstrips):
        shift = (EDGE - t * size) % ny
        moved = pltpu.roll(whole, shift, 1) if shift else whole
        row = lane + (t * size - EDGE)
        part = jnp.where((row >= 0) & (row < ny), moved[:, :LANES], 0.0).astype(BF)
        if t < 3:
            mine_ref[t] = part
        elif t == 3:
            second_ref[second_ref.shape[0] - 16 :] = part
        else:
            lays[t - 4][...] = part
    wait_all(small)

    @pl.when(odd)
    def _():
        write_ends(first_ref, 0, low, dusts[0, :, :2], land[...], mine_ref[0])
        write_ends(second_ref, 0, high, dusts[1, :, EDGE - 2 :], land[...], mine_ref[2])

    @pl.when(jnp.logical_not(odd))
    def _():
        write_ends(first_ref, 0, high, dusts[1, :, EDGE - 2 :], land[...], mine_ref[2])
        write_ends(second_ref, 0, low, dusts[0, :, :2], land[...], mine_ref[0])


def relay(base_ref, second_ref, first_ref):
    first_ref[...] = base_ref[...]

    @pl.when(lax.axis_index("vert") == 2)
    def _():
        first_ref[first_ref.shape[0] - 16 :] = second_ref[second_ref.shape[0] - 16 :]


def sorted_ends(first_ref, second_ref, strip_ref, start, n):
    place = lax.axis_index("vert")
    odd = lax.rem(place, 2) == 1
    base = strip_ref.shape[0] - first_ref.shape[0] + 16 + start
    first, second = (first_ref[start : start + n].astype(F32), second_ref[start : start + n].astype(F32))
    below = jnp.where(place == 1, strip_ref[base : base + n].astype(F32), jnp.where(odd, first, second))
    return (jnp.where(odd, second, first), below)


def rows_before(v_ref, comp, x, a):
    if a:
        return v_ref[comp, x, a - 1 : a + LANES - 1, :]
    edge = pltpu.roll(v_ref[comp, x, :8, :], 1, 0)
    edge = jnp.where(iota(edge.shape, 0) == 0, 0.0, edge)
    return jnp.concatenate([edge, v_ref[comp, x, 7 : LANES - 1, :]], 0)


def rows_after(v_ref, comp, x, a):
    ny = v_ref.shape[2]
    if a + LANES < ny:
        return v_ref[comp, x, a + 1 : a + LANES + 1, :]
    edge = pltpu.roll(v_ref[comp, x, ny - 8 :, :], 7, 0)
    edge = jnp.where(iota(edge.shape, 0) == 7, 0.0, edge)
    return jnp.concatenate([v_ref[comp, x, a + 1 : ny - 7, :], edge], 0)


def advance(v_ref, far_ref, near_ref, first_ref, second_ref, strip_ref, mark_ref, out_ref, buf, sems):
    del mark_ref
    ncomp, nx, ny, nz = v_ref.shape
    odd = lax.rem(lax.axis_index("horiz"), 2) == 1
    row, lane = iota((LANES, nz), 0), iota((LANES, nz), 1)
    nb = ny // LANES
    turned = []
    for half in range(nb):
        over, under = sorted_ends(first_ref, second_ref, strip_ref, half * 16, 16)
        faces = jnp.concatenate([over, under, jnp.zeros((LANES - 32, LANES), F32)], 0)
        turned.append(faces.T.astype(BF))
    copies = []
    for comp in range(ncomp):
        for half in range(nb):
            a = half * LANES
            span = slice(a, a + LANES)
            rows = slice(comp * ny + a, comp * ny + a + LANES)
            near, far = (near_ref[rows].astype(F32), far_ref[rows].astype(F32))
            below = jnp.where(odd, near, far)
            above = jnp.where(odd, far, near)
            for x in range(nx):
                j = comp * nx + x
                place = ((row == j) & (lane == nz - 1)) | ((row == 16 + j) & (lane == 0))
                place = jnp.where(place, 1.0, 0.0).astype(BF)
                sums = lax.dot_general(turned[half], place, (((1,), (0,)), ((), ())), preferred_element_type=F32)
                f = v_ref[comp, x, span, :]
                sums = sums + jnp.where(lane == 0, 0.0, pltpu.roll(f, 1, 1))
                sums = sums + jnp.where(lane == nz - 1, 0.0, pltpu.roll(f, nz - 1, 1))
                sums = sums + rows_before(v_ref, comp, x, a) + rows_after(v_ref, comp, x, a)
                sums = sums + (v_ref[comp, x - 1, span, :] if x else below)
                sums = sums + (v_ref[comp, x + 1, span, :] if x < nx - 1 else above)
                buf[comp, x, span, :] = f + 0.12 * (sums - 6.0 * f)
        copies.append(pltpu.make_async_copy(buf.at[comp], out_ref.at[comp], sems.at[comp]))
        copies[-1].start()
    for copy in copies:
        copy.wait()


def strip_winds(frame, layer, nx, planes):
    nplane, rows, nz = frame.shape
    turned = jnp.concatenate([layer, jnp.zeros((LANES - 16, LANES), F32)], 0).T.astype(BF)[:rows]
    brow, blane = iota((LANES, nz), 0), iota((LANES, nz), 1)
    beside = jnp.where((brow == blane + 1) | (brow == blane - 1), 1.0, 0.0).astype(BF)
    winds = {}
    for comp in range(nplane // nx):
        for x in planes:
            j = comp * nx + x
            f = frame[j]
            near = jnp.dot(f.astype(BF), beside, preferred_element_type=F32)
            top = jnp.where((brow == j) & (blane == nz - 1), 1.0, 0.0).astype(BF)
            near = near + jnp.dot(turned, top, preferred_element_type=F32)
            near = near + pltpu.roll(f, 1, 0) + pltpu.roll(f, rows - 1, 0)
            if x:
                near = near + frame[j - 1]
            if x < nx - 1:
                near = near + frame[j + 1]
            winds[comp, x] = 0.28 * f + 0.12 * near
    return winds


def prepare(nstrips, *refs):
    strips = refs[:nstrips]
    nlay = 1 + max(nstrips - 4, 0)
    lays = refs[nstrips : nstrips + nlay]
    dust_ref, terrain_ref, eligible_ref, first_ref, second_ref = refs[nstrips + nlay : nstrips + nlay + 5]
    wind_ref, conc_ref, cols_ref, far_ref, near_ref, layer_ref, frame = refs[nstrips + nlay + 5 :]
    nx, size, nz = dust_ref.shape
    nplane = frame.shape[0]
    ncomp = nplane // nx
    rows = size + 2 * EDGE
    place = lax.axis_index("vert")
    odd = lax.rem(lax.axis_index("horiz"), 2) == 1
    frame[:, :EDGE] = jnp.zeros((nplane, EDGE, nz), F32)
    frame[:, EDGE + size :] = jnp.zeros((nplane, EDGE, nz), F32)
    for t in range(nstrips):
        @pl.when(place == t)
        def _(t=t):
            count = beside_rows(nplane, t, nstrips)
            beside = strips[t][nplane * size : nplane * size + count].astype(F32)
            for j in range(nplane):
                frame[j, EDGE : EDGE + size] = strips[t][j * size : (j + 1) * size].astype(F32)
                for i, y in enumerate(halo_rows(EDGE, size)[: count // nplane]):
                    frame[j, y : y + 1] = beside[i * nplane + j : i * nplane + j + 1]

    face = first_ref.shape[0] - 32
    over, under = sorted_ends(first_ref, second_ref, strips[1], face, 16)
    zero = jnp.zeros((16, LANES), F32)
    layer = jnp.where(place == 0, first_ref[face + 16 : face + 32].astype(F32), zero)
    layer = layer + jnp.where(place == 1, lays[0][min(1, nstrips - 1)].astype(F32), zero)
    layer = layer + jnp.where(place == 2, second_ref[face + 16 : face + 32].astype(F32), zero)
    layer = layer + jnp.where(place == 3, first_ref[face + 16 : face + 32].astype(F32), zero)
    for got in lays[1:]:
        layer = layer + got[...].astype(F32)
    layer_ref[...] = layer
    winds = strip_winds(frame, layer, nx, (0, nx - 1))
    for comp in range(ncomp):
        wind_ref[comp] = winds[comp, 0]
        wind_ref[ncomp + comp] = winds[comp, nx - 1]
    row = iota((EDGE, nz), 0)
    for x in range(nx):
        one, two = (slice(2 * x, 2 * x + 1), slice(2 * x + 1, 2 * x + 2))
        before = jnp.where(row == EDGE - 2, under[one], jnp.where(row == EDGE - 1, under[two], 0.0))
        after = jnp.where(row == 0, over[one], jnp.where(row == 1, over[two], 0.0))
        conc_ref[x] = jnp.concatenate([before, dust_ref[x], after], 0)
    lane = iota((nx, LANES), 1)
    own = terrain_ref[...].astype(F32)
    own = jnp.concatenate([own, jnp.zeros((nx, LANES - size), F32)], 1)
    land = slice(2 * nx, 3 * nx)
    before = pltpu.roll(under, (EDGE - size) % LANES, 1)[land]
    after = pltpu.roll(over, (EDGE + size) % LANES, 1)[land]
    ground = jnp.where(lane < EDGE, before, jnp.where(lane < EDGE + size, pltpu.roll(own, EDGE, 1), after))
    lifted = lifted_layer(place, ground, eligible_ref, size)
    cols_ref[...] = jnp.zeros_like(cols_ref)
    cols_ref[:nx] = ground
    cols_ref[EDGE : EDGE + nx] = lifted
    fill = jnp.zeros((16 - 2 * ncomp - 2, LANES), F32)
    strip, first, last = (slice(EDGE, EDGE + size), slice(EDGE - 1, EDGE), slice(EDGE + size, EDGE + size + 1))

    def send(ref, x, inner):
        del inner
        for comp in range(ncomp):
            j = comp * nx + x
            ref[comp * size : (comp + 1) * size] = frame[j, strip].astype(BF)
            ref[(ncomp + comp) * size : (ncomp + comp + 1) * size] = wind_ref[(ncomp if x else 0) + comp, strip].astype(BF)
        at = 2 * ncomp * size
        rows = [frame[comp * nx + x, first] for comp in range(ncomp)] + [conc_ref[x, first]]
        rows += [frame[comp * nx + x, last] for comp in range(ncomp)] + [conc_ref[x, last]]
        ref[at : at + 16] = jnp.concatenate(rows + [fill], 0).astype(BF)

    send_both(odd, send, near_ref, far_ref, nx)


def plane_state(comps, rise, base, inside):
    gu, gv, gw = comps
    shape = gu.shape
    layer = iota(shape, 1).astype(F32)
    speed = jnp.sqrt(gu * gu + gv * gv)
    lift = jnp.where(layer == jnp.broadcast_to(rise, shape), 0.5 * jnp.maximum(speed - 1.0, 0.0), 0.0)
    keep = (layer >= jnp.broadcast_to(base, shape)) & inside
    coef, own = ([], 1.0)
    for a in (gu, gv, gw - 0.5):
        scaled = 0.15 * a
        forward, back = (0.015 - jnp.minimum(scaled, 0.0), 0.015 + jnp.maximum(scaled, 0.0))
        own = own - (forward + back)
        coef.append((forward, back))
    forward, back = coef[2]
    coef[2] = (jnp.where(layer == shape[1] - 1.0, 0.0, forward), jnp.where(layer == 0.0, 0.0, back))
    return coef + [(own, lift)], lift, keep


def step(state, c, behind, ahead, span=slice(None)):
    coef, _, keep = state
    rows, nz = c.shape
    here = c[span]
    pairs = (
        (ahead, behind),
        (pltpu.roll(c, rows - 1, 0)[span], pltpu.roll(c, 1, 0)[span]),
        (pltpu.roll(here, nz - 1, 1), pltpu.roll(here, 1, 1)),
    )
    own, lift = coef[3]
    total = own * here + lift
    for (forward, back), (post, prev) in zip(coef[:3], pairs):
        total = total + (forward * post + back * prev)
    return jnp.where(keep, total, 0.0)


def rows_of(state, span):
    coef, lift, keep = state
    return [(forward[span], back[span]) for forward, back in coef], lift[span], keep[span]


def domain_rows(shape, ny, size):
    y = iota(shape, 0) + (lax.axis_index("vert") * size - EDGE)
    return (y >= 0) & (y < ny)


def interior(ny, size, frame, layer_ref, conc_ref, cols_ref, coef_ref, lift_ref, keep_ref, once_ref, mark_ref):
    mark_ref[...] = jnp.zeros_like(mark_ref)
    nx, rows, nz = conc_ref.shape
    ncomp = frame.shape[0] // nx
    winds = strip_winds(frame, layer_ref[...], nx, range(1, nx - 1))
    table = jnp.concatenate([cols_ref[...], jnp.zeros((LANES - 16, LANES), F32)], 0).T[:rows]
    inside = domain_rows((rows, nz), ny, size)
    for x in range(1, nx - 1):
        comps = [winds[comp, x] for comp in range(ncomp)]
        state = plane_state(comps, table[:, EDGE + x : EDGE + x + 1], table[:, x : x + 1], inside)
        coef, lift, keep = state
        for i, pair in enumerate(coef):
            coef_ref[x - 1, 2 * i], coef_ref[x - 1, 2 * i + 1] = pair
        lift_ref[x - 1] = lift
        keep_ref[x - 1] = jnp.where(keep, 1.0, 0.0)
        once_ref[x - 1] = step(state, conc_ref[x], conc_ref[x - 1], conc_ref[x + 1])


def transport(ny, nhoriz, *refs):
    wind_ref, frame, conc_ref, cols_ref, face_far, face_near, far_ref, near_ref = refs[:8]
    coef_ref, lift_ref, keep_ref, once_ref, out_ref, buf, sems = refs[8:]
    nx, size, nz = out_ref.shape
    ncomp = frame.shape[0] // nx
    rows = size + 2 * EDGE
    column = lax.axis_index("horiz")
    odd = lax.rem(column, 2) == 1
    low = iota((EDGE, nz), 0)

    def either(one, other, start, n):
        return jnp.where(odd, one[start : start + n].astype(F32), other[start : start + n].astype(F32))

    def framed(rows, ends=None, halo=0):
        head, tail = (jnp.zeros((EDGE, nz), F32),) * 2
        if ends is not None:
            head = jnp.where(low == EDGE - 1, ends[halo : halo + 1], head)
            tail = jnp.where(low == 0, ends[ncomp + 1 + halo : ncomp + 2 + halo], tail)
        return jnp.concatenate([head, rows, tail], 0)

    pairs_of = {"below": (near_ref, far_ref, face_near, face_far), "above": (far_ref, near_ref, face_far, face_near)}
    ends, dusts, marks = ({}, {}, {})
    for side, (one, other, face_one, face_other) in pairs_of.items():
        ends[side] = either(one, other, 2 * ncomp * size, 16)
        at = ncomp * ny
        dusts[side] = (
            framed(either(face_one, face_other, at, size), ends[side], ncomp),
            either(face_one, face_other, at + size, size),
        )
        marks[side] = either(face_one, face_other, at + 2 * size, 16)

    def part(side, i, halo=None):
        rows = either(*pairs_of[side][:2], i * size, size)
        return rows if halo is None else framed(rows, ends[side], halo)

    below, above = ("below", "above")
    conc = [dusts[below][1], dusts[below][0]]
    conc += [conc_ref[x] for x in range(nx)]
    conc += [dusts[above][0], dusts[above][1]]
    table = jnp.concatenate([marks[below], cols_ref[...], marks[above], jnp.zeros((LANES - 48, LANES), F32)], 0).T[:rows]
    mark = 0
    ground = [mark] + [16 + x for x in range(nx)] + [32 + mark]
    lifted = [mark + 1] + [16 + EDGE + x for x in range(nx)] + [33 + mark]
    inside = domain_rows((rows, nz), ny, size)
    strip = slice(EDGE, EDGE + size)
    state = [None] * (nx + 2)
    for p in range(nx + 2):
        if 1 < p < nx:
            coef = [(coef_ref[p - 2, 2 * i], coef_ref[p - 2, 2 * i + 1]) for i in range(4)]
            state[p] = (coef, lift_ref[p - 2], keep_ref[p - 2] > 0.5)
            continue
        comps = []
        for comp in range(ncomp):
            if p == 0:
                w = part(below, ncomp + comp) + 0.12 * frame[comp * nx, strip]
            elif p == nx + 1:
                w = part(above, ncomp + comp) + 0.12 * frame[comp * nx + nx - 1, strip]
            elif p == 1:
                w = wind_ref[comp] + 0.12 * part(below, comp, comp)
            else:
                w = wind_ref[ncomp + comp] + 0.12 * part(above, comp, comp)
            comps.append(w)
        rise, base = (table[:, lifted[p] : lifted[p] + 1], table[:, ground[p] : ground[p] + 1])
        if p == 0:
            state[p] = plane_state(comps, rise[strip], base[strip], inside[strip] & (column > 0))
        elif p == nx + 1:
            state[p] = plane_state(comps, rise[strip], base[strip], inside[strip] & (column < nhoriz - 1))
        else:
            state[p] = plane_state(comps, rise, base, inside)

    once = []
    for p in range(nx + 2):
        c, behind, ahead = (conc[p + 1], conc[p], conc[p + 2])
        if 1 < p < nx:
            once.append(once_ref[p - 2])
        elif p in (0, nx + 1):
            behind = behind if p == 0 else behind[strip]
            ahead = ahead[strip] if p == 0 else ahead
            once.append(step(state[p], c, behind, ahead, strip))
        else:
            once.append(step(state[p], c, behind, ahead))
    copies = []
    for x in range(nx):
        behind = once[x] if x == 0 else once[x][strip]
        ahead = once[x + 2] if x == nx - 1 else once[x + 2][strip]
        buf[x] = step(rows_of(state[x + 1], strip), once[x + 1], behind, ahead, strip)
        copies.append(pltpu.make_async_copy(buf.at[x], out_ref.at[x], sems.at[x]))
        copies[-1].start()
    wait_all(copies)


def pairs(size, start):
    return [p for i in range(start, size - 1, 2) for p in ((i, i + 1), (i + 1, i))]


def local(velocity, dust, eligible, terrain):
    ncomp, nx, ny, nz = velocity.shape
    size = dust.shape[1]
    nh, nv = (lax.axis_size("horiz"), lax.axis_size("vert"))
    rows = size + 2 * EDGE
    near_pairs, far_pairs = (pairs(nh, 0), pairs(nh, 1))
    nplane = ncomp * nx
    anywhere = pl.BlockSpec(memory_space=pl.ANY)

    ends = ny // LANES * 16 + 32
    held = [pltpu.with_memory_space_constraint(array, pltpu.HBM) for array in (velocity, dust, terrain)]
    strips = call(
        functools.partial(pack_low, size),
        [shaped(nplane * size + beside_rows(nplane, t, nv) + (ends - 16 if t == 1 else 0), LANES) for t in range(nv)],
        "pack_low",
        [
            pltpu.VMEM((ncomp, nx, ny, nz), F32),
            pltpu.VMEM((16, ny), F32),
            pltpu.VMEM((nv, 4 * nplane, LANES), F32),
            pltpu.VMEM((nx, EDGE, nz), F32),
            pltpu.VMEM((nx, size), jnp.int32),
            pltpu.SemaphoreType.DMA((nplane + 2,)),
        ],
        in_specs=[anywhere] * 3,
        out_specs=[VMEM] * nv,
    )(*held)
    got = [strips[0]] + [lax.ppermute(strips[t], "vert", [(0, t)]) for t in range(1, nv)]

    first, second, mine, *lays = call(
        functools.partial(pack_ends, size, nv),
        [shaped(ends, LANES), shaped(ends + 16, LANES), shaped(3, 16, LANES)] + [shaped(16, LANES)] * (nv - 4),
        "pack_ends",
        [pltpu.VMEM((16, ny), F32)] * 2
        + [pltpu.VMEM((2, nx, EDGE, nz), F32), pltpu.VMEM((nx, size), jnp.int32), pltpu.SemaphoreType.DMA((3,))],
        in_specs=[VMEM] + [anywhere] * 3,
    )(velocity, *held[1:], strips[-1])
    second = lax.ppermute(second, "vert", pairs(nv, 1))
    first = call(relay, shaped(ends, LANES), "relay")(first, second)
    first = lax.ppermute(first, "vert", pairs(nv, 0)[1:])
    lays = [mine] + [lax.ppermute(lay, "vert", [(1, t + 4)]) for t, lay in enumerate(lays)]

    far, near = call(
        pack_sides, [shaped(ncomp * ny + 2 * size + 16, LANES)] * 2, "pack_sides", in_specs=[VMEM] * 4 + [anywhere]
    )(velocity, dust, terrain, eligible, second)
    far = lax.ppermute(far, "horiz", far_pairs)
    near = lax.ppermute(near, "horiz", near_pairs)

    wire = 2 * ncomp * size + 16
    wind, conc, cols, mf, mn, layer, frame = call(
        functools.partial(prepare, nv),
        [
            shaped(2 * ncomp, rows, LANES, dtype=F32),
            shaped(nx, rows, LANES, dtype=F32),
            shaped(16, LANES, dtype=F32),
            shaped(wire, LANES),
            shaped(wire, LANES),
            shaped(16, LANES, dtype=F32),
            shaped(nplane, rows, LANES, dtype=F32),
        ],
        "prepare",
    )(*got, *lays, dust, terrain, eligible, first, second)
    mf = lax.ppermute(mf, "horiz", far_pairs)
    mn = lax.ppermute(mn, "horiz", near_pairs)
    inner = [shaped(nx - 2, *dims, rows, LANES, dtype=F32) for dims in ((8,), (), (), ())]
    *inner, mark = call(
        functools.partial(interior, ny, size), inner + [shaped(8, LANES, dtype=F32)], "interior"
    )(frame, layer, conc, cols)
    velocity_next = call(
        advance,
        jax.ShapeDtypeStruct(velocity.shape, F32),
        "advance",
        [pltpu.VMEM((ncomp, nx, ny, nz), F32), pltpu.SemaphoreType.DMA((ncomp,))],
        in_specs=[VMEM] * 7,
        out_specs=anywhere,
    )(velocity, far, near, first, second, got[1], mark)

    dust_next = call(
        functools.partial(transport, ny, nh),
        jax.ShapeDtypeStruct(dust.shape, F32),
        "transport",
        [pltpu.VMEM(dust.shape, F32), pltpu.SemaphoreType.DMA((nx,))],
        in_specs=[VMEM] * 12,
        out_specs=anywhere,
    )(wind, frame, conc, cols, far, near, mf, mn, *inner)
    return (velocity_next, dust_next)


def solution(mesh):
    placed = (
        P(None, "horiz", None, "vert"),
        P("horiz", "vert", None),
        P("horiz", None),
        P("horiz", "vert"),
    )
    return jax.shard_map(
        local,
        mesh=mesh,
        in_specs=placed,
        out_specs=(P(None, "horiz", None, "vert"), P("horiz", "vert", None)),
        check_vma=False,
    )
```

```python
import functools

import jax
import jax.numpy as jnp
from jax import lax
from jax.experimental import pallas as pl
from jax.experimental.pallas import tpu as pltpu
from jax.sharding import PartitionSpec as P

DSTEPS = 2
LANES = 128
EDGE = 8
BF = jnp.bfloat16
F32 = jnp.float32

VMEM = pl.BlockSpec(memory_space=pltpu.VMEM)


def call(kernel, out_shape, name, scratch=(), cost=1 << 20, **kwargs):
    return pl.pallas_call(
        kernel,
        out_shape=out_shape,
        scratch_shapes=list(scratch),
        compiler_params=pltpu.CompilerParams(vmem_limit_bytes=40 << 20),
        cost_estimate=pl.CostEstimate(flops=cost, bytes_accessed=cost, transcendentals=0),
        name=name,
        **kwargs,
    )


def shaped(*dims, dtype=BF):
    return jax.ShapeDtypeStruct(dims, dtype)


def iota(shape, dim):
    return lax.broadcasted_iota(jnp.int32, shape, dim)


def pick(shape, pairs):
    row, col = iota(shape, 0), iota(shape, 1)
    hit = functools.reduce(jnp.logical_or, [(row == r) & (col == c) for r, c in pairs])
    return jnp.where(hit, 1.0, 0.0).astype(BF)


def turn_faces(v_ref, comp, ends, outs):
    _, nx, ny, _ = v_ref.shape
    for x in range(nx):
        j = comp * nx + x
        for half in range(ny // LANES):
            span = slice(half * LANES, (half + 1) * LANES)
            block = v_ref[comp, x, span, :].astype(BF)
            rows = lax.dot_general(ends, block, (((1,), (1,)), ((), ())), preferred_element_type=F32)
            for i, out in enumerate(outs):
                out[j : j + 1, span] = rows[i : i + 1]


def beside_rows(nplane, t, nstrips):
    return -(-2 * nplane // 16) * 16 if t == nstrips - 1 else 4 * nplane


def halo_rows(start, size):
    return (start - 2, start - 1, start + size, start + size + 1)


def columns(place, terrain_ref, eligible_ref):
    nx, size = terrain_ref.shape
    own = jnp.concatenate([terrain_ref[...].astype(F32), jnp.zeros((nx, LANES - size), F32)], 1)
    ground = pltpu.roll(own, EDGE, 1)
    return ground, lifted_layer(place, ground, eligible_ref, size)


def lifted_layer(place, ground, eligible_ref, size):
    y = iota(ground.shape, 1) + (place * size - EDGE)
    flags = jnp.zeros(ground.shape, jnp.int32)
    for b in range(eligible_ref.shape[1]):
        inside = (y >= b * 128) & (y < (b + 1) * 128)
        flags = jnp.where(inside, jnp.broadcast_to(eligible_ref[:, b : b + 1], ground.shape), flags)
    return jnp.where(flags == 1, ground, -1.0)


def pack_sides(v_ref, dust_ref, terrain_ref, eligible_ref, after_ref, far_ref, near_ref):
    del after_ref
    ncomp, nx, ny, _ = v_ref.shape
    size = dust_ref.shape[1]
    odd = lax.rem(lax.axis_index("horiz"), 2) == 1
    ground, lifted = columns(lax.axis_index("vert"), terrain_ref, eligible_ref)
    fill = jnp.zeros((14, LANES), F32)

    def send(ref, x, inner):
        for comp in range(ncomp):
            ref[comp * ny : (comp + 1) * ny] = v_ref[comp, x].astype(BF)
        at = ncomp * ny
        ref[at : at + size] = dust_ref[x].astype(BF)
        ref[at + size : at + 2 * size] = dust_ref[inner].astype(BF)
        at = at + 2 * size
        ref[at : at + 16] = jnp.concatenate([ground[x : x + 1], lifted[x : x + 1], fill], 0).astype(BF)

    send_both(odd, send, near_ref, far_ref, nx)


def send_both(odd, send, near_ref, far_ref, nx):
    @pl.when(odd)
    def _():
        send(near_ref, 0, 1)
        send(far_ref, nx - 1, nx - 2)

    @pl.when(jnp.logical_not(odd))
    def _():
        send(near_ref, nx - 1, nx - 2)
        send(far_ref, 0, 1)


def start_all(copies):
    for copy in copies:
        copy.start()
    return copies


def wait_all(copies):
    for copy in copies:
        copy.wait()


def write_ends(ref, at, face, dust, land, layer=None):
    nx, size = land.shape
    terrain = jnp.concatenate([land.astype(F32), jnp.zeros((nx, LANES - size), F32)], 1)
    fill = jnp.zeros((16 - 3 * nx, LANES), F32)
    for half in range(face.shape[1] // LANES):
        ref[at : at + 16] = face[:, half * LANES : (half + 1) * LANES].astype(BF)
        at = at + 16
    ref[at : at + 16] = jnp.concatenate([dust[x] for x in range(nx)] + [terrain, fill], 0).astype(BF)
    if layer is not None:
        ref[at + 16 : at + 32] = layer


def pack_low(size, v_ref, dust_ref, terrain_ref, *refs):
    outs, (buf, high, side, dusts, land, sems) = (refs[:-6], refs[-6:])
    ncomp, nx, ny, nz = v_ref.shape
    nplane = ncomp * nx

    @pl.when(lax.axis_index("vert") == 0)
    def _():
        planes = start_all(
            [pltpu.make_async_copy(v_ref.at[j // nx, j % nx], buf.at[j // nx, j % nx], sems.at[j]) for j in range(nplane)]
        )
        small = start_all(
            [
                pltpu.make_async_copy(dust_ref.at[:, size - EDGE :], dusts, sems.at[nplane]),
                pltpu.make_async_copy(terrain_ref, land, sems.at[nplane + 1]),
            ]
        )
        side[...] = jnp.zeros_like(side)
        high[...] = jnp.zeros_like(high)
        end = pick((16, nz), [(0, nz - 1)])
        for comp in range(ncomp):
            wait_all(planes[comp * nx : (comp + 1) * nx])
            turn_faces(buf, comp, end, [high])
            for x in range(nx):
                j = comp * nx + x
                for t, out in enumerate(outs):
                    out[j * size : (j + 1) * size] = buf[comp, x, t * size : (t + 1) * size, :].astype(BF)
                    for i, y in enumerate(halo_rows(t * size, size)):
                        if 0 <= y < ny:
                            side[t, i * nplane + j : i * nplane + j + 1] = buf[comp, x, y : y + 1, :]
        for t, out in enumerate(outs):
            count = beside_rows(nplane, t, len(outs))
            out[nplane * size : nplane * size + count] = side[t, :count].astype(BF)
        wait_all(small)
        write_ends(outs[1], nplane * (size + 4), high, dusts[:, EDGE - 2 :], land[...])


def pack_ends(size, nstrips, v_ref, dust_ref, terrain_ref, after_ref, first_ref, second_ref, mine_ref, *refs):
    del after_ref
    lays, (low, high, dusts, land, sems) = (refs[:-5], refs[-5:])
    ncomp, nx, ny, nz = v_ref.shape
    odd = lax.rem(lax.axis_index("vert"), 2) == 1
    small = start_all(
        [
            pltpu.make_async_copy(dust_ref.at[:, :EDGE], dusts.at[0], sems.at[0]),
            pltpu.make_async_copy(dust_ref.at[:, size - EDGE :], dusts.at[1], sems.at[1]),
            pltpu.make_async_copy(terrain_ref, land, sems.at[2]),
        ]
    )
    low[...] = jnp.zeros_like(low)
    high[...] = jnp.zeros_like(high)
    ends = pick((16, nz), [(0, 0), (1, nz - 1)])
    for comp in range(ncomp):
        turn_faces(v_ref, comp, ends, [low, high])
    lane = iota((16, LANES), 1)
    whole = low[...]
    for t in range(nstrips):
        shift = (EDGE - t * size) % ny
        moved = pltpu.roll(whole, shift, 1) if shift else whole
        row = lane + (t * size - EDGE)
        part = jnp.where((row >= 0) & (row < ny), moved[:, :LANES], 0.0).astype(BF)
        if t < 3:
            mine_ref[t] = part
        elif t == 3:
            second_ref[second_ref.shape[0] - 16 :] = part
        else:
            lays[t - 4][...] = part
    wait_all(small)

    @pl.when(odd)
    def _():
        write_ends(first_ref, 0, low, dusts[0, :, :2], land[...], mine_ref[0])
        write_ends(second_ref, 0, high, dusts[1, :, EDGE - 2 :], land[...], mine_ref[2])

    @pl.when(jnp.logical_not(odd))
    def _():
        write_ends(first_ref, 0, high, dusts[1, :, EDGE - 2 :], land[...], mine_ref[2])
        write_ends(second_ref, 0, low, dusts[0, :, :2], land[...], mine_ref[0])


def relay(base_ref, second_ref, first_ref):
    first_ref[...] = base_ref[...]

    @pl.when(lax.axis_index("vert") == 2)
    def _():
        first_ref[first_ref.shape[0] - 16 :] = second_ref[second_ref.shape[0] - 16 :]


def sorted_ends(first_ref, second_ref, strip_ref, start, n):
    place = lax.axis_index("vert")
    odd = lax.rem(place, 2) == 1
    base = strip_ref.shape[0] - first_ref.shape[0] + 16 + start
    first, second = (first_ref[start : start + n].astype(F32), second_ref[start : start + n].astype(F32))
    below = jnp.where(place == 1, strip_ref[base : base + n].astype(F32), jnp.where(odd, first, second))
    return (jnp.where(odd, second, first), below)


def rows_before(v_ref, comp, x, a):
    if a:
        return v_ref[comp, x, a - 1 : a + LANES - 1, :]
    edge = pltpu.roll(v_ref[comp, x, :8, :], 1, 0)
    edge = jnp.where(iota(edge.shape, 0) == 0, 0.0, edge)
    return jnp.concatenate([edge, v_ref[comp, x, 7 : LANES - 1, :]], 0)


def rows_after(v_ref, comp, x, a):
    ny = v_ref.shape[2]
    if a + LANES < ny:
        return v_ref[comp, x, a + 1 : a + LANES + 1, :]
    edge = pltpu.roll(v_ref[comp, x, ny - 8 :, :], 7, 0)
    edge = jnp.where(iota(edge.shape, 0) == 7, 0.0, edge)
    return jnp.concatenate([v_ref[comp, x, a + 1 : ny - 7, :], edge], 0)


def advance(v_ref, far_ref, near_ref, first_ref, second_ref, strip_ref, mark_ref, out_ref, buf, sems):
    del mark_ref
    ncomp, nx, ny, nz = v_ref.shape
    odd = lax.rem(lax.axis_index("horiz"), 2) == 1
    row, lane = iota((LANES, nz), 0), iota((LANES, nz), 1)
    nb = ny // LANES
    turned = []
    for half in range(nb):
        over, under = sorted_ends(first_ref, second_ref, strip_ref, half * 16, 16)
        faces = jnp.concatenate([over, under, jnp.zeros((LANES - 32, LANES), F32)], 0)
        turned.append(faces.T.astype(BF))
    copies = []
    for comp in range(ncomp):
        for half in range(nb):
            a = half * LANES
            span = slice(a, a + LANES)
            rows = slice(comp * ny + a, comp * ny + a + LANES)
            near, far = (near_ref[rows].astype(F32), far_ref[rows].astype(F32))
            below = jnp.where(odd, near, far)
            above = jnp.where(odd, far, near)
            for x in range(nx):
                j = comp * nx + x
                place = ((row == j) & (lane == nz - 1)) | ((row == 16 + j) & (lane == 0))
                place = jnp.where(place, 1.0, 0.0).astype(BF)
                sums = lax.dot_general(turned[half], place, (((1,), (0,)), ((), ())), preferred_element_type=F32)
                f = v_ref[comp, x, span, :]
                sums = sums + jnp.where(lane == 0, 0.0, pltpu.roll(f, 1, 1))
                sums = sums + jnp.where(lane == nz - 1, 0.0, pltpu.roll(f, nz - 1, 1))
                sums = sums + rows_before(v_ref, comp, x, a) + rows_after(v_ref, comp, x, a)
                sums = sums + (v_ref[comp, x - 1, span, :] if x else below)
                sums = sums + (v_ref[comp, x + 1, span, :] if x < nx - 1 else above)
                buf[comp, x, span, :] = f + 0.12 * (sums - 6.0 * f)
        copies.append(pltpu.make_async_copy(buf.at[comp], out_ref.at[comp], sems.at[comp]))
        copies[-1].start()
    for copy in copies:
        copy.wait()


def strip_winds(frame, layer, nx, planes):
    nplane, rows, nz = frame.shape
    turned = jnp.concatenate([layer, jnp.zeros((LANES - 16, LANES), F32)], 0).T.astype(BF)[:rows]
    brow, blane = iota((LANES, nz), 0), iota((LANES, nz), 1)
    beside = jnp.where((brow == blane + 1) | (brow == blane - 1), 1.0, 0.0).astype(BF)
    winds = {}
    for comp in range(nplane // nx):
        for x in planes:
            j = comp * nx + x
            f = frame[j]
            near = jnp.dot(f.astype(BF), beside, preferred_element_type=F32)
            top = jnp.where((brow == j) & (blane == nz - 1), 1.0, 0.0).astype(BF)
            near = near + jnp.dot(turned, top, preferred_element_type=F32)
            near = near + pltpu.roll(f, 1, 0) + pltpu.roll(f, rows - 1, 0)
            if x:
                near = near + frame[j - 1]
            if x < nx - 1:
                near = near + frame[j + 1]
            winds[comp, x] = 0.28 * f + 0.12 * near
    return winds


def prepare(nstrips, *refs):
    strips = refs[:nstrips]
    nlay = 1 + max(nstrips - 4, 0)
    lays = refs[nstrips : nstrips + nlay]
    dust_ref, terrain_ref, eligible_ref, first_ref, second_ref = refs[nstrips + nlay : nstrips + nlay + 5]
    wind_ref, conc_ref, cols_ref, far_ref, near_ref, layer_ref, frame = refs[nstrips + nlay + 5 :]
    nx, size, nz = dust_ref.shape
    nplane = frame.shape[0]
    ncomp = nplane // nx
    rows = size + 2 * EDGE
    place = lax.axis_index("vert")
    odd = lax.rem(lax.axis_index("horiz"), 2) == 1
    frame[:, :EDGE] = jnp.zeros((nplane, EDGE, nz), F32)
    frame[:, EDGE + size :] = jnp.zeros((nplane, EDGE, nz), F32)
    for t in range(nstrips):
        @pl.when(place == t)
        def _(t=t):
            count = beside_rows(nplane, t, nstrips)
            beside = strips[t][nplane * size : nplane * size + count].astype(F32)
            for j in range(nplane):
                frame[j, EDGE : EDGE + size] = strips[t][j * size : (j + 1) * size].astype(F32)
                for i, y in enumerate(halo_rows(EDGE, size)[: count // nplane]):
                    frame[j, y : y + 1] = beside[i * nplane + j : i * nplane + j + 1]

    face = first_ref.shape[0] - 32
    over, under = sorted_ends(first_ref, second_ref, strips[1], face, 16)
    zero = jnp.zeros((16, LANES), F32)
    layer = jnp.where(place == 0, first_ref[face + 16 : face + 32].astype(F32), zero)
    layer = layer + jnp.where(place == 1, lays[0][min(1, nstrips - 1)].astype(F32), zero)
    layer = layer + jnp.where(place == 2, second_ref[face + 16 : face + 32].astype(F32), zero)
    layer = layer + jnp.where(place == 3, first_ref[face + 16 : face + 32].astype(F32), zero)
    for got in lays[1:]:
        layer = layer + got[...].astype(F32)
    layer_ref[...] = layer
    winds = strip_winds(frame, layer, nx, (0, nx - 1))
    for comp in range(ncomp):
        wind_ref[comp] = winds[comp, 0]
        wind_ref[ncomp + comp] = winds[comp, nx - 1]
    row = iota((EDGE, nz), 0)
    for x in range(nx):
        one, two = (slice(2 * x, 2 * x + 1), slice(2 * x + 1, 2 * x + 2))
        before = jnp.where(row == EDGE - 2, under[one], jnp.where(row == EDGE - 1, under[two], 0.0))
        after = jnp.where(row == 0, over[one], jnp.where(row == 1, over[two], 0.0))
        conc_ref[x] = jnp.concatenate([before, dust_ref[x], after], 0)
    lane = iota((nx, LANES), 1)
    own = terrain_ref[...].astype(F32)
    own = jnp.concatenate([own, jnp.zeros((nx, LANES - size), F32)], 1)
    land = slice(2 * nx, 3 * nx)
    before = pltpu.roll(under, (EDGE - size) % LANES, 1)[land]
    after = pltpu.roll(over, (EDGE + size) % LANES, 1)[land]
    ground = jnp.where(lane < EDGE, before, jnp.where(lane < EDGE + size, pltpu.roll(own, EDGE, 1), after))
    lifted = lifted_layer(place, ground, eligible_ref, size)
    cols_ref[...] = jnp.zeros_like(cols_ref)
    cols_ref[:nx] = ground
    cols_ref[EDGE : EDGE + nx] = lifted
    fill = jnp.zeros((16 - 2 * ncomp - 2, LANES), F32)
    strip, first, last = (slice(EDGE, EDGE + size), slice(EDGE - 1, EDGE), slice(EDGE + size, EDGE + size + 1))

    def send(ref, x, inner):
        del inner
        for comp in range(ncomp):
            j = comp * nx + x
            ref[comp * size : (comp + 1) * size] = frame[j, strip].astype(BF)
            ref[(ncomp + comp) * size : (ncomp + comp + 1) * size] = wind_ref[(ncomp if x else 0) + comp, strip].astype(BF)
        at = 2 * ncomp * size
        rows = [frame[comp * nx + x, first] for comp in range(ncomp)] + [conc_ref[x, first]]
        rows += [frame[comp * nx + x, last] for comp in range(ncomp)] + [conc_ref[x, last]]
        ref[at : at + 16] = jnp.concatenate(rows + [fill], 0).astype(BF)

    send_both(odd, send, near_ref, far_ref, nx)


def plane_state(comps, rise, base, inside):
    gu, gv, gw = comps
    shape = gu.shape
    layer = iota(shape, 1).astype(F32)
    speed = jnp.sqrt(gu * gu + gv * gv)
    lift = jnp.where(layer == jnp.broadcast_to(rise, shape), 0.5 * jnp.maximum(speed - 1.0, 0.0), 0.0)
    keep = (layer >= jnp.broadcast_to(base, shape)) & inside
    coef, own = ([], 1.0)
    for a in (gu, gv, gw - 0.5):
        scaled = 0.15 * a
        forward, back = (0.015 - jnp.minimum(scaled, 0.0), 0.015 + jnp.maximum(scaled, 0.0))
        own = own - (forward + back)
        coef.append((forward, back))
    forward, back = coef[2]
    coef[2] = (jnp.where(layer == shape[1] - 1.0, 0.0, forward), jnp.where(layer == 0.0, 0.0, back))
    return coef + [(own, lift)], lift, keep


def step(state, c, behind, ahead, span=slice(None)):
    coef, _, keep = state
    rows, nz = c.shape
    here = c[span]
    pairs = (
        (ahead, behind),
        (pltpu.roll(c, rows - 1, 0)[span], pltpu.roll(c, 1, 0)[span]),
        (pltpu.roll(here, nz - 1, 1), pltpu.roll(here, 1, 1)),
    )
    own, lift = coef[3]
    total = own * here + lift
    for (forward, back), (post, prev) in zip(coef[:3], pairs):
        total = total + (forward * post + back * prev)
    return jnp.where(keep, total, 0.0)


def rows_of(state, span):
    coef, lift, keep = state
    return [(forward[span], back[span]) for forward, back in coef], lift[span], keep[span]


def domain_rows(shape, ny, size):
    y = iota(shape, 0) + (lax.axis_index("vert") * size - EDGE)
    return (y >= 0) & (y < ny)


def interior(ny, size, frame, layer_ref, conc_ref, cols_ref, coef_ref, lift_ref, keep_ref, once_ref, mark_ref):
    mark_ref[...] = jnp.zeros_like(mark_ref)
    nx, rows, nz = conc_ref.shape
    ncomp = frame.shape[0] // nx
    winds = strip_winds(frame, layer_ref[...], nx, range(1, nx - 1))
    table = jnp.concatenate([cols_ref[...], jnp.zeros((LANES - 16, LANES), F32)], 0).T[:rows]
    inside = domain_rows((rows, nz), ny, size)
    for x in range(1, nx - 1):
        comps = [winds[comp, x] for comp in range(ncomp)]
        state = plane_state(comps, table[:, EDGE + x : EDGE + x + 1], table[:, x : x + 1], inside)
        coef, lift, keep = state
        for i, pair in enumerate(coef):
            coef_ref[x - 1, 2 * i], coef_ref[x - 1, 2 * i + 1] = pair
        lift_ref[x - 1] = lift
        keep_ref[x - 1] = jnp.where(keep, 1.0, 0.0)
        once_ref[x - 1] = step(state, conc_ref[x], conc_ref[x - 1], conc_ref[x + 1])


def transport(ny, nhoriz, *refs):
    wind_ref, frame, conc_ref, cols_ref, face_far, face_near, far_ref, near_ref = refs[:8]
    coef_ref, lift_ref, keep_ref, once_ref, out_ref, buf, sems = refs[8:]
    nx, size, nz = out_ref.shape
    ncomp = frame.shape[0] // nx
    rows = size + 2 * EDGE
    column = lax.axis_index("horiz")
    odd = lax.rem(column, 2) == 1

    def run(upper):
        low = iota((EDGE, nz), 0)

        def either(one, other, start, n):
            return (one if upper else other)[start : start + n].astype(F32)

        def framed(rows, ends=None, halo=0):
            head, tail = (jnp.zeros((EDGE, nz), F32),) * 2
            if ends is not None:
                head = jnp.where(low == EDGE - 1, ends[halo : halo + 1], head)
                tail = jnp.where(low == 0, ends[ncomp + 1 + halo : ncomp + 2 + halo], tail)
            return jnp.concatenate([head, rows, tail], 0)

        pairs_of = {"below": (near_ref, far_ref, face_near, face_far), "above": (far_ref, near_ref, face_far, face_near)}
        ends, dusts, marks = ({}, {}, {})
        for side, (one, other, face_one, face_other) in pairs_of.items():
            ends[side] = either(one, other, 2 * ncomp * size, 16)
            at = ncomp * ny
            dusts[side] = (
                framed(either(face_one, face_other, at, size), ends[side], ncomp),
                either(face_one, face_other, at + size, size),
            )
            marks[side] = either(face_one, face_other, at + 2 * size, 16)

        def part(side, i, halo=None):
            rows = either(*pairs_of[side][:2], i * size, size)
            return rows if halo is None else framed(rows, ends[side], halo)

        below, above = ("below", "above")
        conc = [dusts[below][1], dusts[below][0]]
        conc += [conc_ref[x] for x in range(nx)]
        conc += [dusts[above][0], dusts[above][1]]
        table = jnp.concatenate([marks[below], cols_ref[...], marks[above], jnp.zeros((LANES - 48, LANES), F32)], 0).T[:rows]
        mark = 0
        ground = [mark] + [16 + x for x in range(nx)] + [32 + mark]
        lifted = [mark + 1] + [16 + EDGE + x for x in range(nx)] + [33 + mark]
        inside = domain_rows((rows, nz), ny, size)
        strip = slice(EDGE, EDGE + size)
        state = [None] * (nx + 2)
        for p in range(nx + 2):
            if 1 < p < nx:
                coef = [(coef_ref[p - 2, 2 * i], coef_ref[p - 2, 2 * i + 1]) for i in range(4)]
                state[p] = (coef, lift_ref[p - 2], keep_ref[p - 2] > 0.5)
                continue
            comps = []
            for comp in range(ncomp):
                if p == 0:
                    w = part(below, ncomp + comp) + 0.12 * frame[comp * nx, strip]
                elif p == nx + 1:
                    w = part(above, ncomp + comp) + 0.12 * frame[comp * nx + nx - 1, strip]
                elif p == 1:
                    w = wind_ref[comp] + 0.12 * part(below, comp, comp)
                else:
                    w = wind_ref[ncomp + comp] + 0.12 * part(above, comp, comp)
                comps.append(w)
            rise, base = (table[:, lifted[p] : lifted[p] + 1], table[:, ground[p] : ground[p] + 1])
            if p == 0:
                state[p] = plane_state(comps, rise[strip], base[strip], inside[strip] & (column > 0))
            elif p == nx + 1:
                state[p] = plane_state(comps, rise[strip], base[strip], inside[strip] & (column < nhoriz - 1))
            else:
                state[p] = plane_state(comps, rise, base, inside)

        once = []
        for p in range(nx + 2):
            c, behind, ahead = (conc[p + 1], conc[p], conc[p + 2])
            if 1 < p < nx:
                once.append(once_ref[p - 2])
            elif p in (0, nx + 1):
                behind = behind if p == 0 else behind[strip]
                ahead = ahead[strip] if p == 0 else ahead
                once.append(step(state[p], c, behind, ahead, strip))
            else:
                once.append(step(state[p], c, behind, ahead))
        copies = []
        for x in range(nx):
            behind = once[x] if x == 0 else once[x][strip]
            ahead = once[x + 2] if x == nx - 1 else once[x + 2][strip]
            buf[x] = step(rows_of(state[x + 1], strip), once[x + 1], behind, ahead, strip)
            copies.append(pltpu.make_async_copy(buf.at[x], out_ref.at[x], sems.at[x]))
            copies[-1].start()
        wait_all(copies)

    pl.when(odd)(functools.partial(run, True))
    pl.when(jnp.logical_not(odd))(functools.partial(run, False))


def pairs(size, start):
    return [p for i in range(start, size - 1, 2) for p in ((i, i + 1), (i + 1, i))]


def local(velocity, dust, eligible, terrain):
    ncomp, nx, ny, nz = velocity.shape
    size = dust.shape[1]
    nh, nv = (lax.axis_size("horiz"), lax.axis_size("vert"))
    rows = size + 2 * EDGE
    near_pairs, far_pairs = (pairs(nh, 0), pairs(nh, 1))
    nplane = ncomp * nx
    anywhere = pl.BlockSpec(memory_space=pl.ANY)

    ends = ny // LANES * 16 + 32
    held = [pltpu.with_memory_space_constraint(array, pltpu.HBM) for array in (velocity, dust, terrain)]
    strips = call(
        functools.partial(pack_low, size),
        [shaped(nplane * size + beside_rows(nplane, t, nv) + (ends - 16 if t == 1 else 0), LANES) for t in range(nv)],
        "pack_low",
        [
            pltpu.VMEM((ncomp, nx, ny, nz), F32),
            pltpu.VMEM((16, ny), F32),
            pltpu.VMEM((nv, 4 * nplane, LANES), F32),
            pltpu.VMEM((nx, EDGE, nz), F32),
            pltpu.VMEM((nx, size), jnp.int32),
            pltpu.SemaphoreType.DMA((nplane + 2,)),
        ],
        in_specs=[anywhere] * 3,
        out_specs=[VMEM] * nv,
    )(*held)
    got = [strips[0]] + [lax.ppermute(strips[t], "vert", [(0, t)]) for t in range(1, nv)]

    first, second, mine, *lays = call(
        functools.partial(pack_ends, size, nv),
        [shaped(ends, LANES), shaped(ends + 16, LANES), shaped(3, 16, LANES)] + [shaped(16, LANES)] * (nv - 4),
        "pack_ends",
        [pltpu.VMEM((16, ny), F32)] * 2
        + [pltpu.VMEM((2, nx, EDGE, nz), F32), pltpu.VMEM((nx, size), jnp.int32), pltpu.SemaphoreType.DMA((3,))],
        in_specs=[VMEM] + [anywhere] * 3,
    )(velocity, *held[1:], strips[-1])
    second = lax.ppermute(second, "vert", pairs(nv, 1))
    first = call(relay, shaped(ends, LANES), "relay")(first, second)
    first = lax.ppermute(first, "vert", pairs(nv, 0)[1:])
    lays = [mine] + [lax.ppermute(lay, "vert", [(1, t + 4)]) for t, lay in enumerate(lays)]

    far, near = call(
        pack_sides, [shaped(ncomp * ny + 2 * size + 16, LANES)] * 2, "pack_sides", in_specs=[VMEM] * 4 + [anywhere]
    )(velocity, dust, terrain, eligible, second)
    far = lax.ppermute(far, "horiz", far_pairs)
    near = lax.ppermute(near, "horiz", near_pairs)

    wire = 2 * ncomp * size + 16
    wind, conc, cols, mf, mn, layer, frame = call(
        functools.partial(prepare, nv),
        [
            shaped(2 * ncomp, rows, LANES, dtype=F32),
            shaped(nx, rows, LANES, dtype=F32),
            shaped(16, LANES, dtype=F32),
            shaped(wire, LANES),
            shaped(wire, LANES),
            shaped(16, LANES, dtype=F32),
            shaped(nplane, rows, LANES, dtype=F32),
        ],
        "prepare",
    )(*got, *lays, dust, terrain, eligible, first, second)
    mf = lax.ppermute(mf, "horiz", far_pairs)
    mn = lax.ppermute(mn, "horiz", near_pairs)
    inner = [shaped(nx - 2, *dims, rows, LANES, dtype=F32) for dims in ((8,), (), (), ())]
    *inner, mark = call(
        functools.partial(interior, ny, size), inner + [shaped(8, LANES, dtype=F32)], "interior"
    )(frame, layer, conc, cols)
    velocity_next = call(
        advance,
        jax.ShapeDtypeStruct(velocity.shape, F32),
        "advance",
        [pltpu.VMEM((ncomp, nx, ny, nz), F32), pltpu.SemaphoreType.DMA((ncomp,))],
        in_specs=[VMEM] * 7,
        out_specs=anywhere,
    )(velocity, far, near, first, second, got[1], mark)

    dust_next = call(
        functools.partial(transport, ny, nh),
        jax.ShapeDtypeStruct(dust.shape, F32),
        "transport",
        [pltpu.VMEM(dust.shape, F32), pltpu.SemaphoreType.DMA((nx,))],
        in_specs=[VMEM] * 12,
        out_specs=anywhere,
    )(wind, frame, conc, cols, far, near, mf, mn, *inner)
    return (velocity_next, dust_next)


def solution(mesh):
    placed = (
        P(None, "horiz", None, "vert"),
        P("horiz", "vert", None),
        P("horiz", None),
        P("horiz", "vert"),
    )
    return jax.shard_map(
        local,
        mesh=mesh,
        in_specs=placed,
        out_specs=(P(None, "horiz", None, "vert"), P("horiz", "vert", None)),
        check_vma=False,
    )
```
